32 devices in a mesh: seq: 8 (over y, x, core), head: 4 (over z).
Axes of the slice: x: 2, y: 2, z: 4, core: 2. Of those that a mesh axis runs over, the one named last changes fastest.
Arguments:
- ssm_input: bfloat16 [1536, 16384], P('seq', 'head'), may hold values from -6 to 6
- state_in: bfloat16 [1536, 2048], P('seq'), may hold values from -0.375 to 0.375
- state_out: bfloat16 [1536, 2048], P('seq'), may hold values from -0.15625 to 0.15625
- step_size: float32 [1536, 256], P('seq', 'head'), may hold values from 0.5 to 1.5
- decay_rate: float32 [256], P('head'), may hold values from 3.25520833e-05 to 0.04
- forget: float32 [1536], P('seq'), may hold values from 0 to 0.9
- skip_gain: float32 [256], P('head'), may hold values from 0.25 to 1.75
- queries: bfloat16 [1536, 8192], P('seq', 'head'), may hold values from -48 to 48
- new_keys: bfloat16 [1536, 1024], P('seq'), may hold values from -6 to 6
- new_values: bfloat16 [1536, 1024], P('seq'), may hold values from -6 to 6
- cache_keys: bfloat16 [1024, 1024], P('seq'), may hold values from -127 to 127, as said below
- cache_values: bfloat16 [1024, 1024], P('seq'), may hold values from -127 to 127, as said below
- cache_key_scale: float32 [1024], replicated, may hold values from 0.003 to 0.03
- cache_value_scale: float32 [1024], replicated, may hold values from 0.003 to 0.03
Outputs:
- ssm_output: bfloat16 [1536, 16384], P('seq', 'head')
- attended: bfloat16 [1536, 8192], P('seq', 'head')
- key_codes: bfloat16 [1536, 1024], P('seq')
- key_scale: float32 [1024], replicated
The draws below stay inside these ranges and needn't reach their ends.
Inputs may be any that keep to these rules, and one draw needn't show every extreme that they name: `cache_keys`: whole numbers. `cache_values`: whole numbers.
All inputs are finite; a program needn't handle non-finite values.
Results may differ from the reference program's by a relative error of at most 0.019.
Values may be sent and summed in bfloat16 or wider, within the bound.
A program may use at most 128 MiB of HBM per device.

```python
import math
import jax
import jax.numpy as jnp
from jax import lax

SSM_HEADS = 256
HEAD_DIM = 64
STATE = 256
GROUPS = 8
ATT_HEADS = 64
KV_HEADS = 8
ATT_DIM = 128
TOK_DEV = 192
TOKENS = 1536
CACHE = 1024


def draw_decay_rate(key, part):
    key_a, key_b, key_c = jax.random.split(jax.random.fold_in(key, 11), 3)
    slow = jnp.exp(jax.random.uniform(key_a, (SSM_HEADS,), minval=math.log(0.05 / TOKENS), maxval=math.log(0.4 / TOKENS)))
    quick = jax.random.uniform(key_b, (SSM_HEADS,), minval=0.02, maxval=0.04)
    share = 0.5
    picked = jax.random.uniform(key_c, (SSM_HEADS,)) < share
    return jnp.where(picked, quick, slow).astype(jnp.float32)


def draw_forget(key, part):
    key_a, key_b = jax.random.split(jax.random.fold_in(key, 12), 2)
    spots = jax.random.randint(key_a, (4,), 0, TOKENS)
    amount = jax.random.uniform(key_b, (4,), minval=0.2, maxval=0.4)
    hits = (jnp.arange(TOKENS, dtype=jnp.int32)[:, None] == spots[None, :]).astype(jnp.float32)
    return jnp.dot(hits, amount).astype(jnp.float32)


def draw_queries(key, part):
    key_a = jax.random.fold_in(jax.random.fold_in(key, 13), 0)
    base = jax.random.normal(key_a, (TOKENS, ATT_HEADS * ATT_DIM))
    return jnp.clip(base, -48.0, 48.0).astype(jnp.bfloat16)


def cache_codes(key):
    spread = jax.random.uniform(key, (CACHE, KV_HEADS * ATT_DIM), minval=-127.0, maxval=127.0)
    return jnp.clip(jnp.floor(spread + 0.5), -127.0, 127.0).astype(jnp.bfloat16)


def draw_cache_keys(key, part):
    return cache_codes(jax.random.fold_in(key, 14))


def draw_cache_values(key, part):
    return cache_codes(jax.random.fold_in(key, 15))


def block_scale(own_key, dims, cuts, smallest, high):
    factor_of, own = 1.0, jax.random.fold_in(own_key, 6)
    for axis_at, parts in cuts:
        draws = jnp.exp(jax.random.uniform(jax.random.fold_in(own, axis_at), (parts,), jnp.float32, smallest / len(cuts), high / len(cuts)))
        factor_of = factor_of * jnp.repeat(draws, dims[axis_at] // parts).reshape([-1 if axis == axis_at else 1 for axis in range(len(dims))])
    return factor_of


def bell_draw(key, shape, scale, limit, pieces=(), kind=jnp.bfloat16):
    array = scale * jax.random.normal(key, shape, jnp.float32)
    if pieces:
        array = array * block_scale(key, shape, pieces, -0.22, 0.18)
    return jnp.clip(array, -limit, limit).astype(kind)


def setup_inputs(seed: int = 0) -> dict:
    key_list = jax.random.split(jax.random.key(seed), 15)
    return {
        "ssm_input": bell_draw(key_list[0], (TOKENS, SSM_HEADS * HEAD_DIM), 1.0, 6.0, ((0, 8), (1, 4))),
        "state_in": bell_draw(key_list[1], (TOKENS, GROUPS * STATE), STATE ** -0.5, 0.375, ((0, 8),)),
        "state_out": bell_draw(key_list[2], (TOKENS, GROUPS * STATE), TOKENS ** -0.5, 0.15625, ((0, 8),)),
        "step_size": jnp.clip(0.5 + 1.0 * jax.random.uniform(key_list[3], (TOKENS, SSM_HEADS), jnp.float32) ** block_scale(key_list[3], (TOKENS, SSM_HEADS), ((0, 8), (1, 4)), -0.2, 0.2), 0.5, 1.5),
        "decay_rate": draw_decay_rate(jax.random.fold_in(key_list[14], 71), 0),
        "forget": draw_forget(jax.random.fold_in(key_list[14], 71), 0),
        "skip_gain": jnp.clip(1.0 + 0.15 * jax.random.normal(key_list[6], (SSM_HEADS,), jnp.float32), 0.25, 1.75),
        "queries": draw_queries(jax.random.fold_in(key_list[14], 71), 0),
        "new_keys": bell_draw(key_list[8], (TOKENS, KV_HEADS * ATT_DIM), 1.0, 6.0, ((0, 8),)),
        "new_values": bell_draw(key_list[9], (TOKENS, KV_HEADS * ATT_DIM), 1.0, 6.0, ((0, 8),)),
        "cache_keys": draw_cache_keys(jax.random.fold_in(key_list[14], 71), 0),
        "cache_values": draw_cache_values(jax.random.fold_in(key_list[14], 71), 0),
        "cache_key_scale": jnp.clip(jnp.exp(jax.random.uniform(key_list[12], (KV_HEADS * ATT_DIM,), jnp.float32, math.log(0.003), math.log(0.03))), 0.003, 0.03),
        "cache_value_scale": jnp.clip(jnp.exp(jax.random.uniform(key_list[13], (KV_HEADS * ATT_DIM,), jnp.float32, math.log(0.003), math.log(0.03))), 0.003, 0.03),
    }


NEG = -1.0e30


def head_maps(maps, choose):
    highest = lax.Precision.HIGHEST
    length = maps.shape[0]
    grouped = maps.reshape(length, GROUPS, STATE)
    return jnp.einsum('tgn,hg->thn', grouped, choose, precision=highest)


def span_parts(rate, inputs, in_heads, out_heads):
    highest = lax.Precision.HIGHEST
    length = rate.shape[0]
    lower = jnp.tril(jnp.ones((length, length), jnp.float32))
    running = jnp.dot(lower, rate, precision=highest)
    gram = jnp.einsum('thn,shn->hts', out_heads, in_heads, precision=highest)
    across = running.T
    spread = across[:, :, None] - across[:, None, :]
    causal = lower[None, :, :] > 0.0
    weight = jnp.where(causal, jnp.exp(jnp.where(causal, spread, 0.0)), 0.0) * gram
    within = jnp.einsum('hts,shp->thp', weight, inputs, precision=highest)
    final = running[length - 1]
    tail = jnp.exp(final[None, :] - running)
    local = jnp.einsum('sh,shp,shn->hpn', tail, inputs, in_heads, precision=highest)
    return running, within, local, jnp.exp(final)


def prior_term(running, out_heads, carried):
    highest = lax.Precision.HIGHEST
    return jnp.exp(running)[:, :, None] * jnp.einsum('thn,hpn->thp', out_heads, carried, precision=highest)


def ssd_layer(ssm_input, state_in, state_out, step_size, decay_rate, forget, skip_gain):
    blocks = TOKENS // TOK_DEV
    rate = -decay_rate[None, :] * step_size - forget[:, None]
    signal = ssm_input.astype(jnp.float32).reshape(TOKENS, SSM_HEADS, HEAD_DIM)
    inputs = signal * step_size[:, :, None]
    head_group = jnp.arange(SSM_HEADS, dtype=jnp.int32) // (SSM_HEADS // GROUPS)
    choose = (head_group[:, None] == jnp.arange(GROUPS, dtype=jnp.int32)[None, :]).astype(jnp.float32)

    def advance(carried, item):
        rate_b, input_b, in_b, out_b, signal_b = item
        in_heads = head_maps(in_b, choose)
        out_heads = head_maps(out_b, choose)
        running, within, local, decay = span_parts(rate_b, input_b, in_heads, out_heads)
        mixed = within + prior_term(running, out_heads, carried) + skip_gain[None, :, None] * signal_b
        carried = decay[:, None, None] * carried + local
        return carried, mixed

    start = jnp.zeros((SSM_HEADS, HEAD_DIM, STATE), jnp.float32)
    items = (rate.reshape(blocks, TOK_DEV, SSM_HEADS),
             inputs.reshape(blocks, TOK_DEV, SSM_HEADS, HEAD_DIM),
             state_in.astype(jnp.float32).reshape(blocks, TOK_DEV, GROUPS * STATE),
             state_out.astype(jnp.float32).reshape(blocks, TOK_DEV, GROUPS * STATE),
             signal.reshape(blocks, TOK_DEV, SSM_HEADS, HEAD_DIM))
    _, mixed = lax.scan(advance, start, items)
    return mixed.reshape(TOKENS, SSM_HEADS * HEAD_DIM).astype(jnp.bfloat16)


def attention_layer(queries, new_keys, new_values, cache_keys, cache_values, cache_key_scale, cache_value_scale):
    cache_k = (cache_keys.astype(jnp.float32) * cache_key_scale[None, :]).astype(jnp.bfloat16)
    cache_v = (cache_values.astype(jnp.float32) * cache_value_scale[None, :]).astype(jnp.bfloat16)
    keys = jnp.concatenate([cache_k, new_keys], axis=0).reshape(CACHE + TOKENS, KV_HEADS, ATT_DIM)
    values = jnp.concatenate([cache_v, new_values], axis=0).reshape(CACHE + TOKENS, KV_HEADS, ATT_DIM)
    heads = queries.reshape(TOKENS, ATT_HEADS, ATT_DIM)
    group = ATT_HEADS // KV_HEADS
    key_pos = jnp.arange(CACHE + TOKENS, dtype=jnp.int32)
    query_pos = CACHE + jnp.arange(TOKENS, dtype=jnp.int32)
    visible = key_pos[None, :] <= query_pos[:, None]

    def one_head(index):
        query = lax.dynamic_index_in_dim(heads, index, axis=1, keepdims=False)
        key_head = lax.dynamic_index_in_dim(keys, index // group, axis=1, keepdims=False)
        value_head = lax.dynamic_index_in_dim(values, index // group, axis=1, keepdims=False)
        scores = jnp.dot(query, key_head.T, preferred_element_type=jnp.float32) * (ATT_DIM ** -0.5)
        scores = jnp.where(visible, scores, NEG)
        peak = jnp.max(scores, axis=1, keepdims=True)
        weights = jnp.where(visible, jnp.exp(scores - peak), 0.0)
        total = jnp.sum(weights, axis=1, keepdims=True)
        summed = jnp.dot(weights.astype(jnp.bfloat16), value_head, preferred_element_type=jnp.float32)
        return (summed / total).astype(jnp.bfloat16)

    outputs = lax.map(one_head, jnp.arange(ATT_HEADS, dtype=jnp.int32))
    return outputs.transpose(1, 0, 2).reshape(TOKENS, ATT_HEADS * ATT_DIM)


def reference(ssm_input, state_in, state_out, step_size, decay_rate, forget, skip_gain, queries, new_keys, new_values, cache_keys, cache_values, cache_key_scale, cache_value_scale):
    ssm_output = ssd_layer(ssm_input, state_in, state_out, step_size, decay_rate, forget, skip_gain)
    attended = attention_layer(queries, new_keys, new_values, cache_keys, cache_values, cache_key_scale, cache_value_scale)
    magnitude = jnp.max(jnp.abs(new_keys.astype(jnp.float32)), axis=0)
    key_scale = (magnitude + 1e-6) / 127.0
    key_codes = (new_keys.astype(jnp.float32) / key_scale[None, :]).astype(jnp.bfloat16)
    return ssm_output, attended, key_codes, key_scale
```

```python
import functools
import jax
import jax.numpy as jnp
from jax import lax
from jax.experimental import pallas as pl
from jax.experimental.pallas import tpu as pltpu
from jax.sharding import PartitionSpec as P

SSM_HEADS = 256
HEAD_DIM = 64
STATE = 256
GROUPS = 8
ATT_HEADS = 64
KV_HEADS = 8
ATT_DIM = 128

NEG = -1e30
LOG2E = 1.4426950408889634
HIGHEST = lax.Precision.HIGHEST
MESH = pl.DeviceIdType.MESH
VMEM = pl.BlockSpec(memory_space=pltpu.VMEM)
F32 = jnp.float32
BF16 = jnp.bfloat16


def iota(shape, axis):
    return lax.broadcasted_iota(jnp.int32, shape, axis)


def lanes(start, size):
    return pl.ds(pl.multiple_of(start, 128), size)


def local_kernel(
    x_ref,
    sin_ref,
    sout_ref,
    step_ref,
    decay_ref,
    forget_ref,
    skip_ref,
    nk_ref,
    nv_ref,
    ck_ref,
    cv_ref,
    cks_ref,
    cvs_ref,
    state_ref,
    run_ref,
    fade_ref,
    at_ref,
    gram_ref,
    meta_ref,
    kvc_ref,
    kvn_ref,
):
    tokens, width = x_ref.shape
    heads = step_ref.shape[0]
    per_group = min(SSM_HEADS // GROUPS, heads)
    groups_here = heads // per_group
    z = lax.axis_index("head")
    group0 = z * heads // (SSM_HEADS // GROUPS)
    kvw = kvc_ref.shape[1] // 2
    q_heads = heads * ATT_HEADS // SSM_HEADS
    first = z * q_heads // (ATT_HEADS // KV_HEADS)
    cols = lanes(first * ATT_DIM, kvw)
    kvc_ref[:, :kvw] = (ck_ref[:, cols].astype(F32) * cks_ref[:, cols]).astype(BF16)
    kvc_ref[:, kvw:] = (cv_ref[:, cols].astype(F32) * cvs_ref[:, cols]).astype(BF16)
    kvn_ref[:, :kvw] = nk_ref[:, cols]
    kvn_ref[:, kvw:] = nv_ref[:, cols]
    meta_ref[:, width:] = jnp.max(jnp.abs(nk_ref[...].astype(F32)), axis=0, keepdims=True)

    row, col = iota((tokens, tokens), 0), iota((tokens, tokens), 1)
    lower = jnp.where(col <= row, 1.0, 0.0)
    eye = jnp.where(col == row, 1.0, 0.0)
    step = step_ref[...].T
    forgotten = jnp.sum(lower * forget_ref[...], axis=1, keepdims=True)
    decayed = jnp.dot(
        lower, decay_ref[...] * step, precision=HIGHEST, preferred_element_type=F32
    )
    running = -(decayed + forgotten) * LOG2E
    start = running - jnp.log2(step)
    at_ref[...] = start.T
    rest = jnp.concatenate(
        [running, jnp.broadcast_to(skip_ref[...], (16, heads))], axis=0
    )
    for third in range(3):
        piece = rest.astype(BF16)
        run_ref[:, third * heads : (third + 1) * heads] = piece
        rest = rest - piece.astype(F32)
    fade_ref[...] = jnp.exp2(running).astype(BF16)
    tail = jnp.exp2(running[tokens - 1 : tokens] - start).astype(BF16)
    last = running[tokens - 8 : tokens]
    block = min(512, width)
    for g in range(groups_here):
        gcols = lanes((group0 + g) * STATE, STATE)
        maps_in = sin_ref[:, gcols]
        gram_ref[g] = lax.dot_general(
            sout_ref[:, gcols], maps_in, (((1,), (1,)), ((), ())), preferred_element_type=F32
        )
        turned = lax.dot_general(
            maps_in,
            eye.astype(BF16),
            (((0,), (0,)), ((), ())),
            preferred_element_type=F32,
        ).astype(BF16)
        for b in range(per_group * HEAD_DIM // block):
            begin = g * per_group * HEAD_DIM + b * block
            here = pl.ds(begin, block)
            pick = choose(heads, begin, block)
            meta_ref[:, here] = jnp.dot(
                last, pick, precision=HIGHEST, preferred_element_type=F32
            )[7:8]
            scale = jnp.dot(tail, pick.astype(BF16), preferred_element_type=F32)
            scaled = (x_ref[:, here].astype(F32) * scale).astype(BF16)
            state_ref[:, here] = jnp.dot(
                turned, scaled, preferred_element_type=F32
            ).astype(BF16)


def choose(heads, begin, size):
    lane = begin + iota((heads, size), 1)
    return (iota((heads, size), 0) == lane // HEAD_DIM).astype(F32)


def within_pair(p, x_ref, run_ref, at_ref, gram_ref, part_ref):
    tokens = x_ref.shape[0]
    heads = run_ref.shape[1] // 3
    per_group = min(SSM_HEADS // GROUPS, heads)
    here = lanes(p * 128, 128)
    pick = choose(heads, p * 128, 128).astype(BF16)
    both = jnp.dot(
        run_ref[...], jnp.concatenate([pick] * 3, axis=0), preferred_element_type=F32
    )
    run, skip = both[:tokens], both[tokens : tokens + 1]
    x = x_ref[:, here]
    gram = gram_ref[(2 * p) // per_group]
    causal = iota((tokens, tokens), 1) <= iota((tokens, tokens), 0)

    def one(k):
        spread = run[:, k * HEAD_DIM : k * HEAD_DIM + 1] - at_ref[pl.ds(2 * p + k, 1), :]
        return (jnp.exp2(jnp.where(causal, spread, NEG)) * gram).astype(BF16)

    pair = jnp.dot(
        jnp.concatenate([one(0), one(1)], axis=0), x, preferred_element_type=F32
    )
    y = jnp.where(iota((tokens, 128), 1) < HEAD_DIM, pair[:tokens], pair[tokens:])
    part_ref[:, here] = (y + skip * x.astype(F32)).astype(BF16)


def attend(h, q_ref, allc_ref, alln_ref, bias_ref, vc_ref, vn_ref, att_ref):
    q_heads = q_ref.shape[1] // ATT_DIM
    kv_here = vc_ref.shape[0]
    share = q_heads // kv_here
    together = 2 if share % 2 == 0 else 1
    tokens = q_ref.shape[0]
    k = (h * together) // share
    factor = ATT_DIM**-0.5 * LOG2E
    nt = (((1,), (1,)), ((), ()))
    own = [lanes((h * together + e) * ATT_DIM, ATT_DIM) for e in range(together)]
    q = jnp.concatenate([q_ref[:, o] for o in own], axis=0)
    at = lanes(k * ATT_DIM, ATT_DIM)
    keys_c = allc_ref[:, :, at].reshape(-1, ATT_DIM)
    keys_n = alln_ref[:, :, at].reshape(-1, ATT_DIM)
    old = lax.dot_general(q, keys_c, nt, preferred_element_type=F32)
    new = lax.dot_general(q, keys_n, nt, preferred_element_type=F32)
    bias = bias_ref[...]
    new = (new.reshape(together, tokens, -1) + bias[None]).reshape(together * tokens, -1)
    peak = jnp.maximum(
        jnp.max(old, axis=1, keepdims=True), jnp.max(new, axis=1, keepdims=True)
    )
    old = jnp.exp2((old - peak) * factor).astype(BF16)
    new = jnp.exp2((new - peak) * factor).astype(BF16)
    both = jnp.dot(old, vc_ref[k], preferred_element_type=F32) + jnp.dot(
        new, vn_ref[k], preferred_element_type=F32
    )
    result = (both[:, :ATT_DIM] / both[:, ATT_DIM:]).astype(BF16)
    for e in range(together):
        att_ref[:, own[e]] = result[e * tokens : (e + 1) * tokens]


def comm_kernel(
    n,
    chunks,
    state_ref,
    kvc_ref,
    kvn_ref,
    meta_ref,
    x_ref,
    run_ref,
    at_ref,
    gram_ref,
    q_ref,
    out_ref,
    allm_ref,
    part_ref,
    att_ref,
    allc_ref,
    alln_ref,
    vc_ref,
    vn_ref,
    bias_ref,
    sib_ref,
    own_ref,
    incl_ref,
    recv_ref,
    back_ref,
    meta_s,
    meta_r,
    kv_s,
    kv_r,
    kv_f,
    sib_s,
    sib_r,
    pre_s,
    pre_r,
    rel_s,
    back_s,
    back_r,
):
    n2 = n // 2
    levels = n2.bit_length() - 1
    me = lax.axis_index("seq")
    i, c = me % 2, me // 2
    other = me + 1 - 2 * i
    width = state_ref.shape[1]
    half = width // 2
    size = half // chunks

    barrier = pltpu.get_barrier_semaphore()
    for d in range(1, n):
        pl.semaphore_signal(
            barrier, inc=1, device_id={"seq": (me + d) % n}, device_id_type=MESH
        )
    pl.semaphore_wait(barrier, n - 1)

    def remote(src, dst, ssem, rsem, to):
        return pltpu.make_async_remote_copy(
            src_ref=src,
            dst_ref=dst,
            send_sem=ssem,
            recv_sem=rsem,
            device_id={"seq": to},
            device_id_type=MESH,
        )

    def sib_copy(j):
        return remote(
            state_ref.at[:, lanes((1 - i) * half + j * size, size)],
            sib_ref.at[j],
            sib_s.at[j],
            sib_r.at[j],
            other,
        )

    for j in range(chunks):
        sib_copy(j).start()
    for d in range(1, n):
        remote(
            meta_ref, allm_ref.at[me], meta_s.at[d], meta_r.at[me], (me + d) % n
        ).start()

    def cache_copy(d, to):
        return remote(kvc_ref, allc_ref.at[me], kv_s.at[0, d], kv_r.at[0, me], to)

    def new_copy(d, to):
        return remote(kvn_ref, alln_ref.at[me], kv_s.at[1, d], kv_r.at[1, me], to)

    cache_copy(0, other).start()
    new_copy(0, other).start()
    for d in range(1, n2):
        to = ((c + d) % n2) * 2 + i
        cache_copy(d, to).start()

        @pl.when(c + d < n2)
        def _():
            new_copy(d, to).start()

    allm_ref[me] = meta_ref[...]
    allc_ref[me] = kvc_ref[...]
    alln_ref[me] = kvn_ref[...]
    for d in range(1, n2):
        later = c + d

        @pl.when(later < n2)
        def _():
            for k in range(2):
                alln_ref[later * 2 + k] = jnp.zeros(kvn_ref.shape, BF16)

    for d in range(1, n):
        r = (me + d) % n
        remote(meta_ref, allm_ref.at[r], meta_s.at[d], meta_r.at[r], r).wait_recv()

    def sends(l):
        return c % (2 ** (l + 1)) == 2**l - 1

    def targets(l):
        return [0] if l == 0 else list(range(1, 2**l, 2))

    def pre_copy(l, j, r):
        return remote(
            incl_ref.at[l, j],
            recv_ref.at[l, j],
            pre_s.at[l, j, r],
            pre_r.at[l, j],
            ((c + 1 + r) % n2) * 2 + i,
        )

    def relay_copy(l, j):
        return remote(
            recv_ref.at[l, j],
            recv_ref.at[l, j],
            rel_s.at[l, j],
            pre_r.at[l, j],
            ((c + n2 - 1) % n2) * 2 + i,
        )

    def logs(r, j):
        return allm_ref[r, :, lanes(i * half + j * size, size)]

    def gather_first(j, _):
        sib_copy(j).wait_recv()
        mine = state_ref[:, lanes(i * half + j * size, size)].astype(F32)
        theirs = sib_ref[j].astype(F32)
        d1 = jnp.exp2(logs(2 * c + 1, j))
        total = jnp.where(i == 0, d1 * mine + theirs, d1 * theirs + mine)
        incl_ref[0, j] = total.astype(BF16)
        own_ref[j] = jnp.zeros(own_ref.shape[1:], F32)

        @pl.when(sends(0))
        def _():
            pre_copy(0, j, 0).start()

        return 0

    lax.fori_loop(0, chunks, gather_first, 0)
    fresh = bias_ref.shape[1]
    tokens = x_ref.shape[0]
    seen = iota((tokens, fresh), 1) <= me * tokens + iota((tokens, fresh), 0)
    bias_ref[...] = jnp.where(seen, 0.0, NEG)
    pairs = width // 128
    early = n2
    ahead = pairs * 3 // 4

    def pair(p, _):
        within_pair(p, x_ref, run_ref, at_ref, gram_ref, part_ref)
        return 0


    def forward(kind, d):
        src = allc_ref if kind == 0 else alln_ref
        slot = ((c + d) % n2) * 2 + i
        return remote(
            src.at[slot], src.at[slot], kv_f.at[kind, d], kv_r.at[kind, slot], other
        )

    def combine(j, _):
        for l in range(levels):

            @pl.when(c % (2 ** (l + 1)) >= 2**l)
            def _():
                pre_copy(l, j, 0).wait_recv()
                if l >= 1:

                    @pl.when(c % 2 == 1)
                    def _():
                        relay_copy(l, j).start()

                base = c - c % (2**l)
                logsum = jnp.zeros((1, size), F32)
                for back in range(1, 2**l):
                    at = (c + n2 - back) % n2
                    both = logs(2 * at, j) + logs(2 * at + 1, j)
                    logsum += jnp.where(c - back >= base, both, 0.0)
                own_ref[j] = jnp.exp2(logsum) * recv_ref[l, j].astype(F32) + own_ref[j]

            if l + 1 < levels:

                @pl.when(sends(l + 1))
                def _():
                    keep = jnp.exp2(logs(2 * c, j) + logs(2 * c + 1, j))
                    incl_ref[l + 1, j] = (
                        keep * own_ref[j] + incl_ref[0, j].astype(F32)
                    ).astype(BF16)
                    for r in targets(l + 1):
                        pre_copy(l + 1, j, r).start()

        enter = own_ref[j]
        mine = state_ref[:, lanes(i * half + j * size, size)].astype(F32)
        first = jnp.where(i == 0, mine, sib_ref[j].astype(F32))
        middle = jnp.exp2(logs(2 * c, j)) * enter + first
        out_ref[:, lanes(i * half + j * size, size)] = jnp.where(
            i == 0, enter, middle
        ).astype(BF16)
        back_ref[j] = jnp.where(i == 0, middle, enter).astype(BF16)
        back_copy(j, i).start()
        return 0

    def remote_slot(kind, d):
        src = allc_ref if kind == 0 else alln_ref
        mine = kvc_ref if kind == 0 else kvn_ref
        slot = ((c + d) % n2) * 2 + i
        return remote(mine, src.at[slot], kv_s.at[kind, d], kv_r.at[kind, slot], slot)

    def back_copy(j, who):
        return remote(
            back_ref.at[j],
            out_ref.at[:, lanes(who * half + j * size, size)],
            back_s.at[j],
            back_r.at[j],
            other,
        )

    def first_part(j, _):
        lax.fori_loop(j * ahead // early, (j + 1) * ahead // early, pair, 0)
        for d in range(1, n2):

            @pl.when(j == d)
            def _():
                remote_slot(0, d).wait_recv()
                forward(0, d).start()

                @pl.when((c + d) % n2 < c)
                def _():
                    remote_slot(1, d).wait_recv()
                    forward(1, d).start()

        return 0

    lax.fori_loop(0, early, first_part, 0)

    def other_slot(kind, d):
        src = allc_ref if kind == 0 else alln_ref
        mine = kvc_ref if kind == 0 else kvn_ref
        slot = ((c + d) % n2) * 2 + (1 - i)
        return remote(mine, src.at[slot], kv_f.at[kind, d], kv_r.at[kind, slot], other)

    for d in range(n2):
        other_slot(0, d).wait_recv()
    other_slot(1, 0).wait_recv()
    for d in range(1, n2):

        @pl.when((c + d) % n2 < c)
        def _():
            other_slot(1, d).wait_recv()

    kv_here = vc_ref.shape[0]
    for k in range(kv_here):
        at = (kv_here + k) * ATT_DIM
        for all_ref, ext_ref in ((allc_ref, vc_ref), (alln_ref, vn_ref)):
            ext_ref[k, :, :ATT_DIM] = all_ref[:, :, at : at + ATT_DIM].reshape(-1, ATT_DIM)
            ext_ref[k, :, ATT_DIM:] = jnp.ones((ext_ref.shape[1], ATT_DIM), BF16)

    q_heads = q_ref.shape[1] // ATT_DIM
    steps = q_heads // 2 if (q_heads // kv_here) % 2 == 0 else q_heads

    def head(h, _):
        attend(h, q_ref, allc_ref, alln_ref, bias_ref, vc_ref, vn_ref, att_ref)
        return 0

    def second_part(j, _):
        rest = pairs - ahead
        lax.fori_loop(
            ahead + j * rest // chunks, ahead + (j + 1) * rest // chunks, pair, 0
        )
        lax.fori_loop(j * steps // chunks, (j + 1) * steps // chunks, head, 0)
        combine(j, 0)
        return 0

    lax.fori_loop(0, chunks, second_part, 0)

    def drain(j, _):
        back_copy(j, 1 - i).wait_recv()
        back_copy(j, i).wait_send()
        sib_copy(j).wait_send()
        for l in range(levels):

            @pl.when(sends(l))
            def _():
                for r in targets(l):
                    pre_copy(l, j, r).wait_send()

            if l >= 1:

                @pl.when((c % (2 ** (l + 1)) >= 2**l) & (c % 2 == 1))
                def _():
                    relay_copy(l, j).wait_send()

        return 0

    lax.fori_loop(0, chunks, drain, 0)
    for d in range(1, n):
        remote(
            meta_ref, allm_ref.at[me], meta_s.at[d], meta_r.at[me], (me + d) % n
        ).wait_send()
    cache_copy(0, other).wait_send()
    new_copy(0, other).wait_send()
    for d in range(1, n2):
        to = ((c + d) % n2) * 2 + i
        cache_copy(d, to).wait_send()
        forward(0, d).wait_send()

        @pl.when(c + d < n2)
        def _():
            new_copy(d, to).wait_send()

        @pl.when((c + d) % n2 < c)
        def _():
            forward(1, d).wait_send()


def final_kernel(
    part_ref,
    fade_ref,
    sout_ref,
    state_ref,
    meta_ref,
    nk_ref,
    y_ref,
    code_ref,
    scale_ref,
):
    tokens, width = part_ref.shape
    heads = fade_ref.shape[1]
    per_group = min(SSM_HEADS // GROUPS, heads)
    z = lax.axis_index("head")
    group0 = z * heads // (SSM_HEADS // GROUPS)
    block = min(512, width)

    magnitude = jnp.max(meta_ref[:, 0, width:], axis=0, keepdims=True)
    scale = (magnitude + 1e-6) / 127.0
    scale_ref[...] = scale
    code_ref[...] = (nk_ref[...].astype(F32) / scale).astype(BF16)
    fade = fade_ref[...]
    for b in range(width // block):
        here = pl.ds(b * block, block)
        g = group0 + (b * block) // (per_group * HEAD_DIM)
        prior = jnp.dot(
            sout_ref[:, lanes(g * STATE, STATE)], state_ref[:, here], preferred_element_type=F32
        )
        pick = choose(heads, b * block, block).astype(BF16)
        spread = jnp.dot(fade, pick, preferred_element_type=F32)
        y_ref[:, here] = (part_ref[:, here].astype(F32) + spread * prior).astype(BF16)


def body(
    n,
    ssm_input,
    state_in,
    state_out,
    step_size,
    decay_rate,
    forget,
    skip_gain,
    queries,
    new_keys,
    new_values,
    cache_keys,
    cache_values,
    cache_key_scale,
    cache_value_scale,
):
    tokens, width = ssm_input.shape
    heads = step_size.shape[1]
    rows = cache_keys.shape[0]
    channels = new_keys.shape[1]
    q_heads = queries.shape[1] // ATT_DIM
    kv_here = max(1, q_heads // (ATT_HEADS // KV_HEADS))
    kvw = kv_here * ATT_DIM
    per_group = min(SSM_HEADS // GROUPS, heads)
    groups_here = heads // per_group
    limit = pltpu.CompilerParams(vmem_limit_bytes=60 * 1024 * 1024)
    shape = jax.ShapeDtypeStruct
    state, run, fade, at, gram, meta, kvc, kvn = pl.pallas_call(
        local_kernel,
        out_shape=(
            shape((STATE, width), BF16),
            shape((tokens + 16, 3 * heads), BF16),
            shape((tokens, heads), BF16),
            shape((heads, tokens), F32),
            shape((groups_here, tokens, tokens), F32),
            shape((1, width + channels), F32),
            shape((rows, 2 * kvw), BF16),
            shape((tokens, 2 * kvw), BF16),
        ),
        in_specs=[VMEM] * 13,
        out_specs=(VMEM,) * 8,
        compiler_params=limit,
        name="local",
    )(
        ssm_input,
        state_in,
        state_out,
        step_size.T,
        decay_rate.reshape(1, heads),
        forget.reshape(1, tokens),
        skip_gain.reshape(1, heads),
        new_keys,
        new_values,
        cache_keys,
        cache_values,
        cache_key_scale.reshape(1, channels),
        cache_value_scale.reshape(1, channels),
    )
    half = width // 2
    size = min(256, half)
    chunks = half // size
    n2 = n // 2
    levels = n2.bit_length() - 1
    fan = max(1, n2 // 2)
    dma = pltpu.SemaphoreType.DMA
    carried, allm, part, attended = pl.pallas_call(
        functools.partial(comm_kernel, n, chunks),
        out_shape=(
            shape((STATE, width), BF16),
            shape((n, 1, width + channels), F32),
            shape((tokens, width), BF16),
            shape((tokens, queries.shape[1]), BF16),
        ),
        in_specs=[VMEM] * 9,
        out_specs=(VMEM,) * 4,
        scratch_shapes=[
            pltpu.VMEM((n, rows, 2 * kvw), BF16),
            pltpu.VMEM((n, tokens, 2 * kvw), BF16),
            pltpu.VMEM((kv_here, n * rows, 2 * ATT_DIM), BF16),
            pltpu.VMEM((kv_here, n * tokens, 2 * ATT_DIM), BF16),
            pltpu.VMEM((tokens, n * tokens), F32),
            pltpu.VMEM((chunks, STATE, size), BF16),
            pltpu.VMEM((chunks, STATE, size), F32),
            pltpu.VMEM((levels, chunks, STATE, size), BF16),
            pltpu.VMEM((levels, chunks, STATE, size), BF16),
            pltpu.VMEM((chunks, STATE, size), BF16),
            dma((n,)),
            dma((n,)),
            dma((2, n2)),
            dma((2, n)),
            dma((2, n2)),
            dma((chunks,)),
            dma((chunks,)),
            dma((levels, chunks, fan)),
            dma((levels, chunks)),
            dma((levels, chunks)),
            dma((chunks,)),
            dma((chunks,)),
        ],
        compiler_params=pltpu.CompilerParams(
            collective_id=0, has_side_effects=True, vmem_limit_bytes=60 * 1024 * 1024
        ),
        name="exchange",
    )(state, kvc, kvn, meta, ssm_input, run, at, gram, queries)
    y, codes, scale = pl.pallas_call(
        final_kernel,
        out_shape=(
            shape((tokens, width), BF16),
            shape((tokens, channels), BF16),
            shape((1, channels), F32),
        ),
        in_specs=[VMEM] * 6,
        out_specs=(VMEM,) * 3,
        compiler_params=limit,
        name="finish",
    )(part, fade, state_out, carried, allm, new_keys)
    return (y, attended, codes, scale.reshape(channels))

BLOCK = 96


def span_blocks(tokens):
    return max(1, tokens // BLOCK)


def split2(value):
    high = value.astype(BF16)
    low = (value - high.astype(F32)).astype(BF16)
    return jnp.concatenate([high, low], axis=1)


def choose2(heads, begin, size):
    lane = begin + iota((2 * heads, size), 1)
    row = iota((2 * heads, size), 0)
    return (row % heads == lane // HEAD_DIM).astype(BF16)


def factor_rows(tokens):
    nb = span_blocks(tokens)
    size = tokens // nb
    places, at = {}, 0
    for name, rows in (
        [("z", tokens), ("tail", 16)]
        + [(f"z{b}", (b + 1) * size) for b in range(nb - 1)]
        + [("out", tokens), ("skip", 16), ("fade", tokens)]
    ):
        places[name] = (at, at + rows)
        at += rows
    return places, at


def with_ones(v):
    return jnp.concatenate([v, jnp.ones(v.shape, BF16)], axis=1)


def attend_visible(step, streams, together, chip, q_ref, allc_ref, alln_ref, bias_ref, att_ref):
    tokens = q_ref.shape[0]
    kvw = allc_ref.shape[2] // 2
    share = (q_ref.shape[1] // ATT_DIM) // (kvw // ATT_DIM)
    factor = ATT_DIM**-0.5 * LOG2E
    nt = (((1,), (1,)), ((), ()))
    k = (step * streams * together) // share
    at, av = lanes(k * ATT_DIM, ATT_DIM), lanes(kvw + k * ATT_DIM, ATT_DIM)
    seen = 2 * chip + 2

    def rows_of(cols):
        return jnp.concatenate(
            [
                allc_ref[:, :, cols].reshape(-1, ATT_DIM),
                alln_ref[:seen, :, cols].reshape(-1, ATT_DIM),
            ],
            axis=0,
        )

    keys, values = rows_of(at), with_ones(rows_of(av))
    free = keys.shape[0] - 2 * tokens
    own, scores = [], []
    for e in range(streams):
        first = (step * streams + e) * together
        own.append([lanes((first + f) * ATT_DIM, ATT_DIM) for f in range(together)])
        q = jnp.concatenate([q_ref[:, o] for o in own[e]], axis=0)
        scores.append(lax.dot_general(q, keys, nt, preferred_element_type=F32))
    bias = bias_ref[...]
    for e in range(streams):
        near = scores[e][:, free:].reshape(together, tokens, -1) + bias[None]
        s = jnp.concatenate([scores[e][:, :free], near.reshape(together * tokens, -1)], axis=1)
        peak = jnp.max(s, axis=1, keepdims=True)
        p = jnp.exp2((s - peak) * factor).astype(BF16)
        both = jnp.dot(p, values, preferred_element_type=F32)
        result = (both[:, :ATT_DIM] / both[:, ATT_DIM:]).astype(BF16)
        for f, o in enumerate(own[e]):
            att_ref[:, o] = result[f * tokens : (f + 1) * tokens]


def fused_kernel(
    chunks,
    x_hbm,
    sin_hbm,
    sout_hbm,
    step_ref,
    decay_ref,
    forget_ref,
    skip_ref,
    q_hbm,
    nk_hbm,
    nv_hbm,
    ck_hbm,
    cv_hbm,
    cks_ref,
    cvs_ref,
    y_ref,
    att_ref,
    mag_ref,
    x_ref,
    sin_ref,
    sout_ref,
    q_ref,
    nk_ref,
    nv_ref,
    ck_ref,
    cv_ref,
    kvc_ref,
    kvn_ref,
    allc_ref,
    alln_ref,
    bias_ref,
    meta_ref,
    allm_ref,
    fac_ref,
    fade_ref,
    z_ref,
    gram_ref,
    turned_ref,
    give_ref,
    sib_ref,
    mine_ref,
    full_ref,
    tx_ref,
    rx_ref,
    enter_ref,
    back_ref,
    other_ref,
    load_s,
    meta_s,
    meta_r,
    kv_s,
    kv_r,
    kv_f,
    kv_p,
    sib_s,
    sib_r,
    out_s,
    in_r,
    back_s,
    back_r,
):
    n = 8
    tokens, width = x_ref.shape
    heads = step_ref.shape[0]
    per_group = min(SSM_HEADS // GROUPS, heads)
    groups_here = heads // per_group
    channels = nk_ref.shape[1]
    kvw = kvc_ref.shape[1] // 2
    half = width // 2
    size = half // chunks
    near = chunks // 2
    places, _ = factor_rows(tokens)
    nb = span_blocks(tokens)
    bs = tokens // nb

    me = lax.axis_index("seq")
    z = lax.axis_index("head")
    i, c = me % 2, me // 2
    other = me + 1 - 2 * i
    cx, cy = c + 1 - 2 * (c % 2), (c + 2) % 4
    cd = 3 - c
    group0 = z * heads // (SSM_HEADS // GROUPS)
    q_heads = heads * ATT_HEADS // SSM_HEADS
    first_kv = z * q_heads // (ATT_HEADS // KV_HEADS)
    cols = lanes(first_kv * ATT_DIM, kvw)
    gcols = lanes(group0 * STATE, groups_here * STATE)

    barrier = pltpu.get_barrier_semaphore()
    for d in range(1, n):
        pl.semaphore_signal(
            barrier, inc=1, device_id={"seq": (me + d) % n}, device_id_type=MESH
        )

    loads = [
        pltpu.make_async_copy(src, dst, load_s.at[k])
        for k, (src, dst) in enumerate(
            [
                (ck_hbm.at[:, cols], ck_ref),
                (cv_hbm.at[:, cols], cv_ref),
                (nk_hbm, nk_ref),
                (nv_hbm.at[:, cols], nv_ref),
                (sin_hbm.at[:, gcols], sin_ref),
                (sout_hbm.at[:, gcols], sout_ref),
                (x_hbm, x_ref),
                (q_hbm, q_ref),
            ]
        )
    ]
    for copy in loads:
        copy.start()

    def remote(src, dst, ssem, rsem, to):
        return pltpu.make_async_remote_copy(
            src_ref=src,
            dst_ref=dst,
            send_sem=ssem,
            recv_sem=rsem,
            device_id={"seq": to},
            device_id_type=MESH,
        )

    def dev(chip):
        return chip * 2 + i

    alls = (allc_ref, alln_ref)
    owns = (kvc_ref, kvn_ref)

    def own_copy(kind, way):
        to = (other, dev(cx), dev(cy))[way]
        return remote(
            owns[kind], alls[kind].at[me], kv_s.at[kind, way], kv_r.at[kind, me], to
        )

    def pass_copy(kind, way, chip, to):
        slot = dev(chip)
        return remote(
            alls[kind].at[slot],
            alls[kind].at[slot],
            kv_p.at[kind, way],
            kv_r.at[kind, slot],
            dev(to),
        )

    def forward(kind, chip):
        slot = dev(chip)
        return remote(
            alls[kind].at[slot],
            alls[kind].at[slot],
            kv_f.at[kind, chip],
            kv_r.at[kind, slot],
            other,
        )

    def arrived(kind, slot):
        remote(
            owns[kind], alls[kind].at[slot], kv_s.at[kind, 0], kv_r.at[kind, slot], other
        ).wait_recv()

    loads[0].wait()
    loads[1].wait()
    kvc_ref[:, :kvw] = (ck_ref[...].astype(F32) * cks_ref[:, cols]).astype(BF16)
    kvc_ref[:, kvw:] = (cv_ref[...].astype(F32) * cvs_ref[:, cols]).astype(BF16)
    pl.semaphore_wait(barrier, n - 1)
    for way in (1, 2, 0):
        own_copy(0, way).start()
    loads[2].wait()
    loads[3].wait()
    kvn_ref[:, :kvw] = nk_ref[:, cols]
    kvn_ref[:, kvw:] = nv_ref[...]

    @pl.when(cx > c)
    def _():
        own_copy(1, 1).start()

    @pl.when(cy > c)
    def _():
        own_copy(1, 2).start()

    own_copy(1, 0).start()

    row, col = iota((tokens, tokens), 0), iota((tokens, tokens), 1)
    lower = jnp.where(col <= row, 1.0, 0.0)
    eye = jnp.where(col == row, 1.0, 0.0).astype(BF16)
    step = step_ref[...].T
    forgotten = jnp.sum(lower * forget_ref[...], axis=1, keepdims=True)
    decayed = jnp.dot(
        lower, decay_ref[...] * step, precision=HIGHEST, preferred_element_type=F32
    )
    running = -(decayed + forgotten) * LOG2E
    start = running - jnp.log2(step)
    last = running[tokens - 1 : tokens]
    middles = [running[b * bs + bs // 2 - 1 : b * bs + bs // 2] for b in range(nb)]

    meta_ref[:, :channels] = jnp.max(jnp.abs(nk_ref[...].astype(F32)), axis=0, keepdims=True)
    meta_ref[:, channels:] = jnp.concatenate([last, jnp.zeros((1, 128 - heads), F32)], axis=1)

    def meta_copy(d):
        return remote(
            meta_ref, allm_ref.at[me], meta_s.at[d], meta_r.at[me], (me + d) % n
        )

    def meta_arrived(r):
        remote(meta_ref, allm_ref.at[r], meta_s.at[1], meta_r.at[r], r).wait_recv()

    for d in range(1, n):
        meta_copy(d).start()
    allm_ref[me] = meta_ref[...]

    def put(name, value):
        begin, end = places[name]
        fac_ref[begin:end] = split2(jnp.broadcast_to(value, (end - begin, heads)))

    put("z", jnp.exp2(middles[nb - 1] - start))
    put("tail", jnp.exp2(last - middles[nb - 1]))
    for b in range(nb - 1):
        put(f"z{b}", jnp.exp2(middles[b] - start[: (b + 1) * bs]))
    put(
        "out",
        jnp.concatenate(
            [jnp.exp2(running[b * bs : (b + 1) * bs] - middles[b]) for b in range(nb)], axis=0
        ),
    )
    put("skip", skip_ref[...])
    put("fade", jnp.exp2(running))
    loads[4].wait()
    loads[5].wait()
    for g in range(groups_here):
        gc = slice(g * STATE, (g + 1) * STATE)
        maps_in = sin_ref[:, gc]
        gram = lax.dot_general(
            sout_ref[:, gc], maps_in, (((1,), (1,)), ((), ())), preferred_element_type=F32
        )
        gram_ref[g] = jnp.where(col <= row, gram, 0.0).astype(BF16)
        turned_ref[g] = lax.dot_general(
            maps_in, eye, (((0,), (0,)), ((), ())), preferred_element_type=F32
        ).astype(BF16)
    loads[6].wait()

    def spread(first, final, begin):
        rows = fac_ref[places[first][0] : places[final][1]]
        return jnp.dot(rows, choose2(heads, begin, size), preferred_element_type=F32)

    def local_state(begin):
        here = lanes(begin, size)
        by = spread("z", "tail", begin)
        scaled = (x_ref[:, here].astype(F32) * by[:tokens]).astype(BF16)
        z_ref[:, here] = scaled
        sums = jnp.dot(
            turned_ref[begin // (per_group * HEAD_DIM)], scaled, preferred_element_type=F32
        )
        return (sums * by[tokens : tokens + 1]).astype(BF16)

    def sib_copy(j):
        return remote(give_ref.at[j], sib_ref.at[j], sib_s.at[j], sib_r.at[j], other)

    shift = (c % 2) * (1 - c // 2) * near

    def give(s, _):
        j = (s + shift) % chunks
        give_ref[j] = local_state((1 - i) * half + j * size)
        sib_copy(j).start()
        return 0

    lax.fori_loop(0, chunks, give, 0)
    meta_arrived(other)

    def logs_of(r):
        return allm_ref[r, :, channels : channels + heads]

    def set_fades(third):
        logs = jnp.concatenate(
            [logs_of(2 * c), logs_of(2 * c + 1), third, jnp.zeros((13, heads), F32)], axis=0
        )
        fade_ref[...] = split2(jnp.exp2(logs))

    def fades(j):
        return jnp.dot(
            fade_ref[...], choose2(heads, i * half + j * size, size), preferred_element_type=F32
        )

    set_fades(jnp.zeros((1, heads), F32))

    def full_copy(j):
        slot = jnp.where(c == 0, 0, 1)
        return remote(
            full_ref.at[j], rx_ref.at[slot, j], out_s.at[0, j], in_r.at[slot, j], dev(cx)
        )

    def full_sent(j):
        return (c == 0) | ((c == 1) & (j >= near)) | ((c == 2) & (j < near))

    def own(s, _):
        j = (s + shift) % chunks
        mine = local_state(i * half + j * size)
        mine_ref[j] = mine
        sib_copy(j).wait_recv()
        mine, theirs = mine.astype(F32), sib_ref[j].astype(F32)
        d1 = fades(j)[1:2]
        full_ref[j] = jnp.where(i == 0, d1 * mine + theirs, d1 * theirs + mine).astype(BF16)

        @pl.when(full_sent(j))
        def _():
            full_copy(j).start()

        return 0

    lax.fori_loop(0, chunks, own, 0)

    def pass_cache():
        arrived(0, dev(cx))

        @pl.when(c >= 1)
        def _():
            pass_copy(0, 0, cx, cy).start()

        forward(0, cx).start()
        arrived(0, dev(cy))

        @pl.when(c == 3)
        def _():
            pass_copy(0, 1, cy, cx).start()

        forward(0, cy).start()

    pass_cache()
    bias_ref[...] = jnp.where(
        iota((tokens, 2 * tokens), 1) <= i * tokens + iota((tokens, 2 * tokens), 0), 0.0, NEG
    )

    def within(s, _):
        begin = s * size
        here = lanes(begin, size)
        by = spread("z0" if nb > 1 else "out", "skip", begin)
        at = 0
        gram = gram_ref[begin // (per_group * HEAD_DIM)]
        x = x_ref[:, here].astype(F32)
        parts = []
        for b in range(nb):
            high = (b + 1) * bs
            if b + 1 < nb:
                scaled = (x[:high] * by[at : at + high]).astype(BF16)
                at += high
            else:
                scaled = z_ref[:, here]
            parts.append(
                jnp.dot(gram[b * bs : high, :high], scaled, preferred_element_type=F32)
            )
        y = by[at : at + tokens] * jnp.concatenate(parts, axis=0)
        y_ref[:, here] = (y + by[at + tokens : at + tokens + 1] * x).astype(BF16)
        return 0

    lax.fori_loop(0, 2 * chunks, within, 0)

    arrived(0, dev(cd))
    forward(0, cd).start()

    @pl.when(cx < c)
    def _():
        arrived(1, dev(cx))

        @pl.when(c == 1)
        def _():
            pass_copy(1, 0, cx, cy).start()

        forward(1, cx).start()

    @pl.when(cy < c)
    def _():
        arrived(1, dev(cy))

        @pl.when(c == 3)
        def _():
            pass_copy(1, 1, cy, cx).start()

        forward(1, cy).start()

    for d in range(1, n):
        r = (me + d) % n

        @pl.when(r != other)
        def _():
            meta_arrived(r)

    chip = jnp.where(c == 0, 1, jnp.where(c == 3, 2, c))
    set_fades(logs_of(2 * chip) + logs_of(2 * chip + 1))
    mag_ref[...] = jnp.max(allm_ref[:, 0, :channels], axis=0, keepdims=True)

    @pl.when(cd < c)
    def _():
        arrived(1, dev(cd))
        forward(1, cd).start()

    allc_ref[me] = kvc_ref[...]
    alln_ref[me] = kvn_ref[...]
    arrived(0, other)
    arrived(1, other)
    for d in range(1, 4):
        there = (c + d) % 4
        arrived(0, there * 2 + 1 - i)

        @pl.when(there < c)
        def _():
            arrived(1, there * 2 + 1 - i)

    loads[7].wait()

    def order(s):
        left = (1 - c // 2) * ((s + near) % chunks) + (c // 2) * (near * (1 - s % 2) + s // 2)
        return (c % 2) * s + (1 - c % 2) * left

    def prior(begin, carried):
        here = lanes(begin, size)
        group = begin // (per_group * HEAD_DIM)
        term = jnp.dot(sout_ref[:, lanes(group * STATE, STATE)], carried, preferred_element_type=F32)
        by = spread("fade", "fade", begin)
        y_ref[:, here] = (y_ref[:, here].astype(F32) + by * term).astype(BF16)

    def rx_wait(slot, j):
        remote(
            full_ref.at[j], rx_ref.at[slot, j], out_s.at[0, j], in_r.at[slot, j], dev(cx)
        ).wait_recv()

    def tx_copy(j, chip):
        return remote(tx_ref.at[j], rx_ref.at[0, j], out_s.at[1, j], in_r.at[0, j], dev(chip))

    def relay_copy(j):
        return remote(
            rx_ref.at[0, j], rx_ref.at[0, j], out_s.at[2, j], in_r.at[0, j], dev(cx)
        )

    def back_copy(j):
        return remote(back_ref.at[j], other_ref.at[j], back_s.at[j], back_r.at[j], other)

    def combine(s):
        j = order(s)
        by = fades(j)
        d0, keep = by[0:1], by[2:3]

        @pl.when(c > 0)
        def _():
            rx_wait(0, j)

        @pl.when((c == 3) & (j < near))
        def _():
            relay_copy(j).start()
            rx_wait(1, j)
            enter_ref[...] = keep * rx_ref[0, j].astype(F32) + rx_ref[1, j].astype(F32)

        @pl.when(((c == 1) & (j < near)) | ((c == 2) & (j >= near)))
        def _():
            tx_ref[j] = (keep * rx_ref[0, j].astype(F32) + full_ref[j].astype(F32)).astype(BF16)
            tx_copy(j, 3).start()

        @pl.when((c == 0) & (j >= near))
        def _():
            rx_wait(1, j)
            tx_ref[j] = (keep * full_ref[j].astype(F32) + rx_ref[1, j].astype(F32)).astype(BF16)
            tx_copy(j, 2).start()

        @pl.when(c == 0)
        def _():
            enter_ref[...] = jnp.zeros(enter_ref.shape, F32)

        @pl.when((c == 1) | (c == 2) | ((c == 3) & (j >= near)))
        def _():
            enter_ref[...] = rx_ref[0, j].astype(F32)

        enter = enter_ref[...]
        first = jnp.where(i == 0, mine_ref[j].astype(F32), sib_ref[j].astype(F32))
        middle = d0 * enter + first
        back_ref[j] = jnp.where(i == 0, middle, enter).astype(BF16)
        back_copy(j).start()
        prior(i * half + j * size, jnp.where(i == 0, enter, middle).astype(BF16))

    def returned(s):
        j = order(s)
        back_copy(j).wait_recv()
        prior((1 - i) * half + j * size, other_ref[j])

    def slot(s, _):
        combine(s)

        @pl.when(s > 0)
        def _():
            returned(s - 1)

        return 0

    streams, together = 2, 2
    steps = q_heads // (streams * together)

    def part(h, _):
        for chip in range(n // 2):

            @pl.when(c == chip)
            def _():
                attend_visible(
                    h, streams, together, chip, q_ref, allc_ref, alln_ref, bias_ref, att_ref
                )

        return slot(h, 0)

    lax.fori_loop(0, steps, part, 0)
    lax.fori_loop(steps, chunks, slot, 0)
    returned(chunks - 1)

    def drain(j, _):
        back_copy(j).wait_send()
        sib_copy(j).wait_send()

        @pl.when(full_sent(j))
        def _():
            full_copy(j).wait_send()

        @pl.when(((c == 1) & (j < near)) | ((c == 2) & (j >= near)))
        def _():
            tx_copy(j, 3).wait_send()

        @pl.when((c == 0) & (j >= near))
        def _():
            tx_copy(j, 2).wait_send()

        @pl.when((c == 3) & (j < near))
        def _():
            relay_copy(j).wait_send()

        return 0

    lax.fori_loop(0, chunks, drain, 0)
    for d in range(1, n):
        meta_copy(d).wait_send()
    for way in (1, 2, 0):
        own_copy(0, way).wait_send()
    own_copy(1, 0).wait_send()

    @pl.when(cx > c)
    def _():
        own_copy(1, 1).wait_send()

    @pl.when(cy > c)
    def _():
        own_copy(1, 2).wait_send()

    @pl.when(c >= 1)
    def _():
        pass_copy(0, 0, cx, cy).wait_send()

    @pl.when(c == 3)
    def _():
        pass_copy(0, 1, cy, cx).wait_send()
        pass_copy(1, 1, cy, cx).wait_send()

    @pl.when(c == 1)
    def _():
        pass_copy(1, 0, cx, cy).wait_send()

    for chip_ in (cx, cy, cd):
        forward(0, chip_).wait_send()

        @pl.when(chip_ < c)
        def _():
            forward(1, chip_).wait_send()


def codes_kernel(mag_ref, nk_ref, code_ref, scale_ref):
    scale = (mag_ref[...] + 1e-6) / 127.0
    scale_ref[...] = scale
    code_ref[...] = (nk_ref[...].astype(F32) / scale).astype(BF16)


def fused_body(
    ssm_input,
    state_in,
    state_out,
    step_size,
    decay_rate,
    forget,
    skip_gain,
    queries,
    new_keys,
    new_values,
    cache_keys,
    cache_values,
    cache_key_scale,
    cache_value_scale,
):
    n = 8
    tokens, width = ssm_input.shape
    heads = step_size.shape[1]
    rows = cache_keys.shape[0]
    channels = new_keys.shape[1]
    q_width = queries.shape[1]
    kv_here = max(1, q_width // ATT_DIM // (ATT_HEADS // KV_HEADS))
    kvw = kv_here * ATT_DIM
    groups_here = heads // min(SSM_HEADS // GROUPS, heads)
    half = width // 2
    size = min(256, half)
    chunks = half // size
    _, fac = factor_rows(tokens)
    shape = jax.ShapeDtypeStruct
    dma = pltpu.SemaphoreType.DMA
    any_ = pl.BlockSpec(memory_space=pl.ANY)
    piece = pltpu.VMEM((chunks, STATE, size), BF16)
    y, attended, mag = pl.pallas_call(
        functools.partial(fused_kernel, chunks),
        out_shape=(
            shape((tokens, width), BF16),
            shape((tokens, q_width), BF16),
            shape((1, channels), F32),
        ),
        in_specs=[any_] * 3 + [VMEM] * 4 + [any_] * 5 + [VMEM] * 2,
        out_specs=(VMEM,) * 3,
        scratch_shapes=[
            pltpu.VMEM((tokens, width), BF16),
            pltpu.VMEM((tokens, groups_here * STATE), BF16),
            pltpu.VMEM((tokens, groups_here * STATE), BF16),
            pltpu.VMEM((tokens, q_width), BF16),
            pltpu.VMEM((tokens, channels), BF16),
            pltpu.VMEM((tokens, kvw), BF16),
            pltpu.VMEM((rows, kvw), BF16),
            pltpu.VMEM((rows, kvw), BF16),
            pltpu.VMEM((rows, 2 * kvw), BF16),
            pltpu.VMEM((tokens, 2 * kvw), BF16),
            pltpu.VMEM((n, rows, 2 * kvw), BF16),
            pltpu.VMEM((n, tokens, 2 * kvw), BF16),
            pltpu.VMEM((tokens, 2 * tokens), F32),
            pltpu.VMEM((1, channels + 128), F32),
            pltpu.VMEM((n, 1, channels + 128), F32),
            pltpu.VMEM((fac, 2 * heads), BF16),
            pltpu.VMEM((16, 2 * heads), BF16),
            pltpu.VMEM((tokens, width), BF16),
            pltpu.VMEM((groups_here, tokens, tokens), BF16),
            pltpu.VMEM((groups_here, STATE, tokens), BF16),
            piece,
            piece,
            piece,
            piece,
            piece,
            pltpu.VMEM((2, chunks, STATE, size), BF16),
            pltpu.VMEM((STATE, size), F32),
            piece,
            piece,
            dma((8,)),
            dma((n,)),
            dma((n,)),
            dma((2, 3)),
            dma((2, n)),
            dma((2, 4)),
            dma((2, 2)),
            dma((chunks,)),
            dma((chunks,)),
            dma((3, chunks)),
            dma((2, chunks)),
            dma((chunks,)),
            dma((chunks,)),
        ],
        compiler_params=pltpu.CompilerParams(
            collective_id=0, has_side_effects=True, vmem_limit_bytes=60 * 1024 * 1024
        ),
        name="fused",
    )(
        ssm_input,
        state_in,
        state_out,
        step_size.T,
        decay_rate.reshape(1, heads),
        forget.reshape(1, tokens),
        skip_gain.reshape(1, heads),
        queries,
        new_keys,
        new_values,
        cache_keys,
        cache_values,
        cache_key_scale.reshape(1, channels),
        cache_value_scale.reshape(1, channels),
    )
    codes, scale = pl.pallas_call(
        codes_kernel,
        out_shape=(shape((tokens, channels), BF16), shape((1, channels), F32)),
        in_specs=[VMEM] * 2,
        out_specs=(VMEM,) * 2,
        name="codes",
    )(mag, new_keys)
    return (y, attended, codes, scale.reshape(channels))


def fits_fused(mesh):
    heads = SSM_HEADS // mesh.shape["head"]
    return mesh.shape["seq"] == 8 and heads == 64


def solution(mesh):
    in_specs = (
        P("seq", "head"),
        P("seq", None),
        P("seq", None),
        P("seq", "head"),
        P("head"),
        P("seq"),
        P("head"),
        P("seq", "head"),
        P("seq", None),
        P("seq", None),
        P("seq", None),
        P("seq", None),
        P(),
        P(),
    )
    out_specs = (P("seq", "head"), P("seq", "head"), P("seq", None), P())
    general = functools.partial(body, mesh.shape["seq"])
    return jax.shard_map(
        fused_body if fits_fused(mesh) else general,
        mesh=mesh,
        in_specs=in_specs,
        out_specs=out_specs,
        check_vma=False,
    )
```

```python
import functools
import jax
import jax.numpy as jnp
from jax import lax
from jax.experimental import pallas as pl
from jax.experimental.pallas import tpu as pltpu
from jax.sharding import PartitionSpec as P

SSM_HEADS = 256
HEAD_DIM = 64
STATE = 256
GROUPS = 8
ATT_HEADS = 64
KV_HEADS = 8
ATT_DIM = 128

NEG = -1e30
LOG2E = 1.4426950408889634
HIGHEST = lax.Precision.HIGHEST
MESH = pl.DeviceIdType.MESH
VMEM = pl.BlockSpec(memory_space=pltpu.VMEM)
F32 = jnp.float32
BF16 = jnp.bfloat16


def iota(shape, axis):
    return lax.broadcasted_iota(jnp.int32, shape, axis)


def lanes(start, size):
    return pl.ds(pl.multiple_of(start, 128), size)


def local_kernel(
    x_ref,
    sin_ref,
    sout_ref,
    step_ref,
    decay_ref,
    forget_ref,
    skip_ref,
    nk_ref,
    nv_ref,
    ck_ref,
    cv_ref,
    cks_ref,
    cvs_ref,
    state_ref,
    run_ref,
    fade_ref,
    at_ref,
    gram_ref,
    meta_ref,
    kvc_ref,
    kvn_ref,
):
    tokens, width = x_ref.shape
    heads = step_ref.shape[0]
    per_group = min(SSM_HEADS // GROUPS, heads)
    groups_here = heads // per_group
    z = lax.axis_index("head")
    group0 = z * heads // (SSM_HEADS // GROUPS)
    kvw = kvc_ref.shape[1] // 2
    q_heads = heads * ATT_HEADS // SSM_HEADS
    first = z * q_heads // (ATT_HEADS // KV_HEADS)
    cols = lanes(first * ATT_DIM, kvw)
    kvc_ref[:, :kvw] = (ck_ref[:, cols].astype(F32) * cks_ref[:, cols]).astype(BF16)
    kvc_ref[:, kvw:] = (cv_ref[:, cols].astype(F32) * cvs_ref[:, cols]).astype(BF16)
    kvn_ref[:, :kvw] = nk_ref[:, cols]
    kvn_ref[:, kvw:] = nv_ref[:, cols]
    meta_ref[:, width:] = jnp.max(jnp.abs(nk_ref[...].astype(F32)), axis=0, keepdims=True)

    row, col = iota((tokens, tokens), 0), iota((tokens, tokens), 1)
    lower = jnp.where(col <= row, 1.0, 0.0)
    eye = jnp.where(col == row, 1.0, 0.0)
    step = step_ref[...].T
    forgotten = jnp.sum(lower * forget_ref[...], axis=1, keepdims=True)
    decayed = jnp.dot(
        lower, decay_ref[...] * step, precision=HIGHEST, preferred_element_type=F32
    )
    running = -(decayed + forgotten) * LOG2E
    start = running - jnp.log2(step)
    at_ref[...] = start.T
    rest = jnp.concatenate(
        [running, jnp.broadcast_to(skip_ref[...], (16, heads))], axis=0
    )
    for third in range(3):
        piece = rest.astype(BF16)
        run_ref[:, third * heads : (third + 1) * heads] = piece
        rest = rest - piece.astype(F32)
    fade_ref[...] = jnp.exp2(running).astype(BF16)
    tail = jnp.exp2(running[tokens - 1 : tokens] - start).astype(BF16)
    last = running[tokens - 8 : tokens]
    block = min(512, width)
    for g in range(groups_here):
        gcols = lanes((group0 + g) * STATE, STATE)
        maps_in = sin_ref[:, gcols]
        gram_ref[g] = lax.dot_general(
            sout_ref[:, gcols], maps_in, (((1,), (1,)), ((), ())), preferred_element_type=F32
        )
        turned = lax.dot_general(
            maps_in,
            eye.astype(BF16),
            (((0,), (0,)), ((), ())),
            preferred_element_type=F32,
        ).astype(BF16)
        for b in range(per_group * HEAD_DIM // block):
            begin = g * per_group * HEAD_DIM + b * block
            here = pl.ds(begin, block)
            pick = choose(heads, begin, block)
            meta_ref[:, here] = jnp.dot(
                last, pick, precision=HIGHEST, preferred_element_type=F32
            )[7:8]
            scale = jnp.dot(tail, pick.astype(BF16), preferred_element_type=F32)
            scaled = (x_ref[:, here].astype(F32) * scale).astype(BF16)
            state_ref[:, here] = jnp.dot(
                turned, scaled, preferred_element_type=F32
            ).astype(BF16)


def choose(heads, begin, size):
    lane = begin + iota((heads, size), 1)
    return (iota((heads, size), 0) == lane // HEAD_DIM).astype(F32)


def within_pair(p, x_ref, run_ref, at_ref, gram_ref, part_ref):
    tokens = x_ref.shape[0]
    heads = run_ref.shape[1] // 3
    per_group = min(SSM_HEADS // GROUPS, heads)
    here = lanes(p * 128, 128)
    pick = choose(heads, p * 128, 128).astype(BF16)
    both = jnp.dot(
        run_ref[...], jnp.concatenate([pick] * 3, axis=0), preferred_element_type=F32
    )
    run, skip = both[:tokens], both[tokens : tokens + 1]
    x = x_ref[:, here]
    gram = gram_ref[(2 * p) // per_group]
    causal = iota((tokens, tokens), 1) <= iota((tokens, tokens), 0)

    def one(k):
        spread = run[:, k * HEAD_DIM : k * HEAD_DIM + 1] - at_ref[pl.ds(2 * p + k, 1), :]
        return (jnp.exp2(jnp.where(causal, spread, NEG)) * gram).astype(BF16)

    pair = jnp.dot(
        jnp.concatenate([one(0), one(1)], axis=0), x, preferred_element_type=F32
    )
    y = jnp.where(iota((tokens, 128), 1) < HEAD_DIM, pair[:tokens], pair[tokens:])
    part_ref[:, here] = (y + skip * x.astype(F32)).astype(BF16)


def attend(h, q_ref, allc_ref, alln_ref, bias_ref, vc_ref, vn_ref, att_ref):
    q_heads = q_ref.shape[1] // ATT_DIM
    kv_here = vc_ref.shape[0]
    share = q_heads // kv_here
    together = 2 if share % 2 == 0 else 1
    tokens = q_ref.shape[0]
    k = (h * together) // share
    factor = ATT_DIM**-0.5 * LOG2E
    nt = (((1,), (1,)), ((), ()))
    own = [lanes((h * together + e) * ATT_DIM, ATT_DIM) for e in range(together)]
    q = jnp.concatenate([q_ref[:, o] for o in own], axis=0)
    at = lanes(k * ATT_DIM, ATT_DIM)
    keys_c = allc_ref[:, :, at].reshape(-1, ATT_DIM)
    keys_n = alln_ref[:, :, at].reshape(-1, ATT_DIM)
    old = lax.dot_general(q, keys_c, nt, preferred_element_type=F32)
    new = lax.dot_general(q, keys_n, nt, preferred_element_type=F32)
    bias = bias_ref[...]
    new = (new.reshape(together, tokens, -1) + bias[None]).reshape(together * tokens, -1)
    peak = jnp.maximum(
        jnp.max(old, axis=1, keepdims=True), jnp.max(new, axis=1, keepdims=True)
    )
    old = jnp.exp2((old - peak) * factor).astype(BF16)
    new = jnp.exp2((new - peak) * factor).astype(BF16)
    both = jnp.dot(old, vc_ref[k], preferred_element_type=F32) + jnp.dot(
        new, vn_ref[k], preferred_element_type=F32
    )
    result = (both[:, :ATT_DIM] / both[:, ATT_DIM:]).astype(BF16)
    for e in range(together):
        att_ref[:, own[e]] = result[e * tokens : (e + 1) * tokens]


def comm_kernel(
    n,
    chunks,
    state_ref,
    kvc_ref,
    kvn_ref,
    meta_ref,
    x_ref,
    run_ref,
    at_ref,
    gram_ref,
    q_ref,
    out_ref,
    allm_ref,
    part_ref,
    att_ref,
    allc_ref,
    alln_ref,
    vc_ref,
    vn_ref,
    bias_ref,
    sib_ref,
    own_ref,
    incl_ref,
    recv_ref,
    back_ref,
    meta_s,
    meta_r,
    kv_s,
    kv_r,
    kv_f,
    sib_s,
    sib_r,
    pre_s,
    pre_r,
    rel_s,
    back_s,
    back_r,
):
    n2 = n // 2
    levels = n2.bit_length() - 1
    me = lax.axis_index("seq")
    i, c = me % 2, me // 2
    other = me + 1 - 2 * i
    width = state_ref.shape[1]
    half = width // 2
    size = half // chunks

    barrier = pltpu.get_barrier_semaphore()
    for d in range(1, n):
        pl.semaphore_signal(
            barrier, inc=1, device_id={"seq": (me + d) % n}, device_id_type=MESH
        )
    pl.semaphore_wait(barrier, n - 1)

    def remote(src, dst, ssem, rsem, to):
        return pltpu.make_async_remote_copy(
            src_ref=src,
            dst_ref=dst,
            send_sem=ssem,
            recv_sem=rsem,
            device_id={"seq": to},
            device_id_type=MESH,
        )

    def sib_copy(j):
        return remote(
            state_ref.at[:, lanes((1 - i) * half + j * size, size)],
            sib_ref.at[j],
            sib_s.at[j],
            sib_r.at[j],
            other,
        )

    for j in range(chunks):
        sib_copy(j).start()
    for d in range(1, n):
        remote(
            meta_ref, allm_ref.at[me], meta_s.at[d], meta_r.at[me], (me + d) % n
        ).start()

    def cache_copy(d, to):
        return remote(kvc_ref, allc_ref.at[me], kv_s.at[0, d], kv_r.at[0, me], to)

    def new_copy(d, to):
        return remote(kvn_ref, alln_ref.at[me], kv_s.at[1, d], kv_r.at[1, me], to)

    cache_copy(0, other).start()
    new_copy(0, other).start()
    for d in range(1, n2):
        to = ((c + d) % n2) * 2 + i
        cache_copy(d, to).start()

        @pl.when(c + d < n2)
        def _():
            new_copy(d, to).start()

    allm_ref[me] = meta_ref[...]
    allc_ref[me] = kvc_ref[...]
    alln_ref[me] = kvn_ref[...]
    for d in range(1, n2):
        later = c + d

        @pl.when(later < n2)
        def _():
            for k in range(2):
                alln_ref[later * 2 + k] = jnp.zeros(kvn_ref.shape, BF16)

    for d in range(1, n):
        r = (me + d) % n
        remote(meta_ref, allm_ref.at[r], meta_s.at[d], meta_r.at[r], r).wait_recv()

    def sends(l):
        return c % (2 ** (l + 1)) == 2**l - 1

    def targets(l):
        return [0] if l == 0 else list(range(1, 2**l, 2))

    def pre_copy(l, j, r):
        return remote(
            incl_ref.at[l, j],
            recv_ref.at[l, j],
            pre_s.at[l, j, r],
            pre_r.at[l, j],
            ((c + 1 + r) % n2) * 2 + i,
        )

    def relay_copy(l, j):
        return remote(
            recv_ref.at[l, j],
            recv_ref.at[l, j],
            rel_s.at[l, j],
            pre_r.at[l, j],
            ((c + n2 - 1) % n2) * 2 + i,
        )

    def logs(r, j):
        return allm_ref[r, :, lanes(i * half + j * size, size)]

    def gather_first(j, _):
        sib_copy(j).wait_recv()
        mine = state_ref[:, lanes(i * half + j * size, size)].astype(F32)
        theirs = sib_ref[j].astype(F32)
        d1 = jnp.exp2(logs(2 * c + 1, j))
        total = jnp.where(i == 0, d1 * mine + theirs, d1 * theirs + mine)
        incl_ref[0, j] = total.astype(BF16)
        own_ref[j] = jnp.zeros(own_ref.shape[1:], F32)

        @pl.when(sends(0))
        def _():
            pre_copy(0, j, 0).start()

        return 0

    lax.fori_loop(0, chunks, gather_first, 0)
    fresh = bias_ref.shape[1]
    tokens = x_ref.shape[0]
    seen = iota((tokens, fresh), 1) <= me * tokens + iota((tokens, fresh), 0)
    bias_ref[...] = jnp.where(seen, 0.0, NEG)
    pairs = width // 128
    early = n2
    ahead = pairs * 3 // 4

    def pair(p, _):
        within_pair(p, x_ref, run_ref, at_ref, gram_ref, part_ref)
        return 0


    def forward(kind, d):
        src = allc_ref if kind == 0 else alln_ref
        slot = ((c + d) % n2) * 2 + i
        return remote(
            src.at[slot], src.at[slot], kv_f.at[kind, d], kv_r.at[kind, slot], other
        )

    def combine(j, _):
        for l in range(levels):

            @pl.when(c % (2 ** (l + 1)) >= 2**l)
            def _():
                pre_copy(l, j, 0).wait_recv()
                if l >= 1:

                    @pl.when(c % 2 == 1)
                    def _():
                        relay_copy(l, j).start()

                base = c - c % (2**l)
                logsum = jnp.zeros((1, size), F32)
                for back in range(1, 2**l):
                    at = (c + n2 - back) % n2
                    both = logs(2 * at, j) + logs(2 * at + 1, j)
                    logsum += jnp.where(c - back >= base, both, 0.0)
                own_ref[j] = jnp.exp2(logsum) * recv_ref[l, j].astype(F32) + own_ref[j]

            if l + 1 < levels:

                @pl.when(sends(l + 1))
                def _():
                    keep = jnp.exp2(logs(2 * c, j) + logs(2 * c + 1, j))
                    incl_ref[l + 1, j] = (
                        keep * own_ref[j] + incl_ref[0, j].astype(F32)
                    ).astype(BF16)
                    for r in targets(l + 1):
                        pre_copy(l + 1, j, r).start()

        enter = own_ref[j]
        mine = state_ref[:, lanes(i * half + j * size, size)].astype(F32)
        first = jnp.where(i == 0, mine, sib_ref[j].astype(F32))
        middle = jnp.exp2(logs(2 * c, j)) * enter + first
        out_ref[:, lanes(i * half + j * size, size)] = jnp.where(
            i == 0, enter, middle
        ).astype(BF16)
        back_ref[j] = jnp.where(i == 0, middle, enter).astype(BF16)
        back_copy(j, i).start()
        return 0

    def remote_slot(kind, d):
        src = allc_ref if kind == 0 else alln_ref
        mine = kvc_ref if kind == 0 else kvn_ref
        slot = ((c + d) % n2) * 2 + i
        return remote(mine, src.at[slot], kv_s.at[kind, d], kv_r.at[kind, slot], slot)

    def back_copy(j, who):
        return remote(
            back_ref.at[j],
            out_ref.at[:, lanes(who * half + j * size, size)],
            back_s.at[j],
            back_r.at[j],
            other,
        )

    def first_part(j, _):
        lax.fori_loop(j * ahead // early, (j + 1) * ahead // early, pair, 0)
        for d in range(1, n2):

            @pl.when(j == d)
            def _():
                remote_slot(0, d).wait_recv()
                forward(0, d).start()

                @pl.when((c + d) % n2 < c)
                def _():
                    remote_slot(1, d).wait_recv()
                    forward(1, d).start()

        return 0

    lax.fori_loop(0, early, first_part, 0)

    def other_slot(kind, d):
        src = allc_ref if kind == 0 else alln_ref
        mine = kvc_ref if kind == 0 else kvn_ref
        slot = ((c + d) % n2) * 2 + (1 - i)
        return remote(mine, src.at[slot], kv_f.at[kind, d], kv_r.at[kind, slot], other)

    for d in range(n2):
        other_slot(0, d).wait_recv()
    other_slot(1, 0).wait_recv()
    for d in range(1, n2):

        @pl.when((c + d) % n2 < c)
        def _():
            other_slot(1, d).wait_recv()

    kv_here = vc_ref.shape[0]
    for k in range(kv_here):
        at = (kv_here + k) * ATT_DIM
        for all_ref, ext_ref in ((allc_ref, vc_ref), (alln_ref, vn_ref)):
            ext_ref[k, :, :ATT_DIM] = all_ref[:, :, at : at + ATT_DIM].reshape(-1, ATT_DIM)
            ext_ref[k, :, ATT_DIM:] = jnp.ones((ext_ref.shape[1], ATT_DIM), BF16)

    q_heads = q_ref.shape[1] // ATT_DIM
    steps = q_heads // 2 if (q_heads // kv_here) % 2 == 0 else q_heads

    def head(h, _):
        attend(h, q_ref, allc_ref, alln_ref, bias_ref, vc_ref, vn_ref, att_ref)
        return 0

    def second_part(j, _):
        rest = pairs - ahead
        lax.fori_loop(
            ahead + j * rest // chunks, ahead + (j + 1) * rest // chunks, pair, 0
        )
        lax.fori_loop(j * steps // chunks, (j + 1) * steps // chunks, head, 0)
        combine(j, 0)
        return 0

    lax.fori_loop(0, chunks, second_part, 0)

    def drain(j, _):
        back_copy(j, 1 - i).wait_recv()
        back_copy(j, i).wait_send()
        sib_copy(j).wait_send()
        for l in range(levels):

            @pl.when(sends(l))
            def _():
                for r in targets(l):
                    pre_copy(l, j, r).wait_send()

            if l >= 1:

                @pl.when((c % (2 ** (l + 1)) >= 2**l) & (c % 2 == 1))
                def _():
                    relay_copy(l, j).wait_send()

        return 0

    lax.fori_loop(0, chunks, drain, 0)
    for d in range(1, n):
        remote(
            meta_ref, allm_ref.at[me], meta_s.at[d], meta_r.at[me], (me + d) % n
        ).wait_send()
    cache_copy(0, other).wait_send()
    new_copy(0, other).wait_send()
    for d in range(1, n2):
        to = ((c + d) % n2) * 2 + i
        cache_copy(d, to).wait_send()
        forward(0, d).wait_send()

        @pl.when(c + d < n2)
        def _():
            new_copy(d, to).wait_send()

        @pl.when((c + d) % n2 < c)
        def _():
            forward(1, d).wait_send()


def final_kernel(
    part_ref,
    fade_ref,
    sout_ref,
    state_ref,
    meta_ref,
    nk_ref,
    y_ref,
    code_ref,
    scale_ref,
):
    tokens, width = part_ref.shape
    heads = fade_ref.shape[1]
    per_group = min(SSM_HEADS // GROUPS, heads)
    z = lax.axis_index("head")
    group0 = z * heads // (SSM_HEADS // GROUPS)
    block = min(512, width)

    magnitude = jnp.max(meta_ref[:, 0, width:], axis=0, keepdims=True)
    scale = (magnitude + 1e-6) / 127.0
    scale_ref[...] = scale
    code_ref[...] = (nk_ref[...].astype(F32) / scale).astype(BF16)
    fade = fade_ref[...]
    for b in range(width // block):
        here = pl.ds(b * block, block)
        g = group0 + (b * block) // (per_group * HEAD_DIM)
        prior = jnp.dot(
            sout_ref[:, lanes(g * STATE, STATE)], state_ref[:, here], preferred_element_type=F32
        )
        pick = choose(heads, b * block, block).astype(BF16)
        spread = jnp.dot(fade, pick, preferred_element_type=F32)
        y_ref[:, here] = (part_ref[:, here].astype(F32) + spread * prior).astype(BF16)


def body(
    n,
    ssm_input,
    state_in,
    state_out,
    step_size,
    decay_rate,
    forget,
    skip_gain,
    queries,
    new_keys,
    new_values,
    cache_keys,
    cache_values,
    cache_key_scale,
    cache_value_scale,
):
    tokens, width = ssm_input.shape
    heads = step_size.shape[1]
    rows = cache_keys.shape[0]
    channels = new_keys.shape[1]
    q_heads = queries.shape[1] // ATT_DIM
    kv_here = max(1, q_heads // (ATT_HEADS // KV_HEADS))
    kvw = kv_here * ATT_DIM
    per_group = min(SSM_HEADS // GROUPS, heads)
    groups_here = heads // per_group
    limit = pltpu.CompilerParams(vmem_limit_bytes=60 * 1024 * 1024)
    shape = jax.ShapeDtypeStruct
    state, run, fade, at, gram, meta, kvc, kvn = pl.pallas_call(
        local_kernel,
        out_shape=(
            shape((STATE, width), BF16),
            shape((tokens + 16, 3 * heads), BF16),
            shape((tokens, heads), BF16),
            shape((heads, tokens), F32),
            shape((groups_here, tokens, tokens), F32),
            shape((1, width + channels), F32),
            shape((rows, 2 * kvw), BF16),
            shape((tokens, 2 * kvw), BF16),
        ),
        in_specs=[VMEM] * 13,
        out_specs=(VMEM,) * 8,
        compiler_params=limit,
        name="local",
    )(
        ssm_input,
        state_in,
        state_out,
        step_size.T,
        decay_rate.reshape(1, heads),
        forget.reshape(1, tokens),
        skip_gain.reshape(1, heads),
        new_keys,
        new_values,
        cache_keys,
        cache_values,
        cache_key_scale.reshape(1, channels),
        cache_value_scale.reshape(1, channels),
    )
    half = width // 2
    size = min(256, half)
    chunks = half // size
    n2 = n // 2
    levels = n2.bit_length() - 1
    fan = max(1, n2 // 2)
    dma = pltpu.SemaphoreType.DMA
    carried, allm, part, attended = pl.pallas_call(
        functools.partial(comm_kernel, n, chunks),
        out_shape=(
            shape((STATE, width), BF16),
            shape((n, 1, width + channels), F32),
            shape((tokens, width), BF16),
            shape((tokens, queries.shape[1]), BF16),
        ),
        in_specs=[VMEM] * 9,
        out_specs=(VMEM,) * 4,
        scratch_shapes=[
            pltpu.VMEM((n, rows, 2 * kvw), BF16),
            pltpu.VMEM((n, tokens, 2 * kvw), BF16),
            pltpu.VMEM((kv_here, n * rows, 2 * ATT_DIM), BF16),
            pltpu.VMEM((kv_here, n * tokens, 2 * ATT_DIM), BF16),
            pltpu.VMEM((tokens, n * tokens), F32),
            pltpu.VMEM((chunks, STATE, size), BF16),
            pltpu.VMEM((chunks, STATE, size), F32),
            pltpu.VMEM((levels, chunks, STATE, size), BF16),
            pltpu.VMEM((levels, chunks, STATE, size), BF16),
            pltpu.VMEM((chunks, STATE, size), BF16),
            dma((n,)),
            dma((n,)),
            dma((2, n2)),
            dma((2, n)),
            dma((2, n2)),
            dma((chunks,)),
            dma((chunks,)),
            dma((levels, chunks, fan)),
            dma((levels, chunks)),
            dma((levels, chunks)),
            dma((chunks,)),
            dma((chunks,)),
        ],
        compiler_params=pltpu.CompilerParams(
            collective_id=0, has_side_effects=True, vmem_limit_bytes=60 * 1024 * 1024
        ),
        name="exchange",
    )(state, kvc, kvn, meta, ssm_input, run, at, gram, queries)
    y, codes, scale = pl.pallas_call(
        final_kernel,
        out_shape=(
            shape((tokens, width), BF16),
            shape((tokens, channels), BF16),
            shape((1, channels), F32),
        ),
        in_specs=[VMEM] * 6,
        out_specs=(VMEM,) * 3,
        compiler_params=limit,
        name="finish",
    )(part, fade, state_out, carried, allm, new_keys)
    return (y, attended, codes, scale.reshape(channels))

BLOCK = 96


def span_blocks(tokens):
    return max(1, tokens // BLOCK)


def split2(value):
    high = value.astype(BF16)
    low = (value - high.astype(F32)).astype(BF16)
    return jnp.concatenate([high, low], axis=1)


def choose2(heads, begin, size):
    lane = begin + iota((2 * heads, size), 1)
    row = iota((2 * heads, size), 0)
    return (row % heads == lane // HEAD_DIM).astype(BF16)


def factor_rows(tokens):
    nb = span_blocks(tokens)
    size = tokens // nb
    places, at = {}, 0
    for name, rows in (
        [("z", tokens), ("tail", 16)]
        + [(f"z{b}", (b + 1) * size) for b in range(nb - 1)]
        + [("out", tokens), ("skip", 16), ("fade", tokens)]
    ):
        places[name] = (at, at + rows)
        at += rows
    return places, at


def with_ones(v):
    return jnp.concatenate([v, jnp.ones(v.shape, BF16)], axis=1)


def attend_visible(step, streams, together, chip, q_ref, allc_ref, alln_ref, bias_ref, att_ref):
    tokens = q_ref.shape[0]
    kvw = allc_ref.shape[2] // 2
    share = (q_ref.shape[1] // ATT_DIM) // (kvw // ATT_DIM)
    factor = ATT_DIM**-0.5 * LOG2E
    nt = (((1,), (1,)), ((), ()))
    k = (step * streams * together) // share
    at, av = lanes(k * ATT_DIM, ATT_DIM), lanes(kvw + k * ATT_DIM, ATT_DIM)
    seen = 2 * chip + 2

    def rows_of(cols):
        return jnp.concatenate(
            [
                allc_ref[:, :, cols].reshape(-1, ATT_DIM),
                alln_ref[:seen, :, cols].reshape(-1, ATT_DIM),
            ],
            axis=0,
        )

    keys, values = rows_of(at), with_ones(rows_of(av))
    free = keys.shape[0] - 2 * tokens
    own, scores = [], []
    for e in range(streams):
        first = (step * streams + e) * together
        own.append([lanes((first + f) * ATT_DIM, ATT_DIM) for f in range(together)])
        q = jnp.concatenate([q_ref[:, o] for o in own[e]], axis=0)
        scores.append(lax.dot_general(q, keys, nt, preferred_element_type=F32))
    bias = bias_ref[...]
    for e in range(streams):
        near = scores[e][:, free:].reshape(together, tokens, -1) + bias[None]
        s = jnp.concatenate([scores[e][:, :free], near.reshape(together * tokens, -1)], axis=1)
        peak = jnp.max(s, axis=1, keepdims=True)
        p = jnp.exp2((s - peak) * factor).astype(BF16)
        both = jnp.dot(p, values, preferred_element_type=F32)
        result = (both[:, :ATT_DIM] / both[:, ATT_DIM:]).astype(BF16)
        for f, o in enumerate(own[e]):
            att_ref[:, o] = result[f * tokens : (f + 1) * tokens]


def fused_kernel(
    chunks,
    x_hbm,
    sin_hbm,
    sout_hbm,
    step_hbm,
    decay_hbm,
    forget_hbm,
    skip_hbm,
    q_hbm,
    nk_hbm,
    nv_hbm,
    ck_hbm,
    cv_hbm,
    cks_hbm,
    cvs_hbm,
    y_hbm,
    att_hbm,
    mag_hbm,
    y_ref,
    att_ref,
    mag_ref,
    step_ref,
    decay_ref,
    forget_ref,
    skip_ref,
    cks_ref,
    cvs_ref,
    x_ref,
    sin_ref,
    sout_ref,
    q_ref,
    nk_ref,
    nv_ref,
    ck_ref,
    cv_ref,
    kvc_ref,
    kvn_ref,
    allc_ref,
    alln_ref,
    bias_ref,
    meta_ref,
    allm_ref,
    fac_ref,
    fade_ref,
    z_ref,
    gram_ref,
    turned_ref,
    give_ref,
    sib_ref,
    mine_ref,
    full_ref,
    tx_ref,
    rx_ref,
    enter_ref,
    back_ref,
    other_ref,
    load_s,
    store_s,
    meta_s,
    meta_r,
    kv_s,
    kv_r,
    kv_f,
    kv_p,
    sib_s,
    sib_r,
    out_s,
    in_r,
    back_s,
    back_r,
):
    n = 8
    tokens, width = x_ref.shape
    heads = step_ref.shape[0]
    per_group = min(SSM_HEADS // GROUPS, heads)
    groups_here = heads // per_group
    channels = nk_ref.shape[1]
    kvw = kvc_ref.shape[1] // 2
    half = width // 2
    size = half // chunks
    near = chunks // 2
    places, _ = factor_rows(tokens)
    nb = span_blocks(tokens)
    bs = tokens // nb

    me = lax.axis_index("seq")
    z = lax.axis_index("head")
    i, c = me % 2, me // 2
    other = me + 1 - 2 * i
    cx, cy = c + 1 - 2 * (c % 2), (c + 2) % 4
    cd = 3 - c
    group0 = z * heads // (SSM_HEADS // GROUPS)
    q_heads = heads * ATT_HEADS // SSM_HEADS
    first_kv = z * q_heads // (ATT_HEADS // KV_HEADS)
    cols = lanes(first_kv * ATT_DIM, kvw)
    gcols = lanes(group0 * STATE, groups_here * STATE)

    barrier = pltpu.get_barrier_semaphore()
    for d in range(1, n):
        pl.semaphore_signal(
            barrier, inc=1, device_id={"seq": (me + d) % n}, device_id_type=MESH
        )

    moves = dict(
        ck=(ck_hbm.at[:, cols], ck_ref),
        cks=(cks_hbm.at[:, cols], cks_ref),
        cv=(cv_hbm.at[:, cols], cv_ref),
        cvs=(cvs_hbm.at[:, cols], cvs_ref),
        nv=(nv_hbm.at[:, cols], nv_ref),
        nk=(nk_hbm, nk_ref),
        step=(step_hbm, step_ref),
        decay=(decay_hbm, decay_ref),
        forget=(forget_hbm, forget_ref),
        skip=(skip_hbm, skip_ref),
        sin=(sin_hbm.at[:, gcols], sin_ref),
        sout=(sout_hbm.at[:, gcols], sout_ref),
        x=(x_hbm, x_ref),
        q=(q_hbm, q_ref),
    )
    loads = {
        name: pltpu.make_async_copy(src, dst, load_s.at[k])
        for k, (name, (src, dst)) in enumerate(moves.items())
    }
    for copy in loads.values():
        copy.start()

    def ready(*names):
        for name in names:
            loads[name].wait()

    def remote(src, dst, ssem, rsem, to):
        return pltpu.make_async_remote_copy(
            src_ref=src,
            dst_ref=dst,
            send_sem=ssem,
            recv_sem=rsem,
            device_id={"seq": to},
            device_id_type=MESH,
        )

    def dev(chip):
        return chip * 2 + i

    alls = (allc_ref, alln_ref)
    owns = (kvc_ref, kvn_ref)

    def own_copy(kind, way):
        to = (other, dev(cx), dev(cy))[way]
        return remote(
            owns[kind], alls[kind].at[me], kv_s.at[kind, way], kv_r.at[kind, me], to
        )

    def pass_copy(kind, way, chip, to):
        slot = dev(chip)
        return remote(
            alls[kind].at[slot],
            alls[kind].at[slot],
            kv_p.at[kind, way],
            kv_r.at[kind, slot],
            dev(to),
        )

    def forward(kind, chip):
        slot = dev(chip)
        return remote(
            alls[kind].at[slot],
            alls[kind].at[slot],
            kv_f.at[kind, chip],
            kv_r.at[kind, slot],
            other,
        )

    def arrived(kind, slot):
        remote(
            owns[kind], alls[kind].at[slot], kv_s.at[kind, 0], kv_r.at[kind, slot], other
        ).wait_recv()

    ready("ck", "cks", "cv", "cvs")
    kvc_ref[:, :kvw] = (ck_ref[...].astype(F32) * cks_ref[...]).astype(BF16)
    kvc_ref[:, kvw:] = (cv_ref[...].astype(F32) * cvs_ref[...]).astype(BF16)
    pl.semaphore_wait(barrier, n - 1)
    for way in (1, 2, 0):
        own_copy(0, way).start()
    ready("nv", "nk")
    kvn_ref[:, :kvw] = nk_ref[:, cols]
    kvn_ref[:, kvw:] = nv_ref[...]

    @pl.when(cx > c)
    def _():
        own_copy(1, 1).start()

    @pl.when(cy > c)
    def _():
        own_copy(1, 2).start()

    own_copy(1, 0).start()

    row, col = iota((tokens, tokens), 0), iota((tokens, tokens), 1)
    lower = jnp.where(col <= row, 1.0, 0.0)
    eye = jnp.where(col == row, 1.0, 0.0).astype(BF16)
    ready("step", "decay", "forget", "skip")
    step = step_ref[...].T
    forgotten = jnp.sum(lower * forget_ref[...], axis=1, keepdims=True)
    decayed = jnp.dot(
        lower, decay_ref[...] * step, precision=HIGHEST, preferred_element_type=F32
    )
    running = -(decayed + forgotten) * LOG2E
    start = running - jnp.log2(step)
    last = running[tokens - 1 : tokens]
    middles = [running[b * bs + bs // 2 - 1 : b * bs + bs // 2] for b in range(nb)]

    meta_ref[:, :channels] = jnp.max(jnp.abs(nk_ref[...].astype(F32)), axis=0, keepdims=True)
    meta_ref[:, channels:] = jnp.concatenate([last, jnp.zeros((1, 128 - heads), F32)], axis=1)

    def meta_copy(d):
        return remote(
            meta_ref, allm_ref.at[me], meta_s.at[d], meta_r.at[me], (me + d) % n
        )

    def meta_arrived(r):
        remote(meta_ref, allm_ref.at[r], meta_s.at[1], meta_r.at[r], r).wait_recv()

    for d in range(1, n):
        meta_copy(d).start()
    allm_ref[me] = meta_ref[...]

    def put(name, value):
        begin, end = places[name]
        fac_ref[begin:end] = split2(jnp.broadcast_to(value, (end - begin, heads)))

    put("z", jnp.exp2(middles[nb - 1] - start))
    put("tail", jnp.exp2(last - middles[nb - 1]))
    for b in range(nb - 1):
        put(f"z{b}", jnp.exp2(middles[b] - start[: (b + 1) * bs]))
    put(
        "out",
        jnp.concatenate(
            [jnp.exp2(running[b * bs : (b + 1) * bs] - middles[b]) for b in range(nb)], axis=0
        ),
    )
    put("skip", skip_ref[...])
    put("fade", jnp.exp2(running))
    ready("sin", "sout")
    for g in range(groups_here):
        gc = slice(g * STATE, (g + 1) * STATE)
        maps_in = sin_ref[:, gc]
        gram = lax.dot_general(
            sout_ref[:, gc], maps_in, (((1,), (1,)), ((), ())), preferred_element_type=F32
        )
        gram_ref[g] = jnp.where(col <= row, gram, 0.0).astype(BF16)
        turned_ref[g] = lax.dot_general(
            maps_in, eye, (((0,), (0,)), ((), ())), preferred_element_type=F32
        ).astype(BF16)
    ready("x")

    def spread(first, final, begin):
        rows = fac_ref[places[first][0] : places[final][1]]
        return jnp.dot(rows, choose2(heads, begin, size), preferred_element_type=F32)

    def local_state(begin):
        here = lanes(begin, size)
        by = spread("z", "tail", begin)
        scaled = (x_ref[:, here].astype(F32) * by[:tokens]).astype(BF16)
        z_ref[:, here] = scaled
        sums = jnp.dot(
            turned_ref[begin // (per_group * HEAD_DIM)], scaled, preferred_element_type=F32
        )
        return (sums * by[tokens : tokens + 1]).astype(BF16)

    def sib_copy(j):
        return remote(give_ref.at[j], sib_ref.at[j], sib_s.at[j], sib_r.at[j], other)

    shift = (c % 2) * (1 - c // 2) * near

    def give(s, _):
        j = (s + shift) % chunks
        give_ref[j] = local_state((1 - i) * half + j * size)
        sib_copy(j).start()
        return 0

    def pass_cache():
        arrived(0, dev(cx))

        @pl.when(c >= 1)
        def _():
            pass_copy(0, 0, cx, cy).start()

        forward(0, cx).start()
        arrived(0, dev(cy))

        @pl.when(c == 3)
        def _():
            pass_copy(0, 1, cy, cx).start()

        forward(0, cy).start()

    lax.fori_loop(0, chunks, give, 0)
    pass_cache()
    meta_arrived(other)

    def logs_of(r):
        return allm_ref[r, :, channels : channels + heads]

    def set_fades(third):
        logs = jnp.concatenate(
            [logs_of(2 * c), logs_of(2 * c + 1), third, jnp.zeros((13, heads), F32)], axis=0
        )
        fade_ref[...] = split2(jnp.exp2(logs))

    def fades(j):
        return jnp.dot(
            fade_ref[...], choose2(heads, i * half + j * size, size), preferred_element_type=F32
        )

    set_fades(jnp.zeros((1, heads), F32))

    def full_copy(j):
        slot = jnp.where(c == 0, 0, 1)
        return remote(
            full_ref.at[j], rx_ref.at[slot, j], out_s.at[0, j], in_r.at[slot, j], dev(cx)
        )

    def full_sent(j):
        return (c == 0) | ((c == 1) & (j >= near)) | ((c == 2) & (j < near))

    def own(s, _):
        j = (s + shift) % chunks
        mine = local_state(i * half + j * size)
        mine_ref[j] = mine
        sib_copy(j).wait_recv()
        mine, theirs = mine.astype(F32), sib_ref[j].astype(F32)
        d1 = fades(j)[1:2]
        full_ref[j] = jnp.where(i == 0, d1 * mine + theirs, d1 * theirs + mine).astype(BF16)

        @pl.when(full_sent(j))
        def _():
            full_copy(j).start()

        return 0

    lax.fori_loop(0, chunks, own, 0)

    bias_ref[...] = jnp.where(
        iota((tokens, 2 * tokens), 1) <= i * tokens + iota((tokens, 2 * tokens), 0), 0.0, NEG
    )

    def within(s, _):
        begin = s * size
        here = lanes(begin, size)
        by = spread("z0" if nb > 1 else "out", "skip", begin)
        at = 0
        gram = gram_ref[begin // (per_group * HEAD_DIM)]
        x = x_ref[:, here].astype(F32)
        parts = []
        for b in range(nb):
            high = (b + 1) * bs
            if b + 1 < nb:
                scaled = (x[:high] * by[at : at + high]).astype(BF16)
                at += high
            else:
                scaled = z_ref[:, here]
            parts.append(
                jnp.dot(gram[b * bs : high, :high], scaled, preferred_element_type=F32)
            )
        y = by[at : at + tokens] * jnp.concatenate(parts, axis=0)
        y_ref[:, here] = (y + by[at + tokens : at + tokens + 1] * x).astype(BF16)
        return 0

    lax.fori_loop(0, chunks, within, 0)

    @pl.when(cx < c)
    def _():
        arrived(1, dev(cx))

        @pl.when(c == 1)
        def _():
            pass_copy(1, 0, cx, cy).start()

        forward(1, cx).start()

    @pl.when(cy < c)
    def _():
        arrived(1, dev(cy))

        @pl.when(c == 3)
        def _():
            pass_copy(1, 1, cy, cx).start()

        forward(1, cy).start()

    lax.fori_loop(chunks, 2 * chunks, within, 0)
    arrived(0, dev(cd))
    forward(0, cd).start()

    for d in range(1, n):
        r = (me + d) % n

        @pl.when(r != other)
        def _():
            meta_arrived(r)

    chip = jnp.where(c == 0, 1, jnp.where(c == 3, 2, c))
    set_fades(logs_of(2 * chip) + logs_of(2 * chip + 1))
    mag_ref[...] = jnp.max(allm_ref[:, 0, :channels], axis=0, keepdims=True)
    mag_out = pltpu.make_async_copy(mag_ref, mag_hbm, store_s.at[2 * chunks])
    mag_out.start()

    @pl.when(cd < c)
    def _():
        arrived(1, dev(cd))
        forward(1, cd).start()

    allc_ref[me] = kvc_ref[...]
    alln_ref[me] = kvn_ref[...]
    arrived(0, other)
    arrived(1, other)
    for d in range(1, 4):
        there = (c + d) % 4
        arrived(0, there * 2 + 1 - i)

        @pl.when(there < c)
        def _():
            arrived(1, there * 2 + 1 - i)

    ready("q")

    def order(s):
        return (s + (1 - c % 2) * near) % chunks

    def y_out(k):
        here = lanes(k * size, size)
        return pltpu.make_async_copy(y_ref.at[:, here], y_hbm.at[:, here], store_s.at[k])

    def prior(begin, carried):
        here = lanes(begin, size)
        group = begin // (per_group * HEAD_DIM)
        term = jnp.dot(sout_ref[:, lanes(group * STATE, STATE)], carried, preferred_element_type=F32)
        by = spread("fade", "fade", begin)
        y_ref[:, here] = (y_ref[:, here].astype(F32) + by * term).astype(BF16)
        y_out(begin // size).start()

    def rx_wait(slot, j):
        remote(
            full_ref.at[j], rx_ref.at[slot, j], out_s.at[0, j], in_r.at[slot, j], dev(cx)
        ).wait_recv()

    def tx_copy(j, chip):
        return remote(tx_ref.at[j], rx_ref.at[0, j], out_s.at[1, j], in_r.at[0, j], dev(chip))

    def relay_copy(j):
        return remote(
            rx_ref.at[0, j], rx_ref.at[0, j], out_s.at[2, j], in_r.at[0, j], dev(cx)
        )

    def back_copy(j):
        return remote(back_ref.at[j], other_ref.at[j], back_s.at[j], back_r.at[j], other)

    def combine(s):
        j = order(s)
        by = fades(j)
        d0, keep = by[0:1], by[2:3]

        @pl.when(c > 0)
        def _():
            rx_wait(0, j)

        @pl.when((c == 3) & (j < near))
        def _():
            relay_copy(j).start()
            rx_wait(1, j)
            enter_ref[...] = keep * rx_ref[0, j].astype(F32) + rx_ref[1, j].astype(F32)

        @pl.when(((c == 1) & (j < near)) | ((c == 2) & (j >= near)))
        def _():
            tx_ref[j] = (keep * rx_ref[0, j].astype(F32) + full_ref[j].astype(F32)).astype(BF16)
            tx_copy(j, 3).start()

        @pl.when((c == 0) & (j >= near))
        def _():
            rx_wait(1, j)
            tx_ref[j] = (keep * full_ref[j].astype(F32) + rx_ref[1, j].astype(F32)).astype(BF16)
            tx_copy(j, 2).start()

        @pl.when(c == 0)
        def _():
            enter_ref[...] = jnp.zeros(enter_ref.shape, F32)

        @pl.when((c == 1) | (c == 2) | ((c == 3) & (j >= near)))
        def _():
            enter_ref[...] = rx_ref[0, j].astype(F32)

        enter = enter_ref[...]
        first = jnp.where(i == 0, mine_ref[j].astype(F32), sib_ref[j].astype(F32))
        middle = d0 * enter + first
        back_ref[j] = jnp.where(i == 0, middle, enter).astype(BF16)
        back_copy(j).start()
        prior(i * half + j * size, jnp.where(i == 0, enter, middle).astype(BF16))

    def returned(s):
        j = order(s)
        back_copy(j).wait_recv()
        prior((1 - i) * half + j * size, other_ref[j])

    def slot(s, _):
        combine(s)

        @pl.when(s > 0)
        def _():
            returned(s - 1)

        return 0

    streams, together = 2, 2
    steps = q_heads // (streams * together)

    def part(h, _):
        for chip in range(n // 2):

            @pl.when(c == chip)
            def _():
                attend_visible(
                    h, streams, together, chip, q_ref, allc_ref, alln_ref, bias_ref, att_ref
                )

        return slot(h, 0)

    lax.fori_loop(0, steps, part, 0)
    att_out = pltpu.make_async_copy(att_ref, att_hbm, store_s.at[2 * chunks + 1])
    att_out.start()
    lax.fori_loop(steps, chunks, slot, 0)
    returned(chunks - 1)

    def drain(j, _):
        back_copy(j).wait_send()
        sib_copy(j).wait_send()

        @pl.when(full_sent(j))
        def _():
            full_copy(j).wait_send()

        @pl.when(((c == 1) & (j < near)) | ((c == 2) & (j >= near)))
        def _():
            tx_copy(j, 3).wait_send()

        @pl.when((c == 0) & (j >= near))
        def _():
            tx_copy(j, 2).wait_send()

        @pl.when((c == 3) & (j < near))
        def _():
            relay_copy(j).wait_send()

        return 0

    lax.fori_loop(0, chunks, drain, 0)

    def stored(k, _):
        y_out(k).wait()
        return 0

    lax.fori_loop(0, 2 * chunks, stored, 0)
    mag_out.wait()
    att_out.wait()
    for d in range(1, n):
        meta_copy(d).wait_send()
    for way in (1, 2, 0):
        own_copy(0, way).wait_send()
    own_copy(1, 0).wait_send()

    @pl.when(cx > c)
    def _():
        own_copy(1, 1).wait_send()

    @pl.when(cy > c)
    def _():
        own_copy(1, 2).wait_send()

    @pl.when(c >= 1)
    def _():
        pass_copy(0, 0, cx, cy).wait_send()

    @pl.when(c == 3)
    def _():
        pass_copy(0, 1, cy, cx).wait_send()
        pass_copy(1, 1, cy, cx).wait_send()

    @pl.when(c == 1)
    def _():
        pass_copy(1, 0, cx, cy).wait_send()

    for chip_ in (cx, cy, cd):
        forward(0, chip_).wait_send()

        @pl.when(chip_ < c)
        def _():
            forward(1, chip_).wait_send()


def finish_kernel(
    y_hbm, att_hbm, mag_hbm, nk_hbm, yo_hbm, atto_hbm, code_hbm, scale_ref,
    y_ref, att_ref, mag_ref, nk_ref, code_ref, in_s, out_s,
):
    pieces = 4
    wide, slim = y_ref.shape[0] // pieces, att_ref.shape[0] // pieces
    mag_in = pltpu.make_async_copy(mag_hbm, mag_ref, in_s.at[2 * pieces])
    nk_in = pltpu.make_async_copy(nk_hbm, nk_ref, in_s.at[2 * pieces + 1])
    code_out = pltpu.make_async_copy(code_ref, code_hbm, out_s.at[2 * pieces])
    ins, outs = [], []
    for p in range(pieces):
        for k, (src, mid, dst, rows) in enumerate(
            [(y_hbm, y_ref, yo_hbm, wide), (att_hbm, att_ref, atto_hbm, slim)]
        ):
            at = pl.ds(p * rows, rows)
            ins.append(pltpu.make_async_copy(src.at[at], mid.at[at], in_s.at[2 * p + k]))
            outs.append(pltpu.make_async_copy(mid.at[at], dst.at[at], out_s.at[2 * p + k]))
    mag_in.start()
    nk_in.start()
    for copy in ins:
        copy.start()
    mag_in.wait()
    nk_in.wait()
    scale = (mag_ref[...] + 1e-6) / 127.0
    scale_ref[...] = scale
    code_ref[...] = (nk_ref[...].astype(F32) / scale).astype(BF16)
    code_out.start()
    for a, b in zip(ins, outs):
        a.wait()
        b.start()
    code_out.wait()
    for b in outs:
        b.wait()


def fused_body(
    ssm_input,
    state_in,
    state_out,
    step_size,
    decay_rate,
    forget,
    skip_gain,
    queries,
    new_keys,
    new_values,
    cache_keys,
    cache_values,
    cache_key_scale,
    cache_value_scale,
):
    n = 8
    tokens, width = ssm_input.shape
    heads = step_size.shape[1]
    rows = cache_keys.shape[0]
    channels = new_keys.shape[1]
    q_width = queries.shape[1]
    kv_here = max(1, q_width // ATT_DIM // (ATT_HEADS // KV_HEADS))
    kvw = kv_here * ATT_DIM
    groups_here = heads // min(SSM_HEADS // GROUPS, heads)
    half = width // 2
    size = min(256, half)
    chunks = half // size
    _, fac = factor_rows(tokens)
    shape = jax.ShapeDtypeStruct
    dma = pltpu.SemaphoreType.DMA
    any_ = pl.BlockSpec(memory_space=pl.ANY)
    piece = pltpu.VMEM((chunks, STATE, size), BF16)
    y, attended, mag = pl.pallas_call(
        functools.partial(fused_kernel, chunks),
        out_shape=(
            shape((tokens, width), BF16),
            shape((tokens, q_width), BF16),
            shape((1, channels), F32),
        ),
        in_specs=[any_] * 14,
        out_specs=(any_,) * 3,
        scratch_shapes=[
            pltpu.VMEM((tokens, width), BF16),
            pltpu.VMEM((tokens, q_width), BF16),
            pltpu.VMEM((1, channels), F32),
            pltpu.VMEM((heads, tokens), F32),
            pltpu.VMEM((1, heads), F32),
            pltpu.VMEM((1, tokens), F32),
            pltpu.VMEM((1, heads), F32),
            pltpu.VMEM((1, kvw), F32),
            pltpu.VMEM((1, kvw), F32),
            pltpu.VMEM((tokens, width), BF16),
            pltpu.VMEM((tokens, groups_here * STATE), BF16),
            pltpu.VMEM((tokens, groups_here * STATE), BF16),
            pltpu.VMEM((tokens, q_width), BF16),
            pltpu.VMEM((tokens, channels), BF16),
            pltpu.VMEM((tokens, kvw), BF16),
            pltpu.VMEM((rows, kvw), BF16),
            pltpu.VMEM((rows, kvw), BF16),
            pltpu.VMEM((rows, 2 * kvw), BF16),
            pltpu.VMEM((tokens, 2 * kvw), BF16),
            pltpu.VMEM((n, rows, 2 * kvw), BF16),
            pltpu.VMEM((n, tokens, 2 * kvw), BF16),
            pltpu.VMEM((tokens, 2 * tokens), F32),
            pltpu.VMEM((1, channels + 128), F32),
            pltpu.VMEM((n, 1, channels + 128), F32),
            pltpu.VMEM((fac, 2 * heads), BF16),
            pltpu.VMEM((16, 2 * heads), BF16),
            pltpu.VMEM((tokens, width), BF16),
            pltpu.VMEM((groups_here, tokens, tokens), BF16),
            pltpu.VMEM((groups_here, STATE, tokens), BF16),
            piece,
            piece,
            piece,
            piece,
            piece,
            pltpu.VMEM((2, chunks, STATE, size), BF16),
            pltpu.VMEM((STATE, size), F32),
            piece,
            piece,
            dma((14,)),
            dma((2 * chunks + 2,)),
            dma((n,)),
            dma((n,)),
            dma((2, 3)),
            dma((2, n)),
            dma((2, 4)),
            dma((2, 2)),
            dma((chunks,)),
            dma((chunks,)),
            dma((3, chunks)),
            dma((2, chunks)),
            dma((chunks,)),
            dma((chunks,)),
        ],
        compiler_params=pltpu.CompilerParams(
            collective_id=0, has_side_effects=True, vmem_limit_bytes=60 * 1024 * 1024
        ),
        name="fused",
    )(
        ssm_input,
        state_in,
        state_out,
        step_size.T,
        decay_rate.reshape(1, heads),
        forget.reshape(1, tokens),
        skip_gain.reshape(1, heads),
        queries,
        new_keys,
        new_values,
        cache_keys,
        cache_values,
        cache_key_scale.reshape(1, channels),
        cache_value_scale.reshape(1, channels),
    )
    y, attended, codes, scale = pl.pallas_call(
        finish_kernel,
        out_shape=(
            shape((tokens, width), BF16),
            shape((tokens, q_width), BF16),
            shape((tokens, channels), BF16),
            shape((1, channels), F32),
        ),
        in_specs=[any_] * 4,
        out_specs=(any_,) * 3 + (VMEM,),
        scratch_shapes=[
            pltpu.VMEM((tokens, width), BF16),
            pltpu.VMEM((tokens, q_width), BF16),
            pltpu.VMEM((1, channels), F32),
            pltpu.VMEM((tokens, channels), BF16),
            pltpu.VMEM((tokens, channels), BF16),
            dma((10,)),
            dma((9,)),
        ],
        name="finish",
    )(y, attended, mag, new_keys)
    return (y, attended, codes, scale.reshape(channels))


def fits_fused(mesh):
    heads = SSM_HEADS // mesh.shape["head"]
    return mesh.shape["seq"] == 8 and heads == 64


def solution(mesh):
    in_specs = (
        P("seq", "head"),
        P("seq", None),
        P("seq", None),
        P("seq", "head"),
        P("head"),
        P("seq"),
        P("head"),
        P("seq", "head"),
        P("seq", None),
        P("seq", None),
        P("seq", None),
        P("seq", None),
        P(),
        P(),
    )
    out_specs = (P("seq", "head"), P("seq", "head"), P("seq", None), P())
    general = functools.partial(body, mesh.shape["seq"])
    return jax.shard_map(
        fused_body if fits_fused(mesh) else general,
        mesh=mesh,
        in_specs=in_specs,
        out_specs=out_specs,
        check_vma=False,
    )
```

```python
import functools
import jax
import jax.numpy as jnp
from jax import lax
from jax.experimental import pallas as pl
from jax.experimental.pallas import tpu as pltpu
from jax.sharding import PartitionSpec as P

SSM_HEADS = 256
HEAD_DIM = 64
STATE = 256
GROUPS = 8
ATT_HEADS = 64
KV_HEADS = 8
ATT_DIM = 128

NEG = -1e30
LOG2E = 1.4426950408889634
HIGHEST = lax.Precision.HIGHEST
MESH = pl.DeviceIdType.MESH
VMEM = pl.BlockSpec(memory_space=pltpu.VMEM)
F32 = jnp.float32
BF16 = jnp.bfloat16


def iota(shape, axis):
    return lax.broadcasted_iota(jnp.int32, shape, axis)


def lanes(start, size):
    return pl.ds(pl.multiple_of(start, 128), size)


def local_kernel(
    x_ref,
    sin_ref,
    sout_ref,
    step_ref,
    decay_ref,
    forget_ref,
    skip_ref,
    nk_ref,
    nv_ref,
    ck_ref,
    cv_ref,
    cks_ref,
    cvs_ref,
    state_ref,
    run_ref,
    fade_ref,
    at_ref,
    gram_ref,
    meta_ref,
    kvc_ref,
    kvn_ref,
):
    tokens, width = x_ref.shape
    heads = step_ref.shape[0]
    per_group = min(SSM_HEADS // GROUPS, heads)
    groups_here = heads // per_group
    z = lax.axis_index("head")
    group0 = z * heads // (SSM_HEADS // GROUPS)
    kvw = kvc_ref.shape[1] // 2
    q_heads = heads * ATT_HEADS // SSM_HEADS
    first = z * q_heads // (ATT_HEADS // KV_HEADS)
    cols = lanes(first * ATT_DIM, kvw)
    kvc_ref[:, :kvw] = (ck_ref[:, cols].astype(F32) * cks_ref[:, cols]).astype(BF16)
    kvc_ref[:, kvw:] = (cv_ref[:, cols].astype(F32) * cvs_ref[:, cols]).astype(BF16)
    kvn_ref[:, :kvw] = nk_ref[:, cols]
    kvn_ref[:, kvw:] = nv_ref[:, cols]
    meta_ref[:, width:] = jnp.max(jnp.abs(nk_ref[...].astype(F32)), axis=0, keepdims=True)

    row, col = iota((tokens, tokens), 0), iota((tokens, tokens), 1)
    lower = jnp.where(col <= row, 1.0, 0.0)
    eye = jnp.where(col == row, 1.0, 0.0)
    step = step_ref[...].T
    forgotten = jnp.sum(lower * forget_ref[...], axis=1, keepdims=True)
    decayed = jnp.dot(
        lower, decay_ref[...] * step, precision=HIGHEST, preferred_element_type=F32
    )
    running = -(decayed + forgotten) * LOG2E
    start = running - jnp.log2(step)
    at_ref[...] = start.T
    rest = jnp.concatenate(
        [running, jnp.broadcast_to(skip_ref[...], (16, heads))], axis=0
    )
    for third in range(3):
        piece = rest.astype(BF16)
        run_ref[:, third * heads : (third + 1) * heads] = piece
        rest = rest - piece.astype(F32)
    fade_ref[...] = jnp.exp2(running).astype(BF16)
    tail = jnp.exp2(running[tokens - 1 : tokens] - start).astype(BF16)
    last = running[tokens - 8 : tokens]
    block = min(512, width)
    for g in range(groups_here):
        gcols = lanes((group0 + g) * STATE, STATE)
        maps_in = sin_ref[:, gcols]
        gram_ref[g] = lax.dot_general(
            sout_ref[:, gcols], maps_in, (((1,), (1,)), ((), ())), preferred_element_type=F32
        )
        turned = lax.dot_general(
            maps_in,
            eye.astype(BF16),
            (((0,), (0,)), ((), ())),
            preferred_element_type=F32,
        ).astype(BF16)
        for b in range(per_group * HEAD_DIM // block):
            begin = g * per_group * HEAD_DIM + b * block
            here = pl.ds(begin, block)
            pick = choose(heads, begin, block)
            meta_ref[:, here] = jnp.dot(
                last, pick, precision=HIGHEST, preferred_element_type=F32
            )[7:8]
            scale = jnp.dot(tail, pick.astype(BF16), preferred_element_type=F32)
            scaled = (x_ref[:, here].astype(F32) * scale).astype(BF16)
            state_ref[:, here] = jnp.dot(
                turned, scaled, preferred_element_type=F32
            ).astype(BF16)


def choose(heads, begin, size):
    lane = begin + iota((heads, size), 1)
    return (iota((heads, size), 0) == lane // HEAD_DIM).astype(F32)


def within_pair(p, x_ref, run_ref, at_ref, gram_ref, part_ref):
    tokens = x_ref.shape[0]
    heads = run_ref.shape[1] // 3
    per_group = min(SSM_HEADS // GROUPS, heads)
    here = lanes(p * 128, 128)
    pick = choose(heads, p * 128, 128).astype(BF16)
    both = jnp.dot(
        run_ref[...], jnp.concatenate([pick] * 3, axis=0), preferred_element_type=F32
    )
    run, skip = both[:tokens], both[tokens : tokens + 1]
    x = x_ref[:, here]
    gram = gram_ref[(2 * p) // per_group]
    causal = iota((tokens, tokens), 1) <= iota((tokens, tokens), 0)

    def one(k):
        spread = run[:, k * HEAD_DIM : k * HEAD_DIM + 1] - at_ref[pl.ds(2 * p + k, 1), :]
        return (jnp.exp2(jnp.where(causal, spread, NEG)) * gram).astype(BF16)

    pair = jnp.dot(
        jnp.concatenate([one(0), one(1)], axis=0), x, preferred_element_type=F32
    )
    y = jnp.where(iota((tokens, 128), 1) < HEAD_DIM, pair[:tokens], pair[tokens:])
    part_ref[:, here] = (y + skip * x.astype(F32)).astype(BF16)


def attend(h, q_ref, allc_ref, alln_ref, bias_ref, vc_ref, vn_ref, att_ref):
    q_heads = q_ref.shape[1] // ATT_DIM
    kv_here = vc_ref.shape[0]
    share = q_heads // kv_here
    together = 2 if share % 2 == 0 else 1
    tokens = q_ref.shape[0]
    k = (h * together) // share
    factor = ATT_DIM**-0.5 * LOG2E
    nt = (((1,), (1,)), ((), ()))
    own = [lanes((h * together + e) * ATT_DIM, ATT_DIM) for e in range(together)]
    q = jnp.concatenate([q_ref[:, o] for o in own], axis=0)
    at = lanes(k * ATT_DIM, ATT_DIM)
    keys_c = allc_ref[:, :, at].reshape(-1, ATT_DIM)
    keys_n = alln_ref[:, :, at].reshape(-1, ATT_DIM)
    old = lax.dot_general(q, keys_c, nt, preferred_element_type=F32)
    new = lax.dot_general(q, keys_n, nt, preferred_element_type=F32)
    bias = bias_ref[...]
    new = (new.reshape(together, tokens, -1) + bias[None]).reshape(together * tokens, -1)
    peak = jnp.maximum(
        jnp.max(old, axis=1, keepdims=True), jnp.max(new, axis=1, keepdims=True)
    )
    old = jnp.exp2((old - peak) * factor).astype(BF16)
    new = jnp.exp2((new - peak) * factor).astype(BF16)
    both = jnp.dot(old, vc_ref[k], preferred_element_type=F32) + jnp.dot(
        new, vn_ref[k], preferred_element_type=F32
    )
    result = (both[:, :ATT_DIM] / both[:, ATT_DIM:]).astype(BF16)
    for e in range(together):
        att_ref[:, own[e]] = result[e * tokens : (e + 1) * tokens]


def comm_kernel(
    n,
    chunks,
    state_ref,
    kvc_ref,
    kvn_ref,
    meta_ref,
    x_ref,
    run_ref,
    at_ref,
    gram_ref,
    q_ref,
    out_ref,
    allm_ref,
    part_ref,
    att_ref,
    allc_ref,
    alln_ref,
    vc_ref,
    vn_ref,
    bias_ref,
    sib_ref,
    own_ref,
    incl_ref,
    recv_ref,
    back_ref,
    meta_s,
    meta_r,
    kv_s,
    kv_r,
    kv_f,
    sib_s,
    sib_r,
    pre_s,
    pre_r,
    rel_s,
    back_s,
    back_r,
):
    n2 = n // 2
    levels = n2.bit_length() - 1
    me = lax.axis_index("seq")
    i, c = me % 2, me // 2
    other = me + 1 - 2 * i
    width = state_ref.shape[1]
    half = width // 2
    size = half // chunks

    barrier = pltpu.get_barrier_semaphore()
    for d in range(1, n):
        pl.semaphore_signal(
            barrier, inc=1, device_id={"seq": (me + d) % n}, device_id_type=MESH
        )
    pl.semaphore_wait(barrier, n - 1)

    def remote(src, dst, ssem, rsem, to):
        return pltpu.make_async_remote_copy(
            src_ref=src,
            dst_ref=dst,
            send_sem=ssem,
            recv_sem=rsem,
            device_id={"seq": to},
            device_id_type=MESH,
        )

    def sib_copy(j):
        return remote(
            state_ref.at[:, lanes((1 - i) * half + j * size, size)],
            sib_ref.at[j],
            sib_s.at[j],
            sib_r.at[j],
            other,
        )

    for j in range(chunks):
        sib_copy(j).start()
    for d in range(1, n):
        remote(
            meta_ref, allm_ref.at[me], meta_s.at[d], meta_r.at[me], (me + d) % n
        ).start()

    def cache_copy(d, to):
        return remote(kvc_ref, allc_ref.at[me], kv_s.at[0, d], kv_r.at[0, me], to)

    def new_copy(d, to):
        return remote(kvn_ref, alln_ref.at[me], kv_s.at[1, d], kv_r.at[1, me], to)

    cache_copy(0, other).start()
    new_copy(0, other).start()
    for d in range(1, n2):
        to = ((c + d) % n2) * 2 + i
        cache_copy(d, to).start()

        @pl.when(c + d < n2)
        def _():
            new_copy(d, to).start()

    allm_ref[me] = meta_ref[...]
    allc_ref[me] = kvc_ref[...]
    alln_ref[me] = kvn_ref[...]
    for d in range(1, n2):
        later = c + d

        @pl.when(later < n2)
        def _():
            for k in range(2):
                alln_ref[later * 2 + k] = jnp.zeros(kvn_ref.shape, BF16)

    for d in range(1, n):
        r = (me + d) % n
        remote(meta_ref, allm_ref.at[r], meta_s.at[d], meta_r.at[r], r).wait_recv()

    def sends(l):
        return c % (2 ** (l + 1)) == 2**l - 1

    def targets(l):
        return [0] if l == 0 else list(range(1, 2**l, 2))

    def pre_copy(l, j, r):
        return remote(
            incl_ref.at[l, j],
            recv_ref.at[l, j],
            pre_s.at[l, j, r],
            pre_r.at[l, j],
            ((c + 1 + r) % n2) * 2 + i,
        )

    def relay_copy(l, j):
        return remote(
            recv_ref.at[l, j],
            recv_ref.at[l, j],
            rel_s.at[l, j],
            pre_r.at[l, j],
            ((c + n2 - 1) % n2) * 2 + i,
        )

    def logs(r, j):
        return allm_ref[r, :, lanes(i * half + j * size, size)]

    def gather_first(j, _):
        sib_copy(j).wait_recv()
        mine = state_ref[:, lanes(i * half + j * size, size)].astype(F32)
        theirs = sib_ref[j].astype(F32)
        d1 = jnp.exp2(logs(2 * c + 1, j))
        total = jnp.where(i == 0, d1 * mine + theirs, d1 * theirs + mine)
        incl_ref[0, j] = total.astype(BF16)
        own_ref[j] = jnp.zeros(own_ref.shape[1:], F32)

        @pl.when(sends(0))
        def _():
            pre_copy(0, j, 0).start()

        return 0

    lax.fori_loop(0, chunks, gather_first, 0)
    fresh = bias_ref.shape[1]
    tokens = x_ref.shape[0]
    seen = iota((tokens, fresh), 1) <= me * tokens + iota((tokens, fresh), 0)
    bias_ref[...] = jnp.where(seen, 0.0, NEG)
    pairs = width // 128
    early = n2
    ahead = pairs * 3 // 4

    def pair(p, _):
        within_pair(p, x_ref, run_ref, at_ref, gram_ref, part_ref)
        return 0


    def forward(kind, d):
        src = allc_ref if kind == 0 else alln_ref
        slot = ((c + d) % n2) * 2 + i
        return remote(
            src.at[slot], src.at[slot], kv_f.at[kind, d], kv_r.at[kind, slot], other
        )

    def combine(j, _):
        for l in range(levels):

            @pl.when(c % (2 ** (l + 1)) >= 2**l)
            def _():
                pre_copy(l, j, 0).wait_recv()
                if l >= 1:

                    @pl.when(c % 2 == 1)
                    def _():
                        relay_copy(l, j).start()

                base = c - c % (2**l)
                logsum = jnp.zeros((1, size), F32)
                for back in range(1, 2**l):
                    at = (c + n2 - back) % n2
                    both = logs(2 * at, j) + logs(2 * at + 1, j)
                    logsum += jnp.where(c - back >= base, both, 0.0)
                own_ref[j] = jnp.exp2(logsum) * recv_ref[l, j].astype(F32) + own_ref[j]

            if l + 1 < levels:

                @pl.when(sends(l + 1))
                def _():
                    keep = jnp.exp2(logs(2 * c, j) + logs(2 * c + 1, j))
                    incl_ref[l + 1, j] = (
                        keep * own_ref[j] + incl_ref[0, j].astype(F32)
                    ).astype(BF16)
                    for r in targets(l + 1):
                        pre_copy(l + 1, j, r).start()

        enter = own_ref[j]
        mine = state_ref[:, lanes(i * half + j * size, size)].astype(F32)
        first = jnp.where(i == 0, mine, sib_ref[j].astype(F32))
        middle = jnp.exp2(logs(2 * c, j)) * enter + first
        out_ref[:, lanes(i * half + j * size, size)] = jnp.where(
            i == 0, enter, middle
        ).astype(BF16)
        back_ref[j] = jnp.where(i == 0, middle, enter).astype(BF16)
        back_copy(j, i).start()
        return 0

    def remote_slot(kind, d):
        src = allc_ref if kind == 0 else alln_ref
        mine = kvc_ref if kind == 0 else kvn_ref
        slot = ((c + d) % n2) * 2 + i
        return remote(mine, src.at[slot], kv_s.at[kind, d], kv_r.at[kind, slot], slot)

    def back_copy(j, who):
        return remote(
            back_ref.at[j],
            out_ref.at[:, lanes(who * half + j * size, size)],
            back_s.at[j],
            back_r.at[j],
            other,
        )

    def first_part(j, _):
        lax.fori_loop(j * ahead // early, (j + 1) * ahead // early, pair, 0)
        for d in range(1, n2):

            @pl.when(j == d)
            def _():
                remote_slot(0, d).wait_recv()
                forward(0, d).start()

                @pl.when((c + d) % n2 < c)
                def _():
                    remote_slot(1, d).wait_recv()
                    forward(1, d).start()

        return 0

    lax.fori_loop(0, early, first_part, 0)

    def other_slot(kind, d):
        src = allc_ref if kind == 0 else alln_ref
        mine = kvc_ref if kind == 0 else kvn_ref
        slot = ((c + d) % n2) * 2 + (1 - i)
        return remote(mine, src.at[slot], kv_f.at[kind, d], kv_r.at[kind, slot], other)

    for d in range(n2):
        other_slot(0, d).wait_recv()
    other_slot(1, 0).wait_recv()
    for d in range(1, n2):

        @pl.when((c + d) % n2 < c)
        def _():
            other_slot(1, d).wait_recv()

    kv_here = vc_ref.shape[0]
    for k in range(kv_here):
        at = (kv_here + k) * ATT_DIM
        for all_ref, ext_ref in ((allc_ref, vc_ref), (alln_ref, vn_ref)):
            ext_ref[k, :, :ATT_DIM] = all_ref[:, :, at : at + ATT_DIM].reshape(-1, ATT_DIM)
            ext_ref[k, :, ATT_DIM:] = jnp.ones((ext_ref.shape[1], ATT_DIM), BF16)

    q_heads = q_ref.shape[1] // ATT_DIM
    steps = q_heads // 2 if (q_heads // kv_here) % 2 == 0 else q_heads

    def head(h, _):
        attend(h, q_ref, allc_ref, alln_ref, bias_ref, vc_ref, vn_ref, att_ref)
        return 0

    def second_part(j, _):
        rest = pairs - ahead
        lax.fori_loop(
            ahead + j * rest // chunks, ahead + (j + 1) * rest // chunks, pair, 0
        )
        lax.fori_loop(j * steps // chunks, (j + 1) * steps // chunks, head, 0)
        combine(j, 0)
        return 0

    lax.fori_loop(0, chunks, second_part, 0)

    def drain(j, _):
        back_copy(j, 1 - i).wait_recv()
        back_copy(j, i).wait_send()
        sib_copy(j).wait_send()
        for l in range(levels):

            @pl.when(sends(l))
            def _():
                for r in targets(l):
                    pre_copy(l, j, r).wait_send()

            if l >= 1:

                @pl.when((c % (2 ** (l + 1)) >= 2**l) & (c % 2 == 1))
                def _():
                    relay_copy(l, j).wait_send()

        return 0

    lax.fori_loop(0, chunks, drain, 0)
    for d in range(1, n):
        remote(
            meta_ref, allm_ref.at[me], meta_s.at[d], meta_r.at[me], (me + d) % n
        ).wait_send()
    cache_copy(0, other).wait_send()
    new_copy(0, other).wait_send()
    for d in range(1, n2):
        to = ((c + d) % n2) * 2 + i
        cache_copy(d, to).wait_send()
        forward(0, d).wait_send()

        @pl.when(c + d < n2)
        def _():
            new_copy(d, to).wait_send()

        @pl.when((c + d) % n2 < c)
        def _():
            forward(1, d).wait_send()


def final_kernel(
    part_ref,
    fade_ref,
    sout_ref,
    state_ref,
    meta_ref,
    nk_ref,
    y_ref,
    code_ref,
    scale_ref,
):
    tokens, width = part_ref.shape
    heads = fade_ref.shape[1]
    per_group = min(SSM_HEADS // GROUPS, heads)
    z = lax.axis_index("head")
    group0 = z * heads // (SSM_HEADS // GROUPS)
    block = min(512, width)

    magnitude = jnp.max(meta_ref[:, 0, width:], axis=0, keepdims=True)
    scale = (magnitude + 1e-6) / 127.0
    scale_ref[...] = scale
    code_ref[...] = (nk_ref[...].astype(F32) / scale).astype(BF16)
    fade = fade_ref[...]
    for b in range(width // block):
        here = pl.ds(b * block, block)
        g = group0 + (b * block) // (per_group * HEAD_DIM)
        prior = jnp.dot(
            sout_ref[:, lanes(g * STATE, STATE)], state_ref[:, here], preferred_element_type=F32
        )
        pick = choose(heads, b * block, block).astype(BF16)
        spread = jnp.dot(fade, pick, preferred_element_type=F32)
        y_ref[:, here] = (part_ref[:, here].astype(F32) + spread * prior).astype(BF16)


def body(
    n,
    ssm_input,
    state_in,
    state_out,
    step_size,
    decay_rate,
    forget,
    skip_gain,
    queries,
    new_keys,
    new_values,
    cache_keys,
    cache_values,
    cache_key_scale,
    cache_value_scale,
):
    tokens, width = ssm_input.shape
    heads = step_size.shape[1]
    rows = cache_keys.shape[0]
    channels = new_keys.shape[1]
    q_heads = queries.shape[1] // ATT_DIM
    kv_here = max(1, q_heads // (ATT_HEADS // KV_HEADS))
    kvw = kv_here * ATT_DIM
    per_group = min(SSM_HEADS // GROUPS, heads)
    groups_here = heads // per_group
    limit = pltpu.CompilerParams(vmem_limit_bytes=60 * 1024 * 1024)
    shape = jax.ShapeDtypeStruct
    state, run, fade, at, gram, meta, kvc, kvn = pl.pallas_call(
        local_kernel,
        out_shape=(
            shape((STATE, width), BF16),
            shape((tokens + 16, 3 * heads), BF16),
            shape((tokens, heads), BF16),
            shape((heads, tokens), F32),
            shape((groups_here, tokens, tokens), F32),
            shape((1, width + channels), F32),
            shape((rows, 2 * kvw), BF16),
            shape((tokens, 2 * kvw), BF16),
        ),
        in_specs=[VMEM] * 13,
        out_specs=(VMEM,) * 8,
        compiler_params=limit,
        name="local",
    )(
        ssm_input,
        state_in,
        state_out,
        step_size.T,
        decay_rate.reshape(1, heads),
        forget.reshape(1, tokens),
        skip_gain.reshape(1, heads),
        new_keys,
        new_values,
        cache_keys,
        cache_values,
        cache_key_scale.reshape(1, channels),
        cache_value_scale.reshape(1, channels),
    )
    half = width // 2
    size = min(256, half)
    chunks = half // size
    n2 = n // 2
    levels = n2.bit_length() - 1
    fan = max(1, n2 // 2)
    dma = pltpu.SemaphoreType.DMA
    carried, allm, part, attended = pl.pallas_call(
        functools.partial(comm_kernel, n, chunks),
        out_shape=(
            shape((STATE, width), BF16),
            shape((n, 1, width + channels), F32),
            shape((tokens, width), BF16),
            shape((tokens, queries.shape[1]), BF16),
        ),
        in_specs=[VMEM] * 9,
        out_specs=(VMEM,) * 4,
        scratch_shapes=[
            pltpu.VMEM((n, rows, 2 * kvw), BF16),
            pltpu.VMEM((n, tokens, 2 * kvw), BF16),
            pltpu.VMEM((kv_here, n * rows, 2 * ATT_DIM), BF16),
            pltpu.VMEM((kv_here, n * tokens, 2 * ATT_DIM), BF16),
            pltpu.VMEM((tokens, n * tokens), F32),
            pltpu.VMEM((chunks, STATE, size), BF16),
            pltpu.VMEM((chunks, STATE, size), F32),
            pltpu.VMEM((levels, chunks, STATE, size), BF16),
            pltpu.VMEM((levels, chunks, STATE, size), BF16),
            pltpu.VMEM((chunks, STATE, size), BF16),
            dma((n,)),
            dma((n,)),
            dma((2, n2)),
            dma((2, n)),
            dma((2, n2)),
            dma((chunks,)),
            dma((chunks,)),
            dma((levels, chunks, fan)),
            dma((levels, chunks)),
            dma((levels, chunks)),
            dma((chunks,)),
            dma((chunks,)),
        ],
        compiler_params=pltpu.CompilerParams(
            collective_id=0, has_side_effects=True, vmem_limit_bytes=60 * 1024 * 1024
        ),
        name="exchange",
    )(state, kvc, kvn, meta, ssm_input, run, at, gram, queries)
    y, codes, scale = pl.pallas_call(
        final_kernel,
        out_shape=(
            shape((tokens, width), BF16),
            shape((tokens, channels), BF16),
            shape((1, channels), F32),
        ),
        in_specs=[VMEM] * 6,
        out_specs=(VMEM,) * 3,
        compiler_params=limit,
        name="finish",
    )(part, fade, state_out, carried, allm, new_keys)
    return (y, attended, codes, scale.reshape(channels))

BLOCK = 96


def span_blocks(tokens):
    return max(1, tokens // BLOCK)


def split2(value):
    high = value.astype(BF16)
    low = (value - high.astype(F32)).astype(BF16)
    return jnp.concatenate([high, low], axis=1)


def choose2(heads, begin, size):
    lane = begin + iota((2 * heads, size), 1)
    row = iota((2 * heads, size), 0)
    return (row % heads == lane // HEAD_DIM).astype(BF16)


def factor_rows(tokens):
    nb = span_blocks(tokens)
    size = tokens // nb
    places, at = {}, 0
    for name, rows in (
        [("z", tokens), ("tail", 16)]
        + [(f"z{b}", (b + 1) * size) for b in range(nb - 1)]
        + [("out", tokens), ("skip", 16), ("fade", tokens)]
    ):
        places[name] = (at, at + rows)
        at += rows
    return places, at


def with_ones(v):
    return jnp.concatenate([v, jnp.ones(v.shape, BF16)], axis=1)


NT = (((1,), (1,)), ((), ()))
FACTOR = ATT_DIM**-0.5 * LOG2E


def stream_heads(step, streams, together):
    first = step * streams * together
    return [
        [lanes((first + e * together + f) * ATT_DIM, ATT_DIM) for f in range(together)]
        for e in range(streams)
    ]


def key_columns(step, streams, together, q_ref, all_ref):
    kvw = all_ref.shape[2] // 2
    share = (q_ref.shape[1] // ATT_DIM) // (kvw // ATT_DIM)
    k = (step * streams * together) // share
    return lanes(k * ATT_DIM, ATT_DIM), lanes(kvw + k * ATT_DIM, ATT_DIM)


def score_streams(own, q_ref, keys):
    return [
        lax.dot_general(
            jnp.concatenate([q_ref[:, o] for o in heads], axis=0),
            keys,
            NT,
            preferred_element_type=F32,
        )
        for heads in own
    ]


def attend_cache(step, streams, together, q_ref, allc_ref, sum_ref, peak_ref):
    rows = together * q_ref.shape[0]
    at, av = key_columns(step, streams, together, q_ref, allc_ref)
    keys = allc_ref[:, :, at].reshape(-1, ATT_DIM)
    values = with_ones(allc_ref[:, :, av].reshape(-1, ATT_DIM))
    own = stream_heads(step, streams, together)
    scores = score_streams(own, q_ref, keys)
    for e in range(streams):
        peak = jnp.max(scores[e], axis=1, keepdims=True)
        p = jnp.exp2((scores[e] - peak) * FACTOR).astype(BF16)
        here = pl.ds(pl.multiple_of((step * streams + e) * rows, rows), rows)
        sum_ref[here, :] = jnp.dot(p, values, preferred_element_type=F32)
        peak_ref[here, :] = jnp.broadcast_to(peak, (rows, 128))


def attend_span(
    step, streams, together, chip, q_ref, alln_ref, bias_ref, sum_ref, peak_ref, att_ref
):
    tokens = q_ref.shape[0]
    rows = together * tokens
    at, av = key_columns(step, streams, together, q_ref, alln_ref)
    seen = 2 * chip + 2
    keys = alln_ref[:seen, :, at].reshape(-1, ATT_DIM)
    values = with_ones(alln_ref[:seen, :, av].reshape(-1, ATT_DIM))
    free = keys.shape[0] - 2 * tokens
    own = stream_heads(step, streams, together)
    scores = score_streams(own, q_ref, keys)
    bias = bias_ref[...]
    for e in range(streams):
        near = scores[e][:, free:].reshape(together, tokens, -1) + bias[None]
        near = near.reshape(rows, -1)
        s = jnp.concatenate([scores[e][:, :free], near], axis=1) if free else near
        here = pl.ds(pl.multiple_of((step * streams + e) * rows, rows), rows)
        before = peak_ref[here, :][:, :1]
        peak = jnp.maximum(before, jnp.max(s, axis=1, keepdims=True))
        p = jnp.exp2((s - peak) * FACTOR).astype(BF16)
        both = jnp.dot(p, values, preferred_element_type=F32)
        both += sum_ref[here, :] * jnp.exp2((before - peak) * FACTOR)
        result = (both[:, :ATT_DIM] / both[:, ATT_DIM:]).astype(BF16)
        for f, o in enumerate(own[e]):
            att_ref[:, o] = result[f * tokens : (f + 1) * tokens]


def fused_kernel(
    chunks,
    x_hbm,
    sin_hbm,
    sout_hbm,
    step_hbm,
    decay_hbm,
    forget_hbm,
    skip_hbm,
    q_hbm,
    nk_hbm,
    nv_hbm,
    ck_hbm,
    cv_hbm,
    cks_hbm,
    cvs_hbm,
    y_hbm,
    att_hbm,
    mag_hbm,
    y_ref,
    att_ref,
    mag_ref,
    step_ref,
    decay_ref,
    forget_ref,
    skip_ref,
    cks_ref,
    cvs_ref,
    x_ref,
    sin_ref,
    sout_ref,
    q_ref,
    nk_ref,
    nv_ref,
    ck_ref,
    cv_ref,
    kvc_ref,
    kvn_ref,
    allc_ref,
    alln_ref,
    bias_ref,
    meta_ref,
    allm_ref,
    fac_ref,
    fade_ref,
    z_ref,
    gram_ref,
    turned_ref,
    give_ref,
    sib_ref,
    mine_ref,
    full_ref,
    tx_ref,
    rx_ref,
    enter_ref,
    back_ref,
    other_ref,
    sum_ref,
    peak_ref,
    pick_ref,
    carry_ref,
    load_s,
    store_s,
    meta_s,
    meta_r,
    kv_s,
    kv_r,
    kv_f,
    kv_p,
    sib_s,
    sib_r,
    out_s,
    in_r,
    back_s,
    back_r,
):
    n = 8
    tokens, width = x_ref.shape
    heads = step_ref.shape[0]
    per_group = min(SSM_HEADS // GROUPS, heads)
    groups_here = heads // per_group
    channels = nk_ref.shape[1]
    kvw = kvc_ref.shape[1] // 2
    half = width // 2
    size = half // chunks
    near = chunks * 3 // 8
    mid = chunks // 2
    places, _ = factor_rows(tokens)
    nb = span_blocks(tokens)
    bs = tokens // nb

    me = lax.axis_index("seq")
    z = lax.axis_index("head")
    i, c = me % 2, me // 2
    other = me + 1 - 2 * i
    cx, cy = c + 1 - 2 * (c % 2), (c + 2) % 4
    cd = 3 - c
    group0 = z * heads // (SSM_HEADS // GROUPS)
    q_heads = heads * ATT_HEADS // SSM_HEADS
    first_kv = z * q_heads // (ATT_HEADS // KV_HEADS)
    cols = lanes(first_kv * ATT_DIM, kvw)
    gcols = lanes(group0 * STATE, groups_here * STATE)

    barrier = pltpu.get_barrier_semaphore()
    for d in range(1, n):
        pl.semaphore_signal(
            barrier, inc=1, device_id={"seq": (me + d) % n}, device_id_type=MESH
        )

    moves = dict(
        ck=(ck_hbm.at[:, cols], ck_ref),
        cks=(cks_hbm.at[:, cols], cks_ref),
        cv=(cv_hbm.at[:, cols], cv_ref),
        cvs=(cvs_hbm.at[:, cols], cvs_ref),
        nv=(nv_hbm.at[:, cols], nv_ref),
        nk=(nk_hbm, nk_ref),
        step=(step_hbm, step_ref),
        decay=(decay_hbm, decay_ref),
        forget=(forget_hbm, forget_ref),
        skip=(skip_hbm, skip_ref),
        sin=(sin_hbm.at[:, gcols], sin_ref),
        sout=(sout_hbm.at[:, gcols], sout_ref),
        x=(x_hbm, x_ref),
        q=(q_hbm, q_ref),
    )
    loads = {
        name: pltpu.make_async_copy(src, dst, load_s.at[k])
        for k, (name, (src, dst)) in enumerate(moves.items())
    }
    for copy in loads.values():
        copy.start()

    def ready(*names):
        for name in names:
            loads[name].wait()

    def remote(src, dst, ssem, rsem, to):
        return pltpu.make_async_remote_copy(
            src_ref=src,
            dst_ref=dst,
            send_sem=ssem,
            recv_sem=rsem,
            device_id={"seq": to},
            device_id_type=MESH,
        )

    def dev(chip):
        return chip * 2 + i

    alls = (allc_ref, alln_ref)
    owns = (kvc_ref, kvn_ref)

    def own_copy(kind, way):
        to = (other, dev(cx), dev(cy))[way]
        return remote(
            owns[kind], alls[kind].at[me], kv_s.at[kind, way], kv_r.at[kind, me], to
        )

    def pass_copy(kind, way, chip, to):
        slot = dev(chip)
        return remote(
            alls[kind].at[slot],
            alls[kind].at[slot],
            kv_p.at[kind, way],
            kv_r.at[kind, slot],
            dev(to),
        )

    def forward(kind, chip):
        slot = dev(chip)
        return remote(
            alls[kind].at[slot],
            alls[kind].at[slot],
            kv_f.at[kind, chip],
            kv_r.at[kind, slot],
            other,
        )

    def arrived(kind, slot):
        remote(
            owns[kind], alls[kind].at[slot], kv_s.at[kind, 0], kv_r.at[kind, slot], other
        ).wait_recv()

    for k in range(width // 512):
        pick_ref[:, k * 512 : (k + 1) * 512] = choose2(heads, k * 512, 512)
    ready("ck", "cks", "cv", "cvs")
    kvc_ref[:, :kvw] = (ck_ref[...].astype(F32) * cks_ref[...]).astype(BF16)
    kvc_ref[:, kvw:] = (cv_ref[...].astype(F32) * cvs_ref[...]).astype(BF16)
    pl.semaphore_wait(barrier, n - 1)
    for way in (1, 2, 0):
        own_copy(0, way).start()
    ready("nv", "nk")
    kvn_ref[:, :kvw] = nk_ref[:, cols]
    kvn_ref[:, kvw:] = nv_ref[...]

    @pl.when(cx > c)
    def _():
        own_copy(1, 1).start()

    @pl.when(cy > c)
    def _():
        own_copy(1, 2).start()

    own_copy(1, 0).start()

    row, col = iota((tokens, tokens), 0), iota((tokens, tokens), 1)
    lower = jnp.where(col <= row, 1.0, 0.0)
    eye = jnp.where(col == row, 1.0, 0.0).astype(BF16)
    ready("step", "decay", "forget", "skip")
    step = step_ref[...].T
    forgotten = jnp.sum(lower * forget_ref[...], axis=1, keepdims=True)
    decayed = jnp.dot(
        lower, decay_ref[...] * step, precision=HIGHEST, preferred_element_type=F32
    )
    running = -(decayed + forgotten) * LOG2E
    start = running - jnp.log2(step)
    last = running[tokens - 1 : tokens]
    middles = [running[b * bs + bs // 2 - 1 : b * bs + bs // 2] for b in range(nb)]

    meta_ref[:, :channels] = jnp.max(jnp.abs(nk_ref[...].astype(F32)), axis=0, keepdims=True)
    meta_ref[:, channels:] = jnp.concatenate([last, jnp.zeros((1, 128 - heads), F32)], axis=1)

    def meta_copy(d):
        return remote(
            meta_ref, allm_ref.at[me], meta_s.at[d], meta_r.at[me], (me + d) % n
        )

    def meta_arrived(r):
        remote(meta_ref, allm_ref.at[r], meta_s.at[1], meta_r.at[r], r).wait_recv()

    for d in range(1, n):
        meta_copy(d).start()
    allm_ref[me] = meta_ref[...]

    def put(name, value):
        begin, end = places[name]
        fac_ref[begin:end] = split2(jnp.broadcast_to(value, (end - begin, heads)))

    put("z", jnp.exp2(middles[nb - 1] - start))
    put("tail", jnp.exp2(last - middles[nb - 1]))
    for b in range(nb - 1):
        put(f"z{b}", jnp.exp2(middles[b] - start[: (b + 1) * bs]))
    put(
        "out",
        jnp.concatenate(
            [jnp.exp2(running[b * bs : (b + 1) * bs] - middles[b]) for b in range(nb)], axis=0
        ),
    )
    put("skip", skip_ref[...])
    put("fade", jnp.exp2(running))
    ready("sin", "sout")
    for g in range(groups_here):
        gc = slice(g * STATE, (g + 1) * STATE)
        maps_in = sin_ref[:, gc]
        gram = lax.dot_general(
            sout_ref[:, gc], maps_in, (((1,), (1,)), ((), ())), preferred_element_type=F32
        )
        gram_ref[g] = jnp.where(col <= row, gram, 0.0).astype(BF16)
        turned_ref[g] = lax.dot_general(
            maps_in, eye, (((0,), (0,)), ((), ())), preferred_element_type=F32
        ).astype(BF16)
    ready("x")

    def spread(first, final, begin, wide=size):
        rows = fac_ref[places[first][0] : places[final][1]]
        return jnp.dot(rows, pick_ref[:, lanes(begin, wide)], preferred_element_type=F32)

    def local_state(begin):
        here = lanes(begin, 2 * size)
        by = spread("z", "tail", begin, 2 * size)
        scaled = (x_ref[:, here].astype(F32) * by[:tokens]).astype(BF16)
        z_ref[:, here] = scaled
        sums = jnp.dot(
            turned_ref[begin // (per_group * HEAD_DIM)], scaled, preferred_element_type=F32
        )
        sums = (sums * by[tokens : tokens + 1]).astype(BF16)
        return sums[:, :size], sums[:, size:]

    def sib_copy(j):
        return remote(give_ref.at[j], sib_ref.at[j], sib_s.at[j], sib_r.at[j], other)

    shift = (c % 2) * (1 - c // 2) * mid

    def give(s, _):
        j = (2 * s + shift) % chunks
        for e, state in enumerate(local_state((1 - i) * half + j * size)):
            give_ref[j + e] = state
            sib_copy(j + e).start()
        return 0

    def pass_cache():
        arrived(0, dev(cx))

        @pl.when(c >= 1)
        def _():
            pass_copy(0, 0, cx, cy).start()

        forward(0, cx).start()
        arrived(0, dev(cy))

        @pl.when(c == 3)
        def _():
            pass_copy(0, 1, cy, cx).start()

        forward(0, cy).start()

    lax.fori_loop(0, chunks // 2, give, 0)
    pass_cache()
    meta_arrived(other)

    def logs_of(r):
        return allm_ref[r, :, channels : channels + heads]

    def set_fades(third):
        logs = jnp.concatenate(
            [logs_of(2 * c), logs_of(2 * c + 1), third, jnp.zeros((13, heads), F32)], axis=0
        )
        fade_ref[...] = split2(jnp.exp2(logs))

    def fades(j):
        return jnp.dot(
            fade_ref[...],
            pick_ref[:, lanes(i * half + j * size, size)],
            preferred_element_type=F32,
        )

    set_fades(jnp.zeros((1, heads), F32))

    def full_copy(j):
        slot = jnp.where(c == 0, 0, 1)
        return remote(
            full_ref.at[j], rx_ref.at[slot, j], out_s.at[0, j], in_r.at[slot, j], dev(cx)
        )

    def full_sent(j):
        return (c == 0) | ((c == 1) & (j >= near)) | ((c == 2) & (j < near))

    def own(s, _):
        j = (2 * s + shift) % chunks
        states = local_state(i * half + j * size)
        for e, mine in enumerate(states):
            mine_ref[j + e] = mine
        for e in range(2):
            sib_copy(j + e).wait_recv()
        for e, mine in enumerate(states):
            mine, theirs = mine.astype(F32), sib_ref[j + e].astype(F32)
            d1 = fades(j + e)[1:2]
            full = jnp.where(i == 0, d1 * mine + theirs, d1 * theirs + mine)
            full_ref[j + e] = full.astype(BF16)

        for e in range(2):

            @pl.when(full_sent(j + e))
            def _():
                full_copy(j + e).start()

        return 0

    lax.fori_loop(0, chunks // 2, own, 0)
    bias_ref[...] = jnp.where(
        iota((tokens, 2 * tokens), 1) <= i * tokens + iota((tokens, 2 * tokens), 0), 0.0, NEG
    )

    def within(s, _):
        begin = s * 2 * size
        here = lanes(begin, 2 * size)
        by = spread("z0" if nb > 1 else "out", "skip", begin, 2 * size)
        at = 0
        gram = gram_ref[begin // (per_group * HEAD_DIM)]
        x = x_ref[:, here].astype(F32)
        parts = []
        for b in range(nb):
            high = (b + 1) * bs
            if b + 1 < nb:
                scaled = (x[:high] * by[at : at + high]).astype(BF16)
                at += high
            else:
                scaled = z_ref[:, here]
            parts.append(
                jnp.dot(gram[b * bs : high, :high], scaled, preferred_element_type=F32)
            )
        y = by[at : at + tokens] * jnp.concatenate(parts, axis=0)
        y_ref[:, here] = (y + by[at + tokens : at + tokens + 1] * x).astype(BF16)
        return 0

    @pl.when(cx < c)
    def _():
        arrived(1, dev(cx))

        @pl.when(c == 1)
        def _():
            pass_copy(1, 0, cx, cy).start()

        forward(1, cx).start()

    @pl.when(cy < c)
    def _():
        arrived(1, dev(cy))

        @pl.when(c == 3)
        def _():
            pass_copy(1, 1, cy, cx).start()

        forward(1, cy).start()

    lax.fori_loop(0, chunks // 2, within, 0)
    arrived(0, dev(cd))
    forward(0, cd).start()
    lax.fori_loop(chunks // 2, chunks, within, 0)

    for d in range(1, n):
        r = (me + d) % n

        @pl.when(r != other)
        def _():
            meta_arrived(r)

    chip = jnp.where(c == 0, 1, jnp.where(c == 3, 2, c))
    set_fades(logs_of(2 * chip) + logs_of(2 * chip + 1))
    mag_ref[...] = jnp.max(allm_ref[:, 0, :channels], axis=0, keepdims=True)
    mag_out = pltpu.make_async_copy(mag_ref, mag_hbm, store_s.at[2 * chunks])
    mag_out.start()

    allc_ref[me] = kvc_ref[...]
    alln_ref[me] = kvn_ref[...]
    arrived(0, other)
    for d in range(1, 4):
        arrived(0, (c + d) % 4 * 2 + 1 - i)

    ready("q")

    def span_arrived():
        @pl.when(cd < c)
        def _():
            arrived(1, dev(cd))
            forward(1, cd).start()

        arrived(1, other)
        for d in range(1, 4):
            there = (c + d) % 4

            @pl.when(there < c)
            def _():
                arrived(1, there * 2 + 1 - i)

    def second_way(s):
        late = s // mid
        return mid + s - late * (2 * mid - near)

    def order(s):
        later = s // (chunks - near)
        even = (1 - later) * second_way(s * (1 - later)) + later * (s - chunks + near)
        last = (s + chunks - near) // chunks
        odd = (1 - last) * s + last * second_way((s - near) * last)
        third = c // 2
        return (1 - c % 2) * even + (c % 2) * (third * odd + (1 - third) * s)

    def y_out(k):
        here = lanes(k * size, size)
        return pltpu.make_async_copy(y_ref.at[:, here], y_hbm.at[:, here], store_s.at[k])

    def prior(begin, carried):
        here = lanes(begin, size)
        group = begin // (per_group * HEAD_DIM)
        term = jnp.dot(sout_ref[:, lanes(group * STATE, STATE)], carried, preferred_element_type=F32)
        by = spread("fade", "fade", begin)
        return begin, (y_ref[:, here].astype(F32) + by * term).astype(BF16)

    def put_prior(result):
        begin, value = result
        y_ref[:, lanes(begin, size)] = value
        y_out(begin // size).start()

    def rx_wait(slot, j):
        remote(
            full_ref.at[j], rx_ref.at[slot, j], out_s.at[0, j], in_r.at[slot, j], dev(cx)
        ).wait_recv()

    def tx_copy(j, chip):
        return remote(tx_ref.at[j], rx_ref.at[0, j], out_s.at[1, j], in_r.at[0, j], dev(chip))

    def relay_copy(j):
        return remote(
            rx_ref.at[0, j], rx_ref.at[0, j], out_s.at[2, j], in_r.at[0, j], dev(cx)
        )

    def back_copy(j):
        return remote(back_ref.at[j], other_ref.at[j], back_s.at[j], back_r.at[j], other)

    def pass_on(s):
        @pl.when((c == 1) | (c == 2))
        def _():
            j = (c % 2) * s + (1 - c % 2) * second_way(s)
            rx_wait(0, j)
            keep = fades(j)[2:3]
            tx_ref[j] = (keep * rx_ref[0, j].astype(F32) + full_ref[j].astype(F32)).astype(BF16)
            tx_copy(j, 3).start()

        @pl.when(c == 0)
        def _():
            j = second_way(s)
            rx_wait(1, j)
            keep = fades(j)[2:3]
            tx_ref[j] = (keep * full_ref[j].astype(F32) + rx_ref[1, j].astype(F32)).astype(BF16)
            tx_copy(j, 2).start()

        @pl.when(c == 3)
        def _():
            rx_wait(0, s)
            relay_copy(s).start()

    base = 2 + (c // 2) * (4 + c % 2)
    stride = 1 + (c % 2) * (1 - c // 2)
    passes = (c % 2) * near + (1 - c % 2) * (chunks - near)

    def pass_at(place):
        ahead = place - base
        s = ahead // stride

        @pl.when((ahead >= 0) & (ahead % stride == 0) & (s < passes))
        def _():
            pass_on(s)

    def settle(s):
        j = order(s)
        by = fades(j)
        d0, keep = by[0:1], by[2:3]

        @pl.when((c > 0) & (s >= passes))
        def _():
            rx_wait(0, j)

        @pl.when((c == 3) & (s < near))
        def _():
            rx_wait(1, j)
            enter_ref[...] = keep * rx_ref[0, j].astype(F32) + rx_ref[1, j].astype(F32)

        @pl.when(c == 0)
        def _():
            enter_ref[...] = jnp.zeros(enter_ref.shape, F32)

        @pl.when((c == 1) | (c == 2) | ((c == 3) & (s >= near)))
        def _():
            enter_ref[...] = rx_ref[0, j].astype(F32)

        enter = enter_ref[...]
        first = jnp.where(i == 0, mine_ref[j].astype(F32), sib_ref[j].astype(F32))
        middle = d0 * enter + first
        back_ref[j] = jnp.where(i == 0, middle, enter).astype(BF16)
        back_copy(j).start()
        carry_ref[...] = jnp.where(i == 0, enter, middle).astype(BF16)

    def slot(s, _):
        settle(s)

        @pl.when(s == 0)
        def _():
            put_prior(prior(i * half + order(s) * size, carry_ref[...]))

        @pl.when(s > 0)
        def _():
            far = order(s - 1)
            back_copy(far).wait_recv()
            both = [
                prior(i * half + order(s) * size, carry_ref[...]),
                prior((1 - i) * half + far * size, other_ref[far]),
            ]
            for each in both:
                put_prior(each)

        return 0

    streams, together = 4, 1
    steps = q_heads // (streams * together)
    pass_at(2)

    def first_part(h, _):
        attend_cache(h, streams, together, q_ref, allc_ref, sum_ref, peak_ref)
        pass_at(3 + h)
        return 0

    lax.fori_loop(0, steps, first_part, 0)
    span_arrived()

    def second_part(h, _):
        for chip in range(n // 2):

            @pl.when(c == chip)
            def _():
                attend_span(
                    h,
                    streams,
                    together,
                    chip,
                    q_ref,
                    alln_ref,
                    bias_ref,
                    sum_ref,
                    peak_ref,
                    att_ref,
                )

        pass_at(3 + steps + h)
        return slot(h, 0)

    lax.fori_loop(0, steps, second_part, 0)
    att_out = pltpu.make_async_copy(att_ref, att_hbm, store_s.at[2 * chunks + 1])
    att_out.start()
    lax.fori_loop(steps, chunks, slot, 0)
    far = order(chunks - 1)
    back_copy(far).wait_recv()
    put_prior(prior((1 - i) * half + far * size, other_ref[far]))

    def drain(j, _):
        back_copy(j).wait_send()
        sib_copy(j).wait_send()

        @pl.when(full_sent(j))
        def _():
            full_copy(j).wait_send()

        @pl.when(((c == 1) & (j < near)) | ((c == 2) & (j >= near)))
        def _():
            tx_copy(j, 3).wait_send()

        @pl.when((c == 0) & (j >= near))
        def _():
            tx_copy(j, 2).wait_send()

        @pl.when((c == 3) & (j < near))
        def _():
            relay_copy(j).wait_send()

        return 0

    lax.fori_loop(0, chunks, drain, 0)

    def stored(k, _):
        y_out(k).wait()
        return 0

    lax.fori_loop(0, 2 * chunks, stored, 0)
    mag_out.wait()
    att_out.wait()
    for d in range(1, n):
        meta_copy(d).wait_send()
    for way in (1, 2, 0):
        own_copy(0, way).wait_send()
    own_copy(1, 0).wait_send()

    @pl.when(cx > c)
    def _():
        own_copy(1, 1).wait_send()

    @pl.when(cy > c)
    def _():
        own_copy(1, 2).wait_send()

    @pl.when(c >= 1)
    def _():
        pass_copy(0, 0, cx, cy).wait_send()

    @pl.when(c == 3)
    def _():
        pass_copy(0, 1, cy, cx).wait_send()
        pass_copy(1, 1, cy, cx).wait_send()

    @pl.when(c == 1)
    def _():
        pass_copy(1, 0, cx, cy).wait_send()

    for chip_ in (cx, cy, cd):
        forward(0, chip_).wait_send()

        @pl.when(chip_ < c)
        def _():
            forward(1, chip_).wait_send()


def finish_kernel(
    y_hbm, att_hbm, mag_hbm, nk_hbm, yo_hbm, atto_hbm, code_hbm, scale_ref,
    y_ref, att_ref, mag_ref, nk_ref, code_ref, in_s, out_s,
):
    pieces = 4
    wide, slim = y_ref.shape[0] // pieces, att_ref.shape[0] // pieces
    mag_in = pltpu.make_async_copy(mag_hbm, mag_ref, in_s.at[2 * pieces])
    nk_in = pltpu.make_async_copy(nk_hbm, nk_ref, in_s.at[2 * pieces + 1])
    code_out = pltpu.make_async_copy(code_ref, code_hbm, out_s.at[2 * pieces])
    ins, outs = [], []
    for p in range(pieces):
        for k, (src, mid, dst, rows) in enumerate(
            [(y_hbm, y_ref, yo_hbm, wide), (att_hbm, att_ref, atto_hbm, slim)]
        ):
            at = pl.ds(p * rows, rows)
            ins.append(pltpu.make_async_copy(src.at[at], mid.at[at], in_s.at[2 * p + k]))
            outs.append(pltpu.make_async_copy(mid.at[at], dst.at[at], out_s.at[2 * p + k]))
    mag_in.start()
    nk_in.start()
    for copy in ins:
        copy.start()
    mag_in.wait()
    nk_in.wait()
    scale = (mag_ref[...] + 1e-6) / 127.0
    scale_ref[...] = scale
    code_ref[...] = (nk_ref[...].astype(F32) / scale).astype(BF16)
    code_out.start()
    for a, b in zip(ins, outs):
        a.wait()
        b.start()
    code_out.wait()
    for b in outs:
        b.wait()


def fused_body(
    ssm_input,
    state_in,
    state_out,
    step_size,
    decay_rate,
    forget,
    skip_gain,
    queries,
    new_keys,
    new_values,
    cache_keys,
    cache_values,
    cache_key_scale,
    cache_value_scale,
):
    n = 8
    tokens, width = ssm_input.shape
    heads = step_size.shape[1]
    rows = cache_keys.shape[0]
    channels = new_keys.shape[1]
    q_width = queries.shape[1]
    kv_here = max(1, q_width // ATT_DIM // (ATT_HEADS // KV_HEADS))
    kvw = kv_here * ATT_DIM
    groups_here = heads // min(SSM_HEADS // GROUPS, heads)
    half = width // 2
    size = min(256, half)
    chunks = half // size
    _, fac = factor_rows(tokens)
    shape = jax.ShapeDtypeStruct
    dma = pltpu.SemaphoreType.DMA
    any_ = pl.BlockSpec(memory_space=pl.ANY)
    piece = pltpu.VMEM((chunks, STATE, size), BF16)
    y, attended, mag = pl.pallas_call(
        functools.partial(fused_kernel, chunks),
        out_shape=(
            shape((tokens, width), BF16),
            shape((tokens, q_width), BF16),
            shape((1, channels), F32),
        ),
        in_specs=[any_] * 14,
        out_specs=(any_,) * 3,
        scratch_shapes=[
            pltpu.VMEM((tokens, width), BF16),
            pltpu.VMEM((tokens, q_width), BF16),
            pltpu.VMEM((1, channels), F32),
            pltpu.VMEM((heads, tokens), F32),
            pltpu.VMEM((1, heads), F32),
            pltpu.VMEM((1, tokens), F32),
            pltpu.VMEM((1, heads), F32),
            pltpu.VMEM((1, kvw), F32),
            pltpu.VMEM((1, kvw), F32),
            pltpu.VMEM((tokens, width), BF16),
            pltpu.VMEM((tokens, groups_here * STATE), BF16),
            pltpu.VMEM((tokens, groups_here * STATE), BF16),
            pltpu.VMEM((tokens, q_width), BF16),
            pltpu.VMEM((tokens, channels), BF16),
            pltpu.VMEM((tokens, kvw), BF16),
            pltpu.VMEM((rows, kvw), BF16),
            pltpu.VMEM((rows, kvw), BF16),
            pltpu.VMEM((rows, 2 * kvw), BF16),
            pltpu.VMEM((tokens, 2 * kvw), BF16),
            pltpu.VMEM((n, rows, 2 * kvw), BF16),
            pltpu.VMEM((n, tokens, 2 * kvw), BF16),
            pltpu.VMEM((tokens, 2 * tokens), F32),
            pltpu.VMEM((1, channels + 128), F32),
            pltpu.VMEM((n, 1, channels + 128), F32),
            pltpu.VMEM((fac, 2 * heads), BF16),
            pltpu.VMEM((16, 2 * heads), BF16),
            pltpu.VMEM((tokens, width), BF16),
            pltpu.VMEM((groups_here, tokens, tokens), BF16),
            pltpu.VMEM((groups_here, STATE, tokens), BF16),
            piece,
            piece,
            piece,
            piece,
            piece,
            pltpu.VMEM((2, chunks, STATE, size), BF16),
            pltpu.VMEM((STATE, size), F32),
            piece,
            piece,
            pltpu.VMEM((q_width // ATT_DIM * tokens, 2 * ATT_DIM), F32),
            pltpu.VMEM((q_width // ATT_DIM * tokens, 128), F32),
            pltpu.VMEM((2 * heads, width), BF16),
            pltpu.VMEM((STATE, size), BF16),
            dma((14,)),
            dma((2 * chunks + 2,)),
            dma((n,)),
            dma((n,)),
            dma((2, 3)),
            dma((2, n)),
            dma((2, 4)),
            dma((2, 2)),
            dma((chunks,)),
            dma((chunks,)),
            dma((3, chunks)),
            dma((2, chunks)),
            dma((chunks,)),
            dma((chunks,)),
        ],
        compiler_params=pltpu.CompilerParams(
            collective_id=0, has_side_effects=True, vmem_limit_bytes=60 * 1024 * 1024
        ),
        name="fused",
    )(
        ssm_input,
        state_in,
        state_out,
        step_size.T,
        decay_rate.reshape(1, heads),
        forget.reshape(1, tokens),
        skip_gain.reshape(1, heads),
        queries,
        new_keys,
        new_values,
        cache_keys,
        cache_values,
        cache_key_scale.reshape(1, channels),
        cache_value_scale.reshape(1, channels),
    )
    y, attended, codes, scale = pl.pallas_call(
        finish_kernel,
        out_shape=(
            shape((tokens, width), BF16),
            shape((tokens, q_width), BF16),
            shape((tokens, channels), BF16),
            shape((1, channels), F32),
        ),
        in_specs=[any_] * 4,
        out_specs=(any_,) * 3 + (VMEM,),
        scratch_shapes=[
            pltpu.VMEM((tokens, width), BF16),
            pltpu.VMEM((tokens, q_width), BF16),
            pltpu.VMEM((1, channels), F32),
            pltpu.VMEM((tokens, channels), BF16),
            pltpu.VMEM((tokens, channels), BF16),
            dma((10,)),
            dma((9,)),
        ],
        name="finish",
    )(y, attended, mag, new_keys)
    return (y, attended, codes, scale.reshape(channels))


def fits_fused(mesh):
    heads = SSM_HEADS // mesh.shape["head"]
    return mesh.shape["seq"] == 8 and heads == 64


def solution(mesh):
    in_specs = (
        P("seq", "head"),
        P("seq", None),
        P("seq", None),
        P("seq", "head"),
        P("head"),
        P("seq"),
        P("head"),
        P("seq", "head"),
        P("seq", None),
        P("seq", None),
        P("seq", None),
        P("seq", None),
        P(),
        P(),
    )
    out_specs = (P("seq", "head"), P("seq", "head"), P("seq", None), P())
    general = functools.partial(body, mesh.shape["seq"])
    return jax.shard_map(
        fused_body if fits_fused(mesh) else general,
        mesh=mesh,
        in_specs=in_specs,
        out_specs=out_specs,
        check_vma=False,
    )
```

```python
import functools
import jax
import jax.numpy as jnp
from jax import lax
from jax.experimental import pallas as pl
from jax.experimental.pallas import tpu as pltpu
from jax.sharding import PartitionSpec as P

SSM_HEADS = 256
HEAD_DIM = 64
STATE = 256
GROUPS = 8
ATT_HEADS = 64
KV_HEADS = 8
ATT_DIM = 128

NEG = -1e30
LOG2E = 1.4426950408889634
HIGHEST = lax.Precision.HIGHEST
MESH = pl.DeviceIdType.MESH
VMEM = pl.BlockSpec(memory_space=pltpu.VMEM)
F32 = jnp.float32
BF16 = jnp.bfloat16


def iota(shape, axis):
    return lax.broadcasted_iota(jnp.int32, shape, axis)


def lanes(start, size):
    return pl.ds(pl.multiple_of(start, 128), size)


def local_kernel(
    x_ref,
    sin_ref,
    sout_ref,
    step_ref,
    decay_ref,
    forget_ref,
    skip_ref,
    nk_ref,
    nv_ref,
    ck_ref,
    cv_ref,
    cks_ref,
    cvs_ref,
    state_ref,
    run_ref,
    fade_ref,
    at_ref,
    gram_ref,
    meta_ref,
    kvc_ref,
    kvn_ref,
):
    tokens, width = x_ref.shape
    heads = step_ref.shape[0]
    per_group = min(SSM_HEADS // GROUPS, heads)
    groups_here = heads // per_group
    z = lax.axis_index("head")
    group0 = z * heads // (SSM_HEADS // GROUPS)
    kvw = kvc_ref.shape[1] // 2
    q_heads = heads * ATT_HEADS // SSM_HEADS
    first = z * q_heads // (ATT_HEADS // KV_HEADS)
    cols = lanes(first * ATT_DIM, kvw)
    kvc_ref[:, :kvw] = (ck_ref[:, cols].astype(F32) * cks_ref[:, cols]).astype(BF16)
    kvc_ref[:, kvw:] = (cv_ref[:, cols].astype(F32) * cvs_ref[:, cols]).astype(BF16)
    kvn_ref[:, :kvw] = nk_ref[:, cols]
    kvn_ref[:, kvw:] = nv_ref[:, cols]
    meta_ref[:, width:] = jnp.max(jnp.abs(nk_ref[...].astype(F32)), axis=0, keepdims=True)

    row, col = iota((tokens, tokens), 0), iota((tokens, tokens), 1)
    lower = jnp.where(col <= row, 1.0, 0.0)
    eye = jnp.where(col == row, 1.0, 0.0)
    step = step_ref[...].T
    forgotten = jnp.sum(lower * forget_ref[...], axis=1, keepdims=True)
    decayed = jnp.dot(
        lower, decay_ref[...] * step, precision=HIGHEST, preferred_element_type=F32
    )
    running = -(decayed + forgotten) * LOG2E
    start = running - jnp.log2(step)
    at_ref[...] = start.T
    rest = jnp.concatenate(
        [running, jnp.broadcast_to(skip_ref[...], (16, heads))], axis=0
    )
    for third in range(3):
        piece = rest.astype(BF16)
        run_ref[:, third * heads : (third + 1) * heads] = piece
        rest = rest - piece.astype(F32)
    fade_ref[...] = jnp.exp2(running).astype(BF16)
    tail = jnp.exp2(running[tokens - 1 : tokens] - start).astype(BF16)
    last = running[tokens - 8 : tokens]
    block = min(512, width)
    for g in range(groups_here):
        gcols = lanes((group0 + g) * STATE, STATE)
        maps_in = sin_ref[:, gcols]
        gram_ref[g] = lax.dot_general(
            sout_ref[:, gcols], maps_in, (((1,), (1,)), ((), ())), preferred_element_type=F32
        )
        turned = lax.dot_general(
            maps_in,
            eye.astype(BF16),
            (((0,), (0,)), ((), ())),
            preferred_element_type=F32,
        ).astype(BF16)
        for b in range(per_group * HEAD_DIM // block):
            begin = g * per_group * HEAD_DIM + b * block
            here = pl.ds(begin, block)
            pick = choose(heads, begin, block)
            meta_ref[:, here] = jnp.dot(
                last, pick, precision=HIGHEST, preferred_element_type=F32
            )[7:8]
            scale = jnp.dot(tail, pick.astype(BF16), preferred_element_type=F32)
            scaled = (x_ref[:, here].astype(F32) * scale).astype(BF16)
            state_ref[:, here] = jnp.dot(
                turned, scaled, preferred_element_type=F32
            ).astype(BF16)


def choose(heads, begin, size):
    lane = begin + iota((heads, size), 1)
    return (iota((heads, size), 0) == lane // HEAD_DIM).astype(F32)


def within_pair(p, x_ref, run_ref, at_ref, gram_ref, part_ref):
    tokens = x_ref.shape[0]
    heads = run_ref.shape[1] // 3
    per_group = min(SSM_HEADS // GROUPS, heads)
    here = lanes(p * 128, 128)
    pick = choose(heads, p * 128, 128).astype(BF16)
    both = jnp.dot(
        run_ref[...], jnp.concatenate([pick] * 3, axis=0), preferred_element_type=F32
    )
    run, skip = both[:tokens], both[tokens : tokens + 1]
    x = x_ref[:, here]
    gram = gram_ref[(2 * p) // per_group]
    causal = iota((tokens, tokens), 1) <= iota((tokens, tokens), 0)

    def one(k):
        spread = run[:, k * HEAD_DIM : k * HEAD_DIM + 1] - at_ref[pl.ds(2 * p + k, 1), :]
        return (jnp.exp2(jnp.where(causal, spread, NEG)) * gram).astype(BF16)

    pair = jnp.dot(
        jnp.concatenate([one(0), one(1)], axis=0), x, preferred_element_type=F32
    )
    y = jnp.where(iota((tokens, 128), 1) < HEAD_DIM, pair[:tokens], pair[tokens:])
    part_ref[:, here] = (y + skip * x.astype(F32)).astype(BF16)


def attend(h, q_ref, allc_ref, alln_ref, bias_ref, vc_ref, vn_ref, att_ref):
    q_heads = q_ref.shape[1] // ATT_DIM
    kv_here = vc_ref.shape[0]
    share = q_heads // kv_here
    together = 2 if share % 2 == 0 else 1
    tokens = q_ref.shape[0]
    k = (h * together) // share
    factor = ATT_DIM**-0.5 * LOG2E
    nt = (((1,), (1,)), ((), ()))
    own = [lanes((h * together + e) * ATT_DIM, ATT_DIM) for e in range(together)]
    q = jnp.concatenate([q_ref[:, o] for o in own], axis=0)
    at = lanes(k * ATT_DIM, ATT_DIM)
    keys_c = allc_ref[:, :, at].reshape(-1, ATT_DIM)
    keys_n = alln_ref[:, :, at].reshape(-1, ATT_DIM)
    old = lax.dot_general(q, keys_c, nt, preferred_element_type=F32)
    new = lax.dot_general(q, keys_n, nt, preferred_element_type=F32)
    bias = bias_ref[...]
    new = (new.reshape(together, tokens, -1) + bias[None]).reshape(together * tokens, -1)
    peak = jnp.maximum(
        jnp.max(old, axis=1, keepdims=True), jnp.max(new, axis=1, keepdims=True)
    )
    old = jnp.exp2((old - peak) * factor).astype(BF16)
    new = jnp.exp2((new - peak) * factor).astype(BF16)
    both = jnp.dot(old, vc_ref[k], preferred_element_type=F32) + jnp.dot(
        new, vn_ref[k], preferred_element_type=F32
    )
    result = (both[:, :ATT_DIM] / both[:, ATT_DIM:]).astype(BF16)
    for e in range(together):
        att_ref[:, own[e]] = result[e * tokens : (e + 1) * tokens]


def comm_kernel(
    n,
    chunks,
    state_ref,
    kvc_ref,
    kvn_ref,
    meta_ref,
    x_ref,
    run_ref,
    at_ref,
    gram_ref,
    q_ref,
    out_ref,
    allm_ref,
    part_ref,
    att_ref,
    allc_ref,
    alln_ref,
    vc_ref,
    vn_ref,
    bias_ref,
    sib_ref,
    own_ref,
    incl_ref,
    recv_ref,
    back_ref,
    meta_s,
    meta_r,
    kv_s,
    kv_r,
    kv_f,
    sib_s,
    sib_r,
    pre_s,
    pre_r,
    rel_s,
    back_s,
    back_r,
):
    n2 = n // 2
    levels = n2.bit_length() - 1
    me = lax.axis_index("seq")
    i, c = me % 2, me // 2
    other = me + 1 - 2 * i
    width = state_ref.shape[1]
    half = width // 2
    size = half // chunks

    barrier = pltpu.get_barrier_semaphore()
    for d in range(1, n):
        pl.semaphore_signal(
            barrier, inc=1, device_id={"seq": (me + d) % n}, device_id_type=MESH
        )
    pl.semaphore_wait(barrier, n - 1)

    def remote(src, dst, ssem, rsem, to):
        return pltpu.make_async_remote_copy(
            src_ref=src,
            dst_ref=dst,
            send_sem=ssem,
            recv_sem=rsem,
            device_id={"seq": to},
            device_id_type=MESH,
        )

    def sib_copy(j):
        return remote(
            state_ref.at[:, lanes((1 - i) * half + j * size, size)],
            sib_ref.at[j],
            sib_s.at[j],
            sib_r.at[j],
            other,
        )

    for j in range(chunks):
        sib_copy(j).start()
    for d in range(1, n):
        remote(
            meta_ref, allm_ref.at[me], meta_s.at[d], meta_r.at[me], (me + d) % n
        ).start()

    def cache_copy(d, to):
        return remote(kvc_ref, allc_ref.at[me], kv_s.at[0, d], kv_r.at[0, me], to)

    def new_copy(d, to):
        return remote(kvn_ref, alln_ref.at[me], kv_s.at[1, d], kv_r.at[1, me], to)

    cache_copy(0, other).start()
    new_copy(0, other).start()
    for d in range(1, n2):
        to = ((c + d) % n2) * 2 + i
        cache_copy(d, to).start()

        @pl.when(c + d < n2)
        def _():
            new_copy(d, to).start()

    allm_ref[me] = meta_ref[...]
    allc_ref[me] = kvc_ref[...]
    alln_ref[me] = kvn_ref[...]
    for d in range(1, n2):
        later = c + d

        @pl.when(later < n2)
        def _():
            for k in range(2):
                alln_ref[later * 2 + k] = jnp.zeros(kvn_ref.shape, BF16)

    for d in range(1, n):
        r = (me + d) % n
        remote(meta_ref, allm_ref.at[r], meta_s.at[d], meta_r.at[r], r).wait_recv()

    def sends(l):
        return c % (2 ** (l + 1)) == 2**l - 1

    def targets(l):
        return [0] if l == 0 else list(range(1, 2**l, 2))

    def pre_copy(l, j, r):
        return remote(
            incl_ref.at[l, j],
            recv_ref.at[l, j],
            pre_s.at[l, j, r],
            pre_r.at[l, j],
            ((c + 1 + r) % n2) * 2 + i,
        )

    def relay_copy(l, j):
        return remote(
            recv_ref.at[l, j],
            recv_ref.at[l, j],
            rel_s.at[l, j],
            pre_r.at[l, j],
            ((c + n2 - 1) % n2) * 2 + i,
        )

    def logs(r, j):
        return allm_ref[r, :, lanes(i * half + j * size, size)]

    def gather_first(j, _):
        sib_copy(j).wait_recv()
        mine = state_ref[:, lanes(i * half + j * size, size)].astype(F32)
        theirs = sib_ref[j].astype(F32)
        d1 = jnp.exp2(logs(2 * c + 1, j))
        total = jnp.where(i == 0, d1 * mine + theirs, d1 * theirs + mine)
        incl_ref[0, j] = total.astype(BF16)
        own_ref[j] = jnp.zeros(own_ref.shape[1:], F32)

        @pl.when(sends(0))
        def _():
            pre_copy(0, j, 0).start()

        return 0

    lax.fori_loop(0, chunks, gather_first, 0)
    fresh = bias_ref.shape[1]
    tokens = x_ref.shape[0]
    seen = iota((tokens, fresh), 1) <= me * tokens + iota((tokens, fresh), 0)
    bias_ref[...] = jnp.where(seen, 0.0, NEG)
    pairs = width // 128
    early = n2
    ahead = pairs * 3 // 4

    def pair(p, _):
        within_pair(p, x_ref, run_ref, at_ref, gram_ref, part_ref)
        return 0


    def forward(kind, d):
        src = allc_ref if kind == 0 else alln_ref
        slot = ((c + d) % n2) * 2 + i
        return remote(
            src.at[slot], src.at[slot], kv_f.at[kind, d], kv_r.at[kind, slot], other
        )

    def combine(j, _):
        for l in range(levels):

            @pl.when(c % (2 ** (l + 1)) >= 2**l)
            def _():
                pre_copy(l, j, 0).wait_recv()
                if l >= 1:

                    @pl.when(c % 2 == 1)
                    def _():
                        relay_copy(l, j).start()

                base = c - c % (2**l)
                logsum = jnp.zeros((1, size), F32)
                for back in range(1, 2**l):
                    at = (c + n2 - back) % n2
                    both = logs(2 * at, j) + logs(2 * at + 1, j)
                    logsum += jnp.where(c - back >= base, both, 0.0)
                own_ref[j] = jnp.exp2(logsum) * recv_ref[l, j].astype(F32) + own_ref[j]

            if l + 1 < levels:

                @pl.when(sends(l + 1))
                def _():
                    keep = jnp.exp2(logs(2 * c, j) + logs(2 * c + 1, j))
                    incl_ref[l + 1, j] = (
                        keep * own_ref[j] + incl_ref[0, j].astype(F32)
                    ).astype(BF16)
                    for r in targets(l + 1):
                        pre_copy(l + 1, j, r).start()

        enter = own_ref[j]
        mine = state_ref[:, lanes(i * half + j * size, size)].astype(F32)
        first = jnp.where(i == 0, mine, sib_ref[j].astype(F32))
        middle = jnp.exp2(logs(2 * c, j)) * enter + first
        out_ref[:, lanes(i * half + j * size, size)] = jnp.where(
            i == 0, enter, middle
        ).astype(BF16)
        back_ref[j] = jnp.where(i == 0, middle, enter).astype(BF16)
        back_copy(j, i).start()
        return 0

    def remote_slot(kind, d):
        src = allc_ref if kind == 0 else alln_ref
        mine = kvc_ref if kind == 0 else kvn_ref
        slot = ((c + d) % n2) * 2 + i
        return remote(mine, src.at[slot], kv_s.at[kind, d], kv_r.at[kind, slot], slot)

    def back_copy(j, who):
        return remote(
            back_ref.at[j],
            out_ref.at[:, lanes(who * half + j * size, size)],
            back_s.at[j],
            back_r.at[j],
            other,
        )

    def first_part(j, _):
        lax.fori_loop(j * ahead // early, (j + 1) * ahead // early, pair, 0)
        for d in range(1, n2):

            @pl.when(j == d)
            def _():
                remote_slot(0, d).wait_recv()
                forward(0, d).start()

                @pl.when((c + d) % n2 < c)
                def _():
                    remote_slot(1, d).wait_recv()
                    forward(1, d).start()

        return 0

    lax.fori_loop(0, early, first_part, 0)

    def other_slot(kind, d):
        src = allc_ref if kind == 0 else alln_ref
        mine = kvc_ref if kind == 0 else kvn_ref
        slot = ((c + d) % n2) * 2 + (1 - i)
        return remote(mine, src.at[slot], kv_f.at[kind, d], kv_r.at[kind, slot], other)

    for d in range(n2):
        other_slot(0, d).wait_recv()
    other_slot(1, 0).wait_recv()
    for d in range(1, n2):

        @pl.when((c + d) % n2 < c)
        def _():
            other_slot(1, d).wait_recv()

    kv_here = vc_ref.shape[0]
    for k in range(kv_here):
        at = (kv_here + k) * ATT_DIM
        for all_ref, ext_ref in ((allc_ref, vc_ref), (alln_ref, vn_ref)):
            ext_ref[k, :, :ATT_DIM] = all_ref[:, :, at : at + ATT_DIM].reshape(-1, ATT_DIM)
            ext_ref[k, :, ATT_DIM:] = jnp.ones((ext_ref.shape[1], ATT_DIM), BF16)

    q_heads = q_ref.shape[1] // ATT_DIM
    steps = q_heads // 2 if (q_heads // kv_here) % 2 == 0 else q_heads

    def head(h, _):
        attend(h, q_ref, allc_ref, alln_ref, bias_ref, vc_ref, vn_ref, att_ref)
        return 0

    def second_part(j, _):
        rest = pairs - ahead
        lax.fori_loop(
            ahead + j * rest // chunks, ahead + (j + 1) * rest // chunks, pair, 0
        )
        lax.fori_loop(j * steps // chunks, (j + 1) * steps // chunks, head, 0)
        combine(j, 0)
        return 0

    lax.fori_loop(0, chunks, second_part, 0)

    def drain(j, _):
        back_copy(j, 1 - i).wait_recv()
        back_copy(j, i).wait_send()
        sib_copy(j).wait_send()
        for l in range(levels):

            @pl.when(sends(l))
            def _():
                for r in targets(l):
                    pre_copy(l, j, r).wait_send()

            if l >= 1:

                @pl.when((c % (2 ** (l + 1)) >= 2**l) & (c % 2 == 1))
                def _():
                    relay_copy(l, j).wait_send()

        return 0

    lax.fori_loop(0, chunks, drain, 0)
    for d in range(1, n):
        remote(
            meta_ref, allm_ref.at[me], meta_s.at[d], meta_r.at[me], (me + d) % n
        ).wait_send()
    cache_copy(0, other).wait_send()
    new_copy(0, other).wait_send()
    for d in range(1, n2):
        to = ((c + d) % n2) * 2 + i
        cache_copy(d, to).wait_send()
        forward(0, d).wait_send()

        @pl.when(c + d < n2)
        def _():
            new_copy(d, to).wait_send()

        @pl.when((c + d) % n2 < c)
        def _():
            forward(1, d).wait_send()


def final_kernel(
    part_ref,
    fade_ref,
    sout_ref,
    state_ref,
    meta_ref,
    nk_ref,
    y_ref,
    code_ref,
    scale_ref,
):
    tokens, width = part_ref.shape
    heads = fade_ref.shape[1]
    per_group = min(SSM_HEADS // GROUPS, heads)
    z = lax.axis_index("head")
    group0 = z * heads // (SSM_HEADS // GROUPS)
    block = min(512, width)

    magnitude = jnp.max(meta_ref[:, 0, width:], axis=0, keepdims=True)
    scale = (magnitude + 1e-6) / 127.0
    scale_ref[...] = scale
    code_ref[...] = (nk_ref[...].astype(F32) / scale).astype(BF16)
    fade = fade_ref[...]
    for b in range(width // block):
        here = pl.ds(b * block, block)
        g = group0 + (b * block) // (per_group * HEAD_DIM)
        prior = jnp.dot(
            sout_ref[:, lanes(g * STATE, STATE)], state_ref[:, here], preferred_element_type=F32
        )
        pick = choose(heads, b * block, block).astype(BF16)
        spread = jnp.dot(fade, pick, preferred_element_type=F32)
        y_ref[:, here] = (part_ref[:, here].astype(F32) + spread * prior).astype(BF16)


def body(
    n,
    ssm_input,
    state_in,
    state_out,
    step_size,
    decay_rate,
    forget,
    skip_gain,
    queries,
    new_keys,
    new_values,
    cache_keys,
    cache_values,
    cache_key_scale,
    cache_value_scale,
):
    tokens, width = ssm_input.shape
    heads = step_size.shape[1]
    rows = cache_keys.shape[0]
    channels = new_keys.shape[1]
    q_heads = queries.shape[1] // ATT_DIM
    kv_here = max(1, q_heads // (ATT_HEADS // KV_HEADS))
    kvw = kv_here * ATT_DIM
    per_group = min(SSM_HEADS // GROUPS, heads)
    groups_here = heads // per_group
    limit = pltpu.CompilerParams(vmem_limit_bytes=60 * 1024 * 1024)
    shape = jax.ShapeDtypeStruct
    state, run, fade, at, gram, meta, kvc, kvn = pl.pallas_call(
        local_kernel,
        out_shape=(
            shape((STATE, width), BF16),
            shape((tokens + 16, 3 * heads), BF16),
            shape((tokens, heads), BF16),
            shape((heads, tokens), F32),
            shape((groups_here, tokens, tokens), F32),
            shape((1, width + channels), F32),
            shape((rows, 2 * kvw), BF16),
            shape((tokens, 2 * kvw), BF16),
        ),
        in_specs=[VMEM] * 13,
        out_specs=(VMEM,) * 8,
        compiler_params=limit,
        name="local",
    )(
        ssm_input,
        state_in,
        state_out,
        step_size.T,
        decay_rate.reshape(1, heads),
        forget.reshape(1, tokens),
        skip_gain.reshape(1, heads),
        new_keys,
        new_values,
        cache_keys,
        cache_values,
        cache_key_scale.reshape(1, channels),
        cache_value_scale.reshape(1, channels),
    )
    half = width // 2
    size = min(256, half)
    chunks = half // size
    n2 = n // 2
    levels = n2.bit_length() - 1
    fan = max(1, n2 // 2)
    dma = pltpu.SemaphoreType.DMA
    carried, allm, part, attended = pl.pallas_call(
        functools.partial(comm_kernel, n, chunks),
        out_shape=(
            shape((STATE, width), BF16),
            shape((n, 1, width + channels), F32),
            shape((tokens, width), BF16),
            shape((tokens, queries.shape[1]), BF16),
        ),
        in_specs=[VMEM] * 9,
        out_specs=(VMEM,) * 4,
        scratch_shapes=[
            pltpu.VMEM((n, rows, 2 * kvw), BF16),
            pltpu.VMEM((n, tokens, 2 * kvw), BF16),
            pltpu.VMEM((kv_here, n * rows, 2 * ATT_DIM), BF16),
            pltpu.VMEM((kv_here, n * tokens, 2 * ATT_DIM), BF16),
            pltpu.VMEM((tokens, n * tokens), F32),
            pltpu.VMEM((chunks, STATE, size), BF16),
            pltpu.VMEM((chunks, STATE, size), F32),
            pltpu.VMEM((levels, chunks, STATE, size), BF16),
            pltpu.VMEM((levels, chunks, STATE, size), BF16),
            pltpu.VMEM((chunks, STATE, size), BF16),
            dma((n,)),
            dma((n,)),
            dma((2, n2)),
            dma((2, n)),
            dma((2, n2)),
            dma((chunks,)),
            dma((chunks,)),
            dma((levels, chunks, fan)),
            dma((levels, chunks)),
            dma((levels, chunks)),
            dma((chunks,)),
            dma((chunks,)),
        ],
        compiler_params=pltpu.CompilerParams(
            collective_id=0, has_side_effects=True, vmem_limit_bytes=60 * 1024 * 1024
        ),
        name="exchange",
    )(state, kvc, kvn, meta, ssm_input, run, at, gram, queries)
    y, codes, scale = pl.pallas_call(
        final_kernel,
        out_shape=(
            shape((tokens, width), BF16),
            shape((tokens, channels), BF16),
            shape((1, channels), F32),
        ),
        in_specs=[VMEM] * 6,
        out_specs=(VMEM,) * 3,
        compiler_params=limit,
        name="finish",
    )(part, fade, state_out, carried, allm, new_keys)
    return (y, attended, codes, scale.reshape(channels))

BLOCK = 96


def span_blocks(tokens):
    return max(1, tokens // BLOCK)


def split2(value):
    high = value.astype(BF16)
    low = (value - high.astype(F32)).astype(BF16)
    return jnp.concatenate([high, low], axis=1)


def choose2(heads, begin, size):
    lane = begin + iota((2 * heads, size), 1)
    row = iota((2 * heads, size), 0)
    return (row % heads == lane // HEAD_DIM).astype(BF16)


def factor_rows(tokens):
    nb = span_blocks(tokens)
    size = tokens // nb
    places, at = {}, 0
    for name, rows in (
        [("z", tokens), ("tail", 16)]
        + [(f"z{b}", (b + 1) * size) for b in range(nb - 1)]
        + [("out", tokens), ("skip", 16), ("fade", tokens)]
    ):
        places[name] = (at, at + rows)
        at += rows
    return places, at


def with_ones(v):
    return jnp.concatenate([v, jnp.ones(v.shape, BF16)], axis=1)


NT = (((1,), (1,)), ((), ()))
FACTOR = ATT_DIM**-0.5 * LOG2E


def stream_heads(step, streams, together):
    first = step * streams * together
    return [
        [lanes((first + e * together + f) * ATT_DIM, ATT_DIM) for f in range(together)]
        for e in range(streams)
    ]


def key_columns(step, streams, together, q_ref, all_ref):
    kvw = all_ref.shape[2] // 2
    share = (q_ref.shape[1] // ATT_DIM) // (kvw // ATT_DIM)
    k = (step * streams * together) // share
    return lanes(k * ATT_DIM, ATT_DIM), lanes(kvw + k * ATT_DIM, ATT_DIM)


def score_streams(own, q_ref, keys):
    return [
        lax.dot_general(
            jnp.concatenate([q_ref[:, o] for o in heads], axis=0),
            keys,
            NT,
            preferred_element_type=F32,
        )
        for heads in own
    ]


def attend_cache(step, streams, together, q_ref, allc_ref, sum_ref, peak_ref):
    rows = together * q_ref.shape[0]
    at, av = key_columns(step, streams, together, q_ref, allc_ref)
    keys = allc_ref[:, :, at].reshape(-1, ATT_DIM)
    values = with_ones(allc_ref[:, :, av].reshape(-1, ATT_DIM))
    own = stream_heads(step, streams, together)
    scores = score_streams(own, q_ref, keys)
    for e in range(streams):
        peak = jnp.max(scores[e], axis=1, keepdims=True)
        p = jnp.exp2((scores[e] - peak) * FACTOR).astype(BF16)
        here = pl.ds(pl.multiple_of((step * streams + e) * rows, rows), rows)
        sum_ref[here, :] = jnp.dot(p, values, preferred_element_type=F32)
        peak_ref[here, :] = jnp.broadcast_to(peak, (rows, 128))


def attend_span(
    step, streams, together, chip, q_ref, alln_ref, bias_ref, sum_ref, peak_ref, att_ref
):
    tokens = q_ref.shape[0]
    rows = together * tokens
    at, av = key_columns(step, streams, together, q_ref, alln_ref)
    seen = 2 * chip + 2
    keys = alln_ref[:seen, :, at].reshape(-1, ATT_DIM)
    values = with_ones(alln_ref[:seen, :, av].reshape(-1, ATT_DIM))
    free = keys.shape[0] - 2 * tokens
    own = stream_heads(step, streams, together)
    scores = score_streams(own, q_ref, keys)
    bias = bias_ref[...]
    for e in range(streams):
        near = scores[e][:, free:].reshape(together, tokens, -1) + bias[None]
        near = near.reshape(rows, -1)
        s = jnp.concatenate([scores[e][:, :free], near], axis=1) if free else near
        here = pl.ds(pl.multiple_of((step * streams + e) * rows, rows), rows)
        before = peak_ref[here, :][:, :1]
        peak = jnp.maximum(before, jnp.max(s, axis=1, keepdims=True))
        p = jnp.exp2((s - peak) * FACTOR).astype(BF16)
        both = jnp.dot(p, values, preferred_element_type=F32)
        both += sum_ref[here, :] * jnp.exp2((before - peak) * FACTOR)
        result = (both[:, :ATT_DIM] / both[:, ATT_DIM:]).astype(BF16)
        for f, o in enumerate(own[e]):
            att_ref[:, o] = result[f * tokens : (f + 1) * tokens]


def fused_kernel(
    chunks,
    x_hbm,
    sin_hbm,
    sout_hbm,
    step_hbm,
    decay_hbm,
    forget_hbm,
    skip_hbm,
    q_hbm,
    nk_hbm,
    nv_hbm,
    ck_hbm,
    cv_hbm,
    cks_hbm,
    cvs_hbm,
    y_ref,
    att_ref,
    code_ref,
    scale_ref,
    step_ref,
    decay_ref,
    forget_ref,
    skip_ref,
    cks_ref,
    cvs_ref,
    x_ref,
    sin_ref,
    sout_ref,
    q_ref,
    nk_ref,
    nv_ref,
    ck_ref,
    cv_ref,
    kvc_ref,
    kvn_ref,
    allc_ref,
    alln_ref,
    bias_ref,
    meta_ref,
    allm_ref,
    fac_ref,
    fade_ref,
    z_ref,
    gram_ref,
    turned_ref,
    give_ref,
    sib_ref,
    mine_ref,
    full_ref,
    tx_ref,
    rx_ref,
    enter_ref,
    back_ref,
    other_ref,
    sum_ref,
    peak_ref,
    pick_ref,
    carry_ref,
    load_s,
    meta_s,
    meta_r,
    kv_s,
    kv_r,
    kv_f,
    kv_p,
    sib_s,
    sib_r,
    out_s,
    in_r,
    back_s,
    back_r,
):
    n = 8
    tokens, width = x_ref.shape
    heads = step_ref.shape[0]
    per_group = min(SSM_HEADS // GROUPS, heads)
    groups_here = heads // per_group
    channels = nk_ref.shape[1]
    kvw = kvc_ref.shape[1] // 2
    half = width // 2
    size = half // chunks
    near = chunks * 3 // 8
    mid = chunks // 2
    places, _ = factor_rows(tokens)
    nb = span_blocks(tokens)
    bs = tokens // nb

    me = lax.axis_index("seq")
    z = lax.axis_index("head")
    i, c = me % 2, me // 2
    other = me + 1 - 2 * i
    cx, cy = c + 1 - 2 * (c % 2), (c + 2) % 4
    cd = 3 - c
    group0 = z * heads // (SSM_HEADS // GROUPS)
    q_heads = heads * ATT_HEADS // SSM_HEADS
    first_kv = z * q_heads // (ATT_HEADS // KV_HEADS)
    cols = lanes(first_kv * ATT_DIM, kvw)
    gcols = lanes(group0 * STATE, groups_here * STATE)

    barrier = pltpu.get_barrier_semaphore()
    for d in range(1, n):
        pl.semaphore_signal(
            barrier, inc=1, device_id={"seq": (me + d) % n}, device_id_type=MESH
        )

    moves = dict(
        ck=(ck_hbm.at[:, cols], ck_ref),
        cks=(cks_hbm.at[:, cols], cks_ref),
        cv=(cv_hbm.at[:, cols], cv_ref),
        cvs=(cvs_hbm.at[:, cols], cvs_ref),
        nv=(nv_hbm.at[:, cols], nv_ref),
        nk=(nk_hbm, nk_ref),
        step=(step_hbm, step_ref),
        decay=(decay_hbm, decay_ref),
        forget=(forget_hbm, forget_ref),
        skip=(skip_hbm, skip_ref),
        sin=(sin_hbm.at[:, gcols], sin_ref),
        sout=(sout_hbm.at[:, gcols], sout_ref),
        x=(x_hbm, x_ref),
        q=(q_hbm, q_ref),
    )
    loads = {
        name: pltpu.make_async_copy(src, dst, load_s.at[k])
        for k, (name, (src, dst)) in enumerate(moves.items())
    }
    for copy in loads.values():
        copy.start()

    def ready(*names):
        for name in names:
            loads[name].wait()

    def remote(src, dst, ssem, rsem, to):
        return pltpu.make_async_remote_copy(
            src_ref=src,
            dst_ref=dst,
            send_sem=ssem,
            recv_sem=rsem,
            device_id={"seq": to},
            device_id_type=MESH,
        )

    def dev(chip):
        return chip * 2 + i

    alls = (allc_ref, alln_ref)
    owns = (kvc_ref, kvn_ref)

    def own_copy(kind, way):
        to = (other, dev(cx), dev(cy))[way]
        return remote(
            owns[kind], alls[kind].at[me], kv_s.at[kind, way], kv_r.at[kind, me], to
        )

    def pass_copy(kind, way, chip, to):
        slot = dev(chip)
        return remote(
            alls[kind].at[slot],
            alls[kind].at[slot],
            kv_p.at[kind, way],
            kv_r.at[kind, slot],
            dev(to),
        )

    def forward(kind, chip):
        slot = dev(chip)
        return remote(
            alls[kind].at[slot],
            alls[kind].at[slot],
            kv_f.at[kind, chip],
            kv_r.at[kind, slot],
            other,
        )

    def arrived(kind, slot):
        remote(
            owns[kind], alls[kind].at[slot], kv_s.at[kind, 0], kv_r.at[kind, slot], other
        ).wait_recv()

    for k in range(width // 512):
        pick_ref[:, k * 512 : (k + 1) * 512] = choose2(heads, k * 512, 512)
    ready("ck", "cks", "cv", "cvs")
    kvc_ref[:, :kvw] = (ck_ref[...].astype(F32) * cks_ref[...]).astype(BF16)
    kvc_ref[:, kvw:] = (cv_ref[...].astype(F32) * cvs_ref[...]).astype(BF16)
    pl.semaphore_wait(barrier, n - 1)
    for way in (1, 2, 0):
        own_copy(0, way).start()
    ready("nv", "nk")
    kvn_ref[:, :kvw] = nk_ref[:, cols]
    kvn_ref[:, kvw:] = nv_ref[...]

    @pl.when(cx > c)
    def _():
        own_copy(1, 1).start()

    @pl.when(cy > c)
    def _():
        own_copy(1, 2).start()

    own_copy(1, 0).start()

    row, col = iota((tokens, tokens), 0), iota((tokens, tokens), 1)
    lower = jnp.where(col <= row, 1.0, 0.0)
    eye = jnp.where(col == row, 1.0, 0.0).astype(BF16)
    ready("step", "decay", "forget", "skip")
    step = step_ref[...].T
    forgotten = jnp.sum(lower * forget_ref[...], axis=1, keepdims=True)
    decayed = jnp.dot(
        lower, decay_ref[...] * step, precision=HIGHEST, preferred_element_type=F32
    )
    running = -(decayed + forgotten) * LOG2E
    start = running - jnp.log2(step)
    last = running[tokens - 1 : tokens]
    middles = [running[b * bs + bs // 2 - 1 : b * bs + bs // 2] for b in range(nb)]

    meta_ref[:, :channels] = jnp.max(jnp.abs(nk_ref[...].astype(F32)), axis=0, keepdims=True)
    meta_ref[:, channels:] = jnp.concatenate([last, jnp.zeros((1, 128 - heads), F32)], axis=1)

    def meta_copy(d):
        return remote(
            meta_ref, allm_ref.at[me], meta_s.at[d], meta_r.at[me], (me + d) % n
        )

    def meta_arrived(r):
        remote(meta_ref, allm_ref.at[r], meta_s.at[1], meta_r.at[r], r).wait_recv()

    for d in range(1, n):
        meta_copy(d).start()
    allm_ref[me] = meta_ref[...]

    def put(name, value):
        begin, end = places[name]
        fac_ref[begin:end] = split2(jnp.broadcast_to(value, (end - begin, heads)))

    put("z", jnp.exp2(middles[nb - 1] - start))
    put("tail", jnp.exp2(last - middles[nb - 1]))
    for b in range(nb - 1):
        put(f"z{b}", jnp.exp2(middles[b] - start[: (b + 1) * bs]))
    put(
        "out",
        jnp.concatenate(
            [jnp.exp2(running[b * bs : (b + 1) * bs] - middles[b]) for b in range(nb)], axis=0
        ),
    )
    put("skip", skip_ref[...])
    put("fade", jnp.exp2(running))
    ready("sin", "sout")
    for g in range(groups_here):
        gc = slice(g * STATE, (g + 1) * STATE)
        maps_in = sin_ref[:, gc]
        gram = lax.dot_general(
            sout_ref[:, gc], maps_in, (((1,), (1,)), ((), ())), preferred_element_type=F32
        )
        gram_ref[g] = jnp.where(col <= row, gram, 0.0).astype(BF16)
        turned_ref[g] = lax.dot_general(
            maps_in, eye, (((0,), (0,)), ((), ())), preferred_element_type=F32
        ).astype(BF16)
    ready("x")

    def spread(first, final, begin, wide=size):
        rows = fac_ref[places[first][0] : places[final][1]]
        return jnp.dot(rows, pick_ref[:, lanes(begin, wide)], preferred_element_type=F32)

    def local_state(begin):
        here = lanes(begin, 2 * size)
        by = spread("z", "tail", begin, 2 * size)
        scaled = (x_ref[:, here].astype(F32) * by[:tokens]).astype(BF16)
        z_ref[:, here] = scaled
        sums = jnp.dot(
            turned_ref[begin // (per_group * HEAD_DIM)], scaled, preferred_element_type=F32
        )
        sums = (sums * by[tokens : tokens + 1]).astype(BF16)
        return sums[:, :size], sums[:, size:]

    def sib_copy(j):
        return remote(give_ref.at[j], sib_ref.at[j], sib_s.at[j], sib_r.at[j], other)

    shift = (c % 2) * (1 - c // 2) * mid

    def give(s, _):
        j = (2 * s + shift) % chunks
        for e, state in enumerate(local_state((1 - i) * half + j * size)):
            give_ref[j + e] = state
            sib_copy(j + e).start()
        return 0

    def pass_cache():
        arrived(0, dev(cx))

        @pl.when(c >= 1)
        def _():
            pass_copy(0, 0, cx, cy).start()

        forward(0, cx).start()
        arrived(0, dev(cy))

        @pl.when(c == 3)
        def _():
            pass_copy(0, 1, cy, cx).start()

        forward(0, cy).start()

    lax.fori_loop(0, chunks // 2, give, 0)
    pass_cache()
    meta_arrived(other)

    def logs_of(r):
        return allm_ref[r, :, channels : channels + heads]

    def set_fades(third):
        logs = jnp.concatenate(
            [logs_of(2 * c), logs_of(2 * c + 1), third, jnp.zeros((13, heads), F32)], axis=0
        )
        fade_ref[...] = split2(jnp.exp2(logs))

    def fades(j):
        return jnp.dot(
            fade_ref[...],
            pick_ref[:, lanes(i * half + j * size, size)],
            preferred_element_type=F32,
        )

    set_fades(jnp.zeros((1, heads), F32))

    def full_copy(j):
        slot = jnp.where(c == 0, 0, 1)
        return remote(
            full_ref.at[j], rx_ref.at[slot, j], out_s.at[0, j], in_r.at[slot, j], dev(cx)
        )

    def full_sent(j):
        return (c == 0) | ((c == 1) & (j >= near)) | ((c == 2) & (j < near))

    def own(s, _):
        j = (2 * s + shift) % chunks
        states = local_state(i * half + j * size)
        for e, mine in enumerate(states):
            mine_ref[j + e] = mine
        for e in range(2):
            sib_copy(j + e).wait_recv()
        for e, mine in enumerate(states):
            mine, theirs = mine.astype(F32), sib_ref[j + e].astype(F32)
            d1 = fades(j + e)[1:2]
            full = jnp.where(i == 0, d1 * mine + theirs, d1 * theirs + mine)
            full_ref[j + e] = full.astype(BF16)

        for e in range(2):

            @pl.when(full_sent(j + e))
            def _():
                full_copy(j + e).start()

        return 0

    lax.fori_loop(0, chunks // 2, own, 0)
    bias_ref[...] = jnp.where(
        iota((tokens, 2 * tokens), 1) <= i * tokens + iota((tokens, 2 * tokens), 0), 0.0, NEG
    )

    def within(s, _):
        begin = s * 2 * size
        here = lanes(begin, 2 * size)
        by = spread("z0" if nb > 1 else "out", "skip", begin, 2 * size)
        at = 0
        gram = gram_ref[begin // (per_group * HEAD_DIM)]
        x = x_ref[:, here].astype(F32)
        parts = []
        for b in range(nb):
            high = (b + 1) * bs
            if b + 1 < nb:
                scaled = (x[:high] * by[at : at + high]).astype(BF16)
                at += high
            else:
                scaled = z_ref[:, here]
            parts.append(
                jnp.dot(gram[b * bs : high, :high], scaled, preferred_element_type=F32)
            )
        y = by[at : at + tokens] * jnp.concatenate(parts, axis=0)
        y_ref[:, here] = (y + by[at + tokens : at + tokens + 1] * x).astype(BF16)
        return 0

    @pl.when(cx < c)
    def _():
        arrived(1, dev(cx))

        @pl.when(c == 1)
        def _():
            pass_copy(1, 0, cx, cy).start()

        forward(1, cx).start()

    @pl.when(cy < c)
    def _():
        arrived(1, dev(cy))

        @pl.when(c == 3)
        def _():
            pass_copy(1, 1, cy, cx).start()

        forward(1, cy).start()

    lax.fori_loop(0, chunks // 2, within, 0)
    arrived(0, dev(cd))
    forward(0, cd).start()
    lax.fori_loop(chunks // 2, chunks, within, 0)

    for d in range(1, n):
        r = (me + d) % n

        @pl.when(r != other)
        def _():
            meta_arrived(r)

    chip = jnp.where(c == 0, 1, jnp.where(c == 3, 2, c))
    set_fades(logs_of(2 * chip) + logs_of(2 * chip + 1))
    scale = (jnp.max(allm_ref[:, 0, :channels], axis=0, keepdims=True) + 1e-6) / 127.0
    scale_ref[...] = scale
    code_ref[...] = (nk_ref[...].astype(F32) / scale).astype(BF16)

    allc_ref[me] = kvc_ref[...]
    alln_ref[me] = kvn_ref[...]
    arrived(0, other)
    for d in range(1, 4):
        arrived(0, (c + d) % 4 * 2 + 1 - i)

    ready("q")

    def span_arrived():
        @pl.when(cd < c)
        def _():
            arrived(1, dev(cd))
            forward(1, cd).start()

        arrived(1, other)
        for d in range(1, 4):
            there = (c + d) % 4

            @pl.when(there < c)
            def _():
                arrived(1, there * 2 + 1 - i)

    def second_way(s):
        late = s // mid
        return mid + s - late * (2 * mid - near)

    def order(s):
        later = s // (chunks - near)
        even = (1 - later) * second_way(s * (1 - later)) + later * (s - chunks + near)
        last = (s + chunks - near) // chunks
        odd = (1 - last) * s + last * second_way((s - near) * last)
        third = c // 2
        return (1 - c % 2) * even + (c % 2) * (third * odd + (1 - third) * s)

    def prior(begin, carried):
        here = lanes(begin, size)
        group = begin // (per_group * HEAD_DIM)
        term = jnp.dot(sout_ref[:, lanes(group * STATE, STATE)], carried, preferred_element_type=F32)
        by = spread("fade", "fade", begin)
        return begin, (y_ref[:, here].astype(F32) + by * term).astype(BF16)

    def put_prior(result):
        begin, value = result
        y_ref[:, lanes(begin, size)] = value

    def rx_wait(slot, j):
        remote(
            full_ref.at[j], rx_ref.at[slot, j], out_s.at[0, j], in_r.at[slot, j], dev(cx)
        ).wait_recv()

    def tx_copy(j, chip):
        return remote(tx_ref.at[j], rx_ref.at[0, j], out_s.at[1, j], in_r.at[0, j], dev(chip))

    def relay_copy(j):
        return remote(
            rx_ref.at[0, j], rx_ref.at[0, j], out_s.at[2, j], in_r.at[0, j], dev(cx)
        )

    def back_copy(j):
        return remote(back_ref.at[j], other_ref.at[j], back_s.at[j], back_r.at[j], other)

    def pass_on(s):
        @pl.when((c == 1) | (c == 2))
        def _():
            j = (c % 2) * s + (1 - c % 2) * second_way(s)
            rx_wait(0, j)
            keep = fades(j)[2:3]
            tx_ref[j] = (keep * rx_ref[0, j].astype(F32) + full_ref[j].astype(F32)).astype(BF16)
            tx_copy(j, 3).start()

        @pl.when(c == 0)
        def _():
            j = second_way(s)
            rx_wait(1, j)
            keep = fades(j)[2:3]
            tx_ref[j] = (keep * full_ref[j].astype(F32) + rx_ref[1, j].astype(F32)).astype(BF16)
            tx_copy(j, 2).start()

        @pl.when(c == 3)
        def _():
            rx_wait(0, s)
            relay_copy(s).start()

    base = 2 + (c // 2) * (4 + c % 2)
    stride = 1 + (c % 2) * (1 - c // 2)
    passes = (c % 2) * near + (1 - c % 2) * (chunks - near)

    def pass_at(place):
        ahead = place - base
        s = ahead // stride

        @pl.when((ahead >= 0) & (ahead % stride == 0) & (s < passes))
        def _():
            pass_on(s)

    def settle(s):
        j = order(s)
        by = fades(j)
        d0, keep = by[0:1], by[2:3]

        @pl.when((c > 0) & (s >= passes))
        def _():
            rx_wait(0, j)

        @pl.when((c == 3) & (s < near))
        def _():
            rx_wait(1, j)
            enter_ref[...] = keep * rx_ref[0, j].astype(F32) + rx_ref[1, j].astype(F32)

        @pl.when(c == 0)
        def _():
            enter_ref[...] = jnp.zeros(enter_ref.shape, F32)

        @pl.when((c == 1) | (c == 2) | ((c == 3) & (s >= near)))
        def _():
            enter_ref[...] = rx_ref[0, j].astype(F32)

        enter = enter_ref[...]
        first = jnp.where(i == 0, mine_ref[j].astype(F32), sib_ref[j].astype(F32))
        middle = d0 * enter + first
        back_ref[j] = jnp.where(i == 0, middle, enter).astype(BF16)
        back_copy(j).start()
        carry_ref[...] = jnp.where(i == 0, enter, middle).astype(BF16)

    def slot(s, _):
        settle(s)

        @pl.when(s == 0)
        def _():
            put_prior(prior(i * half + order(s) * size, carry_ref[...]))

        @pl.when(s > 0)
        def _():
            far = order(s - 1)
            back_copy(far).wait_recv()
            both = [
                prior(i * half + order(s) * size, carry_ref[...]),
                prior((1 - i) * half + far * size, other_ref[far]),
            ]
            for each in both:
                put_prior(each)

        return 0

    streams, together = 4, 1
    steps = q_heads // (streams * together)
    pass_at(2)

    def first_part(h, _):
        attend_cache(h, streams, together, q_ref, allc_ref, sum_ref, peak_ref)
        pass_at(3 + h)
        return 0

    lax.fori_loop(0, steps, first_part, 0)
    span_arrived()

    def second_part(h, _):
        for chip in range(n // 2):

            @pl.when(c == chip)
            def _():
                attend_span(
                    h,
                    streams,
                    together,
                    chip,
                    q_ref,
                    alln_ref,
                    bias_ref,
                    sum_ref,
                    peak_ref,
                    att_ref,
                )

        pass_at(3 + steps + h)
        return slot(h, 0)

    lax.fori_loop(0, steps, second_part, 0)
    lax.fori_loop(steps, chunks, slot, 0)
    far = order(chunks - 1)
    back_copy(far).wait_recv()
    put_prior(prior((1 - i) * half + far * size, other_ref[far]))

    def drain(j, _):
        back_copy(j).wait_send()
        sib_copy(j).wait_send()

        @pl.when(full_sent(j))
        def _():
            full_copy(j).wait_send()

        @pl.when(((c == 1) & (j < near)) | ((c == 2) & (j >= near)))
        def _():
            tx_copy(j, 3).wait_send()

        @pl.when((c == 0) & (j >= near))
        def _():
            tx_copy(j, 2).wait_send()

        @pl.when((c == 3) & (j < near))
        def _():
            relay_copy(j).wait_send()

        return 0

    lax.fori_loop(0, chunks, drain, 0)
    for d in range(1, n):
        meta_copy(d).wait_send()
    for way in (1, 2, 0):
        own_copy(0, way).wait_send()
    own_copy(1, 0).wait_send()

    @pl.when(cx > c)
    def _():
        own_copy(1, 1).wait_send()

    @pl.when(cy > c)
    def _():
        own_copy(1, 2).wait_send()

    @pl.when(c >= 1)
    def _():
        pass_copy(0, 0, cx, cy).wait_send()

    @pl.when(c == 3)
    def _():
        pass_copy(0, 1, cy, cx).wait_send()
        pass_copy(1, 1, cy, cx).wait_send()

    @pl.when(c == 1)
    def _():
        pass_copy(1, 0, cx, cy).wait_send()

    for chip_ in (cx, cy, cd):
        forward(0, chip_).wait_send()

        @pl.when(chip_ < c)
        def _():
            forward(1, chip_).wait_send()


def finish_kernel(*refs):
    count = (len(refs) - 1) // 2
    copies = [
        pltpu.make_async_copy(refs[k], refs[count + k], refs[-1].at[k]) for k in range(count)
    ]
    for copy in copies:
        copy.start()
    for copy in copies:
        copy.wait()


def fused_body(
    ssm_input,
    state_in,
    state_out,
    step_size,
    decay_rate,
    forget,
    skip_gain,
    queries,
    new_keys,
    new_values,
    cache_keys,
    cache_values,
    cache_key_scale,
    cache_value_scale,
):
    n = 8
    tokens, width = ssm_input.shape
    heads = step_size.shape[1]
    rows = cache_keys.shape[0]
    channels = new_keys.shape[1]
    q_width = queries.shape[1]
    kv_here = max(1, q_width // ATT_DIM // (ATT_HEADS // KV_HEADS))
    kvw = kv_here * ATT_DIM
    groups_here = heads // min(SSM_HEADS // GROUPS, heads)
    half = width // 2
    size = min(256, half)
    chunks = half // size
    _, fac = factor_rows(tokens)
    shape = jax.ShapeDtypeStruct
    dma = pltpu.SemaphoreType.DMA
    any_ = pl.BlockSpec(memory_space=pl.ANY)
    piece = pltpu.VMEM((chunks, STATE, size), BF16)
    results = pl.pallas_call(
        functools.partial(fused_kernel, chunks),
        out_shape=(
            pltpu.VMEM((tokens, width), BF16),
            pltpu.VMEM((tokens, q_width), BF16),
            pltpu.VMEM((tokens, channels), BF16),
            pltpu.VMEM((1, channels), F32),
        ),
        in_specs=[any_] * 14,
        out_specs=(VMEM,) * 4,
        scratch_shapes=[
            pltpu.VMEM((heads, tokens), F32),
            pltpu.VMEM((1, heads), F32),
            pltpu.VMEM((1, tokens), F32),
            pltpu.VMEM((1, heads), F32),
            pltpu.VMEM((1, kvw), F32),
            pltpu.VMEM((1, kvw), F32),
            pltpu.VMEM((tokens, width), BF16),
            pltpu.VMEM((tokens, groups_here * STATE), BF16),
            pltpu.VMEM((tokens, groups_here * STATE), BF16),
            pltpu.VMEM((tokens, q_width), BF16),
            pltpu.VMEM((tokens, channels), BF16),
            pltpu.VMEM((tokens, kvw), BF16),
            pltpu.VMEM((rows, kvw), BF16),
            pltpu.VMEM((rows, kvw), BF16),
            pltpu.VMEM((rows, 2 * kvw), BF16),
            pltpu.VMEM((tokens, 2 * kvw), BF16),
            pltpu.VMEM((n, rows, 2 * kvw), BF16),
            pltpu.VMEM((n, tokens, 2 * kvw), BF16),
            pltpu.VMEM((tokens, 2 * tokens), F32),
            pltpu.VMEM((1, channels + 128), F32),
            pltpu.VMEM((n, 1, channels + 128), F32),
            pltpu.VMEM((fac, 2 * heads), BF16),
            pltpu.VMEM((16, 2 * heads), BF16),
            pltpu.VMEM((tokens, width), BF16),
            pltpu.VMEM((groups_here, tokens, tokens), BF16),
            pltpu.VMEM((groups_here, STATE, tokens), BF16),
            piece,
            piece,
            piece,
            piece,
            piece,
            pltpu.VMEM((2, chunks, STATE, size), BF16),
            pltpu.VMEM((STATE, size), F32),
            piece,
            piece,
            pltpu.VMEM((q_width // ATT_DIM * tokens, 2 * ATT_DIM), F32),
            pltpu.VMEM((q_width // ATT_DIM * tokens, 128), F32),
            pltpu.VMEM((2 * heads, width), BF16),
            pltpu.VMEM((STATE, size), BF16),
            dma((14,)),
            dma((n,)),
            dma((n,)),
            dma((2, 3)),
            dma((2, n)),
            dma((2, 4)),
            dma((2, 2)),
            dma((chunks,)),
            dma((chunks,)),
            dma((3, chunks)),
            dma((2, chunks)),
            dma((chunks,)),
            dma((chunks,)),
        ],
        compiler_params=pltpu.CompilerParams(
            collective_id=0, has_side_effects=True, vmem_limit_bytes=612 * 1024 * 1024 // 10
        ),
        name="fused",
    )(
        ssm_input,
        state_in,
        state_out,
        step_size.T,
        decay_rate.reshape(1, heads),
        forget.reshape(1, tokens),
        skip_gain.reshape(1, heads),
        queries,
        new_keys,
        new_values,
        cache_keys,
        cache_values,
        cache_key_scale.reshape(1, channels),
        cache_value_scale.reshape(1, channels),
    )
    y, attended, codes, scale = pl.pallas_call(
        finish_kernel,
        out_shape=(
            shape((tokens, width), BF16),
            shape((tokens, q_width), BF16),
            shape((tokens, channels), BF16),
            shape((1, channels), F32),
        ),
        in_specs=[VMEM] * 4,
        out_specs=(any_,) * 4,
        scratch_shapes=[dma((4,))],
        compiler_params=pltpu.CompilerParams(vmem_limit_bytes=4 * 1024 * 1024),
        name="finish",
    )(*results)
    return (y, attended, codes, scale.reshape(channels))


def fits_fused(mesh):
    heads = SSM_HEADS // mesh.shape["head"]
    return mesh.shape["seq"] == 8 and heads == 64


def solution(mesh):
    in_specs = (
        P("seq", "head"),
        P("seq", None),
        P("seq", None),
        P("seq", "head"),
        P("head"),
        P("seq"),
        P("head"),
        P("seq", "head"),
        P("seq", None),
        P("seq", None),
        P("seq", None),
        P("seq", None),
        P(),
        P(),
    )
    out_specs = (P("seq", "head"), P("seq", "head"), P("seq", None), P())
    general = functools.partial(body, mesh.shape["seq"])
    return jax.shard_map(
        fused_body if fits_fused(mesh) else general,
        mesh=mesh,
        in_specs=in_specs,
        out_specs=out_specs,
        check_vma=False,
    )
```

```python
import functools
import jax
import jax.numpy as jnp
from jax import lax
from jax.experimental import pallas as pl
from jax.experimental.pallas import tpu as pltpu
from jax.sharding import PartitionSpec as P

SSM_HEADS = 256
HEAD_DIM = 64
STATE = 256
GROUPS = 8
ATT_HEADS = 64
KV_HEADS = 8
ATT_DIM = 128

NEG = -1e30
LOG2E = 1.4426950408889634
HIGHEST = lax.Precision.HIGHEST
MESH = pl.DeviceIdType.MESH
VMEM = pl.BlockSpec(memory_space=pltpu.VMEM)
F32 = jnp.float32
BF16 = jnp.bfloat16


def iota(shape, axis):
    return lax.broadcasted_iota(jnp.int32, shape, axis)


def lanes(start, size):
    return pl.ds(pl.multiple_of(start, 128), size)


def local_kernel(
    x_ref,
    sin_ref,
    sout_ref,
    step_ref,
    decay_ref,
    forget_ref,
    skip_ref,
    nk_ref,
    nv_ref,
    ck_ref,
    cv_ref,
    cks_ref,
    cvs_ref,
    state_ref,
    run_ref,
    fade_ref,
    at_ref,
    gram_ref,
    meta_ref,
    kvc_ref,
    kvn_ref,
):
    tokens, width = x_ref.shape
    heads = step_ref.shape[0]
    per_group = min(SSM_HEADS // GROUPS, heads)
    groups_here = heads // per_group
    z = lax.axis_index("head")
    group0 = z * heads // (SSM_HEADS // GROUPS)
    kvw = kvc_ref.shape[1] // 2
    q_heads = heads * ATT_HEADS // SSM_HEADS
    first = z * q_heads // (ATT_HEADS // KV_HEADS)
    cols = lanes(first * ATT_DIM, kvw)
    kvc_ref[:, :kvw] = (ck_ref[:, cols].astype(F32) * cks_ref[:, cols]).astype(BF16)
    kvc_ref[:, kvw:] = (cv_ref[:, cols].astype(F32) * cvs_ref[:, cols]).astype(BF16)
    kvn_ref[:, :kvw] = nk_ref[:, cols]
    kvn_ref[:, kvw:] = nv_ref[:, cols]
    meta_ref[:, width:] = jnp.max(jnp.abs(nk_ref[...].astype(F32)), axis=0, keepdims=True)

    row, col = iota((tokens, tokens), 0), iota((tokens, tokens), 1)
    lower = jnp.where(col <= row, 1.0, 0.0)
    eye = jnp.where(col == row, 1.0, 0.0)
    step = step_ref[...].T
    forgotten = jnp.sum(lower * forget_ref[...], axis=1, keepdims=True)
    decayed = jnp.dot(
        lower, decay_ref[...] * step, precision=HIGHEST, preferred_element_type=F32
    )
    running = -(decayed + forgotten) * LOG2E
    start = running - jnp.log2(step)
    at_ref[...] = start.T
    rest = jnp.concatenate(
        [running, jnp.broadcast_to(skip_ref[...], (16, heads))], axis=0
    )
    for third in range(3):
        piece = rest.astype(BF16)
        run_ref[:, third * heads : (third + 1) * heads] = piece
        rest = rest - piece.astype(F32)
    fade_ref[...] = jnp.exp2(running).astype(BF16)
    tail = jnp.exp2(running[tokens - 1 : tokens] - start).astype(BF16)
    last = running[tokens - 8 : tokens]
    block = min(512, width)
    for g in range(groups_here):
        gcols = lanes((group0 + g) * STATE, STATE)
        maps_in = sin_ref[:, gcols]
        gram_ref[g] = lax.dot_general(
            sout_ref[:, gcols], maps_in, (((1,), (1,)), ((), ())), preferred_element_type=F32
        )
        turned = lax.dot_general(
            maps_in,
            eye.astype(BF16),
            (((0,), (0,)), ((), ())),
            preferred_element_type=F32,
        ).astype(BF16)
        for b in range(per_group * HEAD_DIM // block):
            begin = g * per_group * HEAD_DIM + b * block
            here = pl.ds(begin, block)
            pick = choose(heads, begin, block)
            meta_ref[:, here] = jnp.dot(
                last, pick, precision=HIGHEST, preferred_element_type=F32
            )[7:8]
            scale = jnp.dot(tail, pick.astype(BF16), preferred_element_type=F32)
            scaled = (x_ref[:, here].astype(F32) * scale).astype(BF16)
            state_ref[:, here] = jnp.dot(
                turned, scaled, preferred_element_type=F32
            ).astype(BF16)


def choose(heads, begin, size):
    lane = begin + iota((heads, size), 1)
    return (iota((heads, size), 0) == lane // HEAD_DIM).astype(F32)


def within_pair(p, x_ref, run_ref, at_ref, gram_ref, part_ref):
    tokens = x_ref.shape[0]
    heads = run_ref.shape[1] // 3
    per_group = min(SSM_HEADS // GROUPS, heads)
    here = lanes(p * 128, 128)
    pick = choose(heads, p * 128, 128).astype(BF16)
    both = jnp.dot(
        run_ref[...], jnp.concatenate([pick] * 3, axis=0), preferred_element_type=F32
    )
    run, skip = both[:tokens], both[tokens : tokens + 1]
    x = x_ref[:, here]
    gram = gram_ref[(2 * p) // per_group]
    causal = iota((tokens, tokens), 1) <= iota((tokens, tokens), 0)

    def one(k):
        spread = run[:, k * HEAD_DIM : k * HEAD_DIM + 1] - at_ref[pl.ds(2 * p + k, 1), :]
        return (jnp.exp2(jnp.where(causal, spread, NEG)) * gram).astype(BF16)

    pair = jnp.dot(
        jnp.concatenate([one(0), one(1)], axis=0), x, preferred_element_type=F32
    )
    y = jnp.where(iota((tokens, 128), 1) < HEAD_DIM, pair[:tokens], pair[tokens:])
    part_ref[:, here] = (y + skip * x.astype(F32)).astype(BF16)


def attend(h, q_ref, allc_ref, alln_ref, bias_ref, vc_ref, vn_ref, att_ref):
    q_heads = q_ref.shape[1] // ATT_DIM
    kv_here = vc_ref.shape[0]
    share = q_heads // kv_here
    together = 2 if share % 2 == 0 else 1
    tokens = q_ref.shape[0]
    k = (h * together) // share
    factor = ATT_DIM**-0.5 * LOG2E
    nt = (((1,), (1,)), ((), ()))
    own = [lanes((h * together + e) * ATT_DIM, ATT_DIM) for e in range(together)]
    q = jnp.concatenate([q_ref[:, o] for o in own], axis=0)
    at = lanes(k * ATT_DIM, ATT_DIM)
    keys_c = allc_ref[:, :, at].reshape(-1, ATT_DIM)
    keys_n = alln_ref[:, :, at].reshape(-1, ATT_DIM)
    old = lax.dot_general(q, keys_c, nt, preferred_element_type=F32)
    new = lax.dot_general(q, keys_n, nt, preferred_element_type=F32)
    bias = bias_ref[...]
    new = (new.reshape(together, tokens, -1) + bias[None]).reshape(together * tokens, -1)
    peak = jnp.maximum(
        jnp.max(old, axis=1, keepdims=True), jnp.max(new, axis=1, keepdims=True)
    )
    old = jnp.exp2((old - peak) * factor).astype(BF16)
    new = jnp.exp2((new - peak) * factor).astype(BF16)
    both = jnp.dot(old, vc_ref[k], preferred_element_type=F32) + jnp.dot(
        new, vn_ref[k], preferred_element_type=F32
    )
    result = (both[:, :ATT_DIM] / both[:, ATT_DIM:]).astype(BF16)
    for e in range(together):
        att_ref[:, own[e]] = result[e * tokens : (e + 1) * tokens]


def comm_kernel(
    n,
    chunks,
    state_ref,
    kvc_ref,
    kvn_ref,
    meta_ref,
    x_ref,
    run_ref,
    at_ref,
    gram_ref,
    q_ref,
    out_ref,
    allm_ref,
    part_ref,
    att_ref,
    allc_ref,
    alln_ref,
    vc_ref,
    vn_ref,
    bias_ref,
    sib_ref,
    own_ref,
    incl_ref,
    recv_ref,
    back_ref,
    meta_s,
    meta_r,
    kv_s,
    kv_r,
    kv_f,
    sib_s,
    sib_r,
    pre_s,
    pre_r,
    rel_s,
    back_s,
    back_r,
):
    n2 = n // 2
    levels = n2.bit_length() - 1
    me = lax.axis_index("seq")
    i, c = me % 2, me // 2
    other = me + 1 - 2 * i
    width = state_ref.shape[1]
    half = width // 2
    size = half // chunks

    barrier = pltpu.get_barrier_semaphore()
    for d in range(1, n):
        pl.semaphore_signal(
            barrier, inc=1, device_id={"seq": (me + d) % n}, device_id_type=MESH
        )
    pl.semaphore_wait(barrier, n - 1)

    def remote(src, dst, ssem, rsem, to):
        return pltpu.make_async_remote_copy(
            src_ref=src,
            dst_ref=dst,
            send_sem=ssem,
            recv_sem=rsem,
            device_id={"seq": to},
            device_id_type=MESH,
        )

    def sib_copy(j):
        return remote(
            state_ref.at[:, lanes((1 - i) * half + j * size, size)],
            sib_ref.at[j],
            sib_s.at[j],
            sib_r.at[j],
            other,
        )

    for j in range(chunks):
        sib_copy(j).start()
    for d in range(1, n):
        remote(
            meta_ref, allm_ref.at[me], meta_s.at[d], meta_r.at[me], (me + d) % n
        ).start()

    def cache_copy(d, to):
        return remote(kvc_ref, allc_ref.at[me], kv_s.at[0, d], kv_r.at[0, me], to)

    def new_copy(d, to):
        return remote(kvn_ref, alln_ref.at[me], kv_s.at[1, d], kv_r.at[1, me], to)

    cache_copy(0, other).start()
    new_copy(0, other).start()
    for d in range(1, n2):
        to = ((c + d) % n2) * 2 + i
        cache_copy(d, to).start()

        @pl.when(c + d < n2)
        def _():
            new_copy(d, to).start()

    allm_ref[me] = meta_ref[...]
    allc_ref[me] = kvc_ref[...]
    alln_ref[me] = kvn_ref[...]
    for d in range(1, n2):
        later = c + d

        @pl.when(later < n2)
        def _():
            for k in range(2):
                alln_ref[later * 2 + k] = jnp.zeros(kvn_ref.shape, BF16)

    for d in range(1, n):
        r = (me + d) % n
        remote(meta_ref, allm_ref.at[r], meta_s.at[d], meta_r.at[r], r).wait_recv()

    def sends(l):
        return c % (2 ** (l + 1)) == 2**l - 1

    def targets(l):
        return [0] if l == 0 else list(range(1, 2**l, 2))

    def pre_copy(l, j, r):
        return remote(
            incl_ref.at[l, j],
            recv_ref.at[l, j],
            pre_s.at[l, j, r],
            pre_r.at[l, j],
            ((c + 1 + r) % n2) * 2 + i,
        )

    def relay_copy(l, j):
        return remote(
            recv_ref.at[l, j],
            recv_ref.at[l, j],
            rel_s.at[l, j],
            pre_r.at[l, j],
            ((c + n2 - 1) % n2) * 2 + i,
        )

    def logs(r, j):
        return allm_ref[r, :, lanes(i * half + j * size, size)]

    def gather_first(j, _):
        sib_copy(j).wait_recv()
        mine = state_ref[:, lanes(i * half + j * size, size)].astype(F32)
        theirs = sib_ref[j].astype(F32)
        d1 = jnp.exp2(logs(2 * c + 1, j))
        total = jnp.where(i == 0, d1 * mine + theirs, d1 * theirs + mine)
        incl_ref[0, j] = total.astype(BF16)
        own_ref[j] = jnp.zeros(own_ref.shape[1:], F32)

        @pl.when(sends(0))
        def _():
            pre_copy(0, j, 0).start()

        return 0

    lax.fori_loop(0, chunks, gather_first, 0)
    fresh = bias_ref.shape[1]
    tokens = x_ref.shape[0]
    seen = iota((tokens, fresh), 1) <= me * tokens + iota((tokens, fresh), 0)
    bias_ref[...] = jnp.where(seen, 0.0, NEG)
    pairs = width // 128
    early = n2
    ahead = pairs * 3 // 4

    def pair(p, _):
        within_pair(p, x_ref, run_ref, at_ref, gram_ref, part_ref)
        return 0


    def forward(kind, d):
        src = allc_ref if kind == 0 else alln_ref
        slot = ((c + d) % n2) * 2 + i
        return remote(
            src.at[slot], src.at[slot], kv_f.at[kind, d], kv_r.at[kind, slot], other
        )

    def combine(j, _):
        for l in range(levels):

            @pl.when(c % (2 ** (l + 1)) >= 2**l)
            def _():
                pre_copy(l, j, 0).wait_recv()
                if l >= 1:

                    @pl.when(c % 2 == 1)
                    def _():
                        relay_copy(l, j).start()

                base = c - c % (2**l)
                logsum = jnp.zeros((1, size), F32)
                for back in range(1, 2**l):
                    at = (c + n2 - back) % n2
                    both = logs(2 * at, j) + logs(2 * at + 1, j)
                    logsum += jnp.where(c - back >= base, both, 0.0)
                own_ref[j] = jnp.exp2(logsum) * recv_ref[l, j].astype(F32) + own_ref[j]

            if l + 1 < levels:

                @pl.when(sends(l + 1))
                def _():
                    keep = jnp.exp2(logs(2 * c, j) + logs(2 * c + 1, j))
                    incl_ref[l + 1, j] = (
                        keep * own_ref[j] + incl_ref[0, j].astype(F32)
                    ).astype(BF16)
                    for r in targets(l + 1):
                        pre_copy(l + 1, j, r).start()

        enter = own_ref[j]
        mine = state_ref[:, lanes(i * half + j * size, size)].astype(F32)
        first = jnp.where(i == 0, mine, sib_ref[j].astype(F32))
        middle = jnp.exp2(logs(2 * c, j)) * enter + first
        out_ref[:, lanes(i * half + j * size, size)] = jnp.where(
            i == 0, enter, middle
        ).astype(BF16)
        back_ref[j] = jnp.where(i == 0, middle, enter).astype(BF16)
        back_copy(j, i).start()
        return 0

    def remote_slot(kind, d):
        src = allc_ref if kind == 0 else alln_ref
        mine = kvc_ref if kind == 0 else kvn_ref
        slot = ((c + d) % n2) * 2 + i
        return remote(mine, src.at[slot], kv_s.at[kind, d], kv_r.at[kind, slot], slot)

    def back_copy(j, who):
        return remote(
            back_ref.at[j],
            out_ref.at[:, lanes(who * half + j * size, size)],
            back_s.at[j],
            back_r.at[j],
            other,
        )

    def first_part(j, _):
        lax.fori_loop(j * ahead // early, (j + 1) * ahead // early, pair, 0)
        for d in range(1, n2):

            @pl.when(j == d)
            def _():
                remote_slot(0, d).wait_recv()
                forward(0, d).start()

                @pl.when((c + d) % n2 < c)
                def _():
                    remote_slot(1, d).wait_recv()
                    forward(1, d).start()

        return 0

    lax.fori_loop(0, early, first_part, 0)

    def other_slot(kind, d):
        src = allc_ref if kind == 0 else alln_ref
        mine = kvc_ref if kind == 0 else kvn_ref
        slot = ((c + d) % n2) * 2 + (1 - i)
        return remote(mine, src.at[slot], kv_f.at[kind, d], kv_r.at[kind, slot], other)

    for d in range(n2):
        other_slot(0, d).wait_recv()
    other_slot(1, 0).wait_recv()
    for d in range(1, n2):

        @pl.when((c + d) % n2 < c)
        def _():
            other_slot(1, d).wait_recv()

    kv_here = vc_ref.shape[0]
    for k in range(kv_here):
        at = (kv_here + k) * ATT_DIM
        for all_ref, ext_ref in ((allc_ref, vc_ref), (alln_ref, vn_ref)):
            ext_ref[k, :, :ATT_DIM] = all_ref[:, :, at : at + ATT_DIM].reshape(-1, ATT_DIM)
            ext_ref[k, :, ATT_DIM:] = jnp.ones((ext_ref.shape[1], ATT_DIM), BF16)

    q_heads = q_ref.shape[1] // ATT_DIM
    steps = q_heads // 2 if (q_heads // kv_here) % 2 == 0 else q_heads

    def head(h, _):
        attend(h, q_ref, allc_ref, alln_ref, bias_ref, vc_ref, vn_ref, att_ref)
        return 0

    def second_part(j, _):
        rest = pairs - ahead
        lax.fori_loop(
            ahead + j * rest // chunks, ahead + (j + 1) * rest // chunks, pair, 0
        )
        lax.fori_loop(j * steps // chunks, (j + 1) * steps // chunks, head, 0)
        combine(j, 0)
        return 0

    lax.fori_loop(0, chunks, second_part, 0)

    def drain(j, _):
        back_copy(j, 1 - i).wait_recv()
        back_copy(j, i).wait_send()
        sib_copy(j).wait_send()
        for l in range(levels):

            @pl.when(sends(l))
            def _():
                for r in targets(l):
                    pre_copy(l, j, r).wait_send()

            if l >= 1:

                @pl.when((c % (2 ** (l + 1)) >= 2**l) & (c % 2 == 1))
                def _():
                    relay_copy(l, j).wait_send()

        return 0

    lax.fori_loop(0, chunks, drain, 0)
    for d in range(1, n):
        remote(
            meta_ref, allm_ref.at[me], meta_s.at[d], meta_r.at[me], (me + d) % n
        ).wait_send()
    cache_copy(0, other).wait_send()
    new_copy(0, other).wait_send()
    for d in range(1, n2):
        to = ((c + d) % n2) * 2 + i
        cache_copy(d, to).wait_send()
        forward(0, d).wait_send()

        @pl.when(c + d < n2)
        def _():
            new_copy(d, to).wait_send()

        @pl.when((c + d) % n2 < c)
        def _():
            forward(1, d).wait_send()


def final_kernel(
    part_ref,
    fade_ref,
    sout_ref,
    state_ref,
    meta_ref,
    nk_ref,
    y_ref,
    code_ref,
    scale_ref,
):
    tokens, width = part_ref.shape
    heads = fade_ref.shape[1]
    per_group = min(SSM_HEADS // GROUPS, heads)
    z = lax.axis_index("head")
    group0 = z * heads // (SSM_HEADS // GROUPS)
    block = min(512, width)

    magnitude = jnp.max(meta_ref[:, 0, width:], axis=0, keepdims=True)
    scale = (magnitude + 1e-6) / 127.0
    scale_ref[...] = scale
    code_ref[...] = (nk_ref[...].astype(F32) / scale).astype(BF16)
    fade = fade_ref[...]
    for b in range(width // block):
        here = pl.ds(b * block, block)
        g = group0 + (b * block) // (per_group * HEAD_DIM)
        prior = jnp.dot(
            sout_ref[:, lanes(g * STATE, STATE)], state_ref[:, here], preferred_element_type=F32
        )
        pick = choose(heads, b * block, block).astype(BF16)
        spread = jnp.dot(fade, pick, preferred_element_type=F32)
        y_ref[:, here] = (part_ref[:, here].astype(F32) + spread * prior).astype(BF16)


def body(
    n,
    ssm_input,
    state_in,
    state_out,
    step_size,
    decay_rate,
    forget,
    skip_gain,
    queries,
    new_keys,
    new_values,
    cache_keys,
    cache_values,
    cache_key_scale,
    cache_value_scale,
):
    tokens, width = ssm_input.shape
    heads = step_size.shape[1]
    rows = cache_keys.shape[0]
    channels = new_keys.shape[1]
    q_heads = queries.shape[1] // ATT_DIM
    kv_here = max(1, q_heads // (ATT_HEADS // KV_HEADS))
    kvw = kv_here * ATT_DIM
    per_group = min(SSM_HEADS // GROUPS, heads)
    groups_here = heads // per_group
    limit = pltpu.CompilerParams(vmem_limit_bytes=60 * 1024 * 1024)
    shape = jax.ShapeDtypeStruct
    state, run, fade, at, gram, meta, kvc, kvn = pl.pallas_call(
        local_kernel,
        out_shape=(
            shape((STATE, width), BF16),
            shape((tokens + 16, 3 * heads), BF16),
            shape((tokens, heads), BF16),
            shape((heads, tokens), F32),
            shape((groups_here, tokens, tokens), F32),
            shape((1, width + channels), F32),
            shape((rows, 2 * kvw), BF16),
            shape((tokens, 2 * kvw), BF16),
        ),
        in_specs=[VMEM] * 13,
        out_specs=(VMEM,) * 8,
        compiler_params=limit,
        name="local",
    )(
        ssm_input,
        state_in,
        state_out,
        step_size.T,
        decay_rate.reshape(1, heads),
        forget.reshape(1, tokens),
        skip_gain.reshape(1, heads),
        new_keys,
        new_values,
        cache_keys,
        cache_values,
        cache_key_scale.reshape(1, channels),
        cache_value_scale.reshape(1, channels),
    )
    half = width // 2
    size = min(256, half)
    chunks = half // size
    n2 = n // 2
    levels = n2.bit_length() - 1
    fan = max(1, n2 // 2)
    dma = pltpu.SemaphoreType.DMA
    carried, allm, part, attended = pl.pallas_call(
        functools.partial(comm_kernel, n, chunks),
        out_shape=(
            shape((STATE, width), BF16),
            shape((n, 1, width + channels), F32),
            shape((tokens, width), BF16),
            shape((tokens, queries.shape[1]), BF16),
        ),
        in_specs=[VMEM] * 9,
        out_specs=(VMEM,) * 4,
        scratch_shapes=[
            pltpu.VMEM((n, rows, 2 * kvw), BF16),
            pltpu.VMEM((n, tokens, 2 * kvw), BF16),
            pltpu.VMEM((kv_here, n * rows, 2 * ATT_DIM), BF16),
            pltpu.VMEM((kv_here, n * tokens, 2 * ATT_DIM), BF16),
            pltpu.VMEM((tokens, n * tokens), F32),
            pltpu.VMEM((chunks, STATE, size), BF16),
            pltpu.VMEM((chunks, STATE, size), F32),
            pltpu.VMEM((levels, chunks, STATE, size), BF16),
            pltpu.VMEM((levels, chunks, STATE, size), BF16),
            pltpu.VMEM((chunks, STATE, size), BF16),
            dma((n,)),
            dma((n,)),
            dma((2, n2)),
            dma((2, n)),
            dma((2, n2)),
            dma((chunks,)),
            dma((chunks,)),
            dma((levels, chunks, fan)),
            dma((levels, chunks)),
            dma((levels, chunks)),
            dma((chunks,)),
            dma((chunks,)),
        ],
        compiler_params=pltpu.CompilerParams(
            collective_id=0, has_side_effects=True, vmem_limit_bytes=60 * 1024 * 1024
        ),
        name="exchange",
    )(state, kvc, kvn, meta, ssm_input, run, at, gram, queries)
    y, codes, scale = pl.pallas_call(
        final_kernel,
        out_shape=(
            shape((tokens, width), BF16),
            shape((tokens, channels), BF16),
            shape((1, channels), F32),
        ),
        in_specs=[VMEM] * 6,
        out_specs=(VMEM,) * 3,
        compiler_params=limit,
        name="finish",
    )(part, fade, state_out, carried, allm, new_keys)
    return (y, attended, codes, scale.reshape(channels))

BLOCK = 96


def span_blocks(tokens):
    return max(1, tokens // BLOCK)


def split2(value):
    high = value.astype(BF16)
    low = (value - high.astype(F32)).astype(BF16)
    return jnp.concatenate([high, low], axis=1)


def choose2(heads, begin, size):
    lane = begin + iota((2 * heads, size), 1)
    row = iota((2 * heads, size), 0)
    return (row % heads == lane // HEAD_DIM).astype(BF16)


def factor_rows(tokens):
    nb = span_blocks(tokens)
    size = tokens // nb
    places, at = {}, 0
    for name, rows in (
        [("z", tokens), ("tail", 16)]
        + [(f"z{b}", (b + 1) * size) for b in range(nb - 1)]
        + [("out", tokens), ("skip", 16), ("fade", tokens)]
    ):
        places[name] = (at, at + rows)
        at += rows
    return places, at


def with_ones(v):
    return jnp.concatenate([v, jnp.ones(v.shape, BF16)], axis=1)


NT = (((1,), (1,)), ((), ()))
FACTOR = ATT_DIM**-0.5 * LOG2E


def stream_heads(step, streams, together):
    first = step * streams * together
    return [
        [lanes((first + e * together + f) * ATT_DIM, ATT_DIM) for f in range(together)]
        for e in range(streams)
    ]


def key_columns(step, streams, together, q_ref, all_ref):
    kvw = all_ref.shape[2] // 2
    share = (q_ref.shape[1] // ATT_DIM) // (kvw // ATT_DIM)
    k = (step * streams * together) // share
    return lanes(k * ATT_DIM, ATT_DIM), lanes(kvw + k * ATT_DIM, ATT_DIM)


def score_streams(own, q_ref, keys):
    return [
        lax.dot_general(
            jnp.concatenate([q_ref[:, o] for o in heads], axis=0),
            keys,
            NT,
            preferred_element_type=F32,
        )
        for heads in own
    ]


def attend_cache(step, streams, together, q_ref, allc_ref, sum_ref, peak_ref):
    rows = together * q_ref.shape[0]
    at, av = key_columns(step, streams, together, q_ref, allc_ref)
    keys = allc_ref[:, :, at].reshape(-1, ATT_DIM)
    values = with_ones(allc_ref[:, :, av].reshape(-1, ATT_DIM))
    own = stream_heads(step, streams, together)
    scores = score_streams(own, q_ref, keys)
    for e in range(streams):
        peak = jnp.max(scores[e], axis=1, keepdims=True)
        p = jnp.exp2((scores[e] - peak) * FACTOR).astype(BF16)
        here = pl.ds(pl.multiple_of((step * streams + e) * rows, rows), rows)
        sum_ref[here, :] = jnp.dot(p, values, preferred_element_type=F32)
        peak_ref[here, :] = jnp.broadcast_to(peak, (rows, 128))


def attend_span(
    step, streams, together, chip, q_ref, alln_ref, bias_ref, sum_ref, peak_ref, att_ref
):
    tokens = q_ref.shape[0]
    rows = together * tokens
    at, av = key_columns(step, streams, together, q_ref, alln_ref)
    seen = 2 * chip + 2
    keys = alln_ref[:seen, :, at].reshape(-1, ATT_DIM)
    values = with_ones(alln_ref[:seen, :, av].reshape(-1, ATT_DIM))
    free = keys.shape[0] - 2 * tokens
    own = stream_heads(step, streams, together)
    scores = score_streams(own, q_ref, keys)
    bias = bias_ref[...]
    for e in range(streams):
        near = scores[e][:, free:].reshape(together, tokens, -1) + bias[None]
        near = near.reshape(rows, -1)
        s = jnp.concatenate([scores[e][:, :free], near], axis=1) if free else near
        here = pl.ds(pl.multiple_of((step * streams + e) * rows, rows), rows)
        before = peak_ref[here, :][:, :1]
        peak = jnp.maximum(before, jnp.max(s, axis=1, keepdims=True))
        p = jnp.exp2((s - peak) * FACTOR).astype(BF16)
        both = jnp.dot(p, values, preferred_element_type=F32)
        both += sum_ref[here, :] * jnp.exp2((before - peak) * FACTOR)
        result = (both[:, :ATT_DIM] / both[:, ATT_DIM:]).astype(BF16)
        for f, o in enumerate(own[e]):
            att_ref[:, o] = result[f * tokens : (f + 1) * tokens]


def fused_kernel(
    chunks,
    x_hbm,
    sin_hbm,
    sout_hbm,
    step_hbm,
    decay_hbm,
    forget_hbm,
    skip_hbm,
    q_hbm,
    nk_hbm,
    nv_hbm,
    ck_hbm,
    cv_hbm,
    cks_hbm,
    cvs_hbm,
    y_ref,
    att_ref,
    code_ref,
    scale_ref,
    step_ref,
    decay_ref,
    forget_ref,
    skip_ref,
    cks_ref,
    cvs_ref,
    x_ref,
    sin_ref,
    sout_ref,
    q_ref,
    nk_ref,
    nv_ref,
    ck_ref,
    cv_ref,
    kvc_ref,
    kvn_ref,
    allc_ref,
    alln_ref,
    bias_ref,
    meta_ref,
    allm_ref,
    fac_ref,
    fade_ref,
    z_ref,
    gram_ref,
    turned_ref,
    give_ref,
    sib_ref,
    mine_ref,
    full_ref,
    tx_ref,
    rx_ref,
    enter_ref,
    back_ref,
    other_ref,
    sum_ref,
    peak_ref,
    pick_ref,
    carry_ref,
    wide_ref,
    load_s,
    meta_s,
    meta_r,
    kv_s,
    kv_r,
    kv_f,
    kv_p,
    sib_s,
    sib_r,
    out_s,
    in_r,
    back_s,
    back_r,
):
    n = 8
    tokens, width = x_ref.shape
    heads = step_ref.shape[0]
    per_group = min(SSM_HEADS // GROUPS, heads)
    groups_here = heads // per_group
    channels = nk_ref.shape[1]
    kvw = kvc_ref.shape[1] // 2
    half = width // 2
    size = half // chunks
    near = chunks * 3 // 8
    mid = chunks // 2
    places, _ = factor_rows(tokens)
    nb = span_blocks(tokens)
    bs = tokens // nb

    me = lax.axis_index("seq")
    z = lax.axis_index("head")
    i, c = me % 2, me // 2
    other = me + 1 - 2 * i
    cx, cy = c + 1 - 2 * (c % 2), (c + 2) % 4
    cd = 3 - c
    group0 = z * heads // (SSM_HEADS // GROUPS)
    q_heads = heads * ATT_HEADS // SSM_HEADS
    first_kv = z * q_heads // (ATT_HEADS // KV_HEADS)
    cols = lanes(first_kv * ATT_DIM, kvw)
    gcols = lanes(group0 * STATE, groups_here * STATE)

    barrier = pltpu.get_barrier_semaphore()
    for d in range(1, n):
        pl.semaphore_signal(
            barrier, inc=1, device_id={"seq": (me + d) % n}, device_id_type=MESH
        )

    moves = dict(
        ck=(ck_hbm.at[:, cols], ck_ref),
        cks=(cks_hbm.at[:, cols], cks_ref),
        cv=(cv_hbm.at[:, cols], cv_ref),
        cvs=(cvs_hbm.at[:, cols], cvs_ref),
        nv=(nv_hbm.at[:, cols], nv_ref),
        nk=(nk_hbm, nk_ref),
        step=(step_hbm, step_ref),
        decay=(decay_hbm, decay_ref),
        forget=(forget_hbm, forget_ref),
        skip=(skip_hbm, skip_ref),
        sin=(sin_hbm.at[:, gcols], sin_ref),
        sout=(sout_hbm.at[:, gcols], sout_ref),
        x=(x_hbm, x_ref),
        q=(q_hbm, q_ref),
    )
    loads = {
        name: pltpu.make_async_copy(src, dst, load_s.at[k])
        for k, (name, (src, dst)) in enumerate(moves.items())
    }
    for copy in loads.values():
        copy.start()

    def ready(*names):
        for name in names:
            loads[name].wait()

    def remote(src, dst, ssem, rsem, to):
        return pltpu.make_async_remote_copy(
            src_ref=src,
            dst_ref=dst,
            send_sem=ssem,
            recv_sem=rsem,
            device_id={"seq": to},
            device_id_type=MESH,
        )

    def dev(chip):
        return chip * 2 + i

    alls = (allc_ref, alln_ref)
    owns = (kvc_ref, kvn_ref)

    def own_copy(kind, way):
        to = (other, dev(cx), dev(cy))[way]
        return remote(
            owns[kind], alls[kind].at[me], kv_s.at[kind, way], kv_r.at[kind, me], to
        )

    def pass_copy(kind, way, chip, to):
        slot = dev(chip)
        return remote(
            alls[kind].at[slot],
            alls[kind].at[slot],
            kv_p.at[kind, way],
            kv_r.at[kind, slot],
            dev(to),
        )

    def forward(kind, chip):
        slot = dev(chip)
        return remote(
            alls[kind].at[slot],
            alls[kind].at[slot],
            kv_f.at[kind, chip],
            kv_r.at[kind, slot],
            other,
        )

    def arrived(kind, slot):
        remote(
            owns[kind], alls[kind].at[slot], kv_s.at[kind, 0], kv_r.at[kind, slot], other
        ).wait_recv()

    for k in range(width // 512):
        pick_ref[:, k * 512 : (k + 1) * 512] = choose2(heads, k * 512, 512)
    ready("ck", "cks", "cv", "cvs")
    kvc_ref[:, :kvw] = (ck_ref[...].astype(F32) * cks_ref[...]).astype(BF16)
    kvc_ref[:, kvw:] = (cv_ref[...].astype(F32) * cvs_ref[...]).astype(BF16)
    pl.semaphore_wait(barrier, n - 1)
    for way in (1, 2, 0):
        own_copy(0, way).start()
    ready("nv", "nk")
    kvn_ref[:, :kvw] = nk_ref[:, cols]
    kvn_ref[:, kvw:] = nv_ref[...]

    @pl.when(cx > c)
    def _():
        own_copy(1, 1).start()

    @pl.when(cy > c)
    def _():
        own_copy(1, 2).start()

    own_copy(1, 0).start()

    row, col = iota((tokens, tokens), 0), iota((tokens, tokens), 1)
    lower = jnp.where(col <= row, 1.0, 0.0)
    eye = jnp.where(col == row, 1.0, 0.0).astype(BF16)
    ready("step", "decay", "forget", "skip")
    step = step_ref[...].T
    forgotten = jnp.sum(lower * forget_ref[...], axis=1, keepdims=True)
    decayed = jnp.dot(
        lower, decay_ref[...] * step, precision=HIGHEST, preferred_element_type=F32
    )
    running = -(decayed + forgotten) * LOG2E
    start = running - jnp.log2(step)
    last = running[tokens - 1 : tokens]
    middles = [running[b * bs + bs // 2 - 1 : b * bs + bs // 2] for b in range(nb)]

    meta_ref[:, :channels] = jnp.max(jnp.abs(nk_ref[...].astype(F32)), axis=0, keepdims=True)
    meta_ref[:, channels:] = jnp.concatenate([last, jnp.zeros((1, 128 - heads), F32)], axis=1)

    def meta_copy(d):
        return remote(
            meta_ref, allm_ref.at[me], meta_s.at[d], meta_r.at[me], (me + d) % n
        )

    def meta_arrived(r):
        remote(meta_ref, allm_ref.at[r], meta_s.at[1], meta_r.at[r], r).wait_recv()

    for d in range(1, n):
        meta_copy(d).start()
    allm_ref[me] = meta_ref[...]

    def put(name, value):
        begin, end = places[name]
        fac_ref[begin:end] = split2(jnp.broadcast_to(value, (end - begin, heads)))

    put("z", jnp.exp2(middles[nb - 1] - start))
    put("tail", jnp.exp2(last - middles[nb - 1]))
    for b in range(nb - 1):
        put(f"z{b}", jnp.exp2(middles[b] - start[: (b + 1) * bs]))
    put(
        "out",
        jnp.concatenate(
            [jnp.exp2(running[b * bs : (b + 1) * bs] - middles[b]) for b in range(nb)], axis=0
        ),
    )
    put("skip", skip_ref[...])
    put("fade", jnp.exp2(running))
    ready("sin", "sout")
    for g in range(groups_here):
        gc = slice(g * STATE, (g + 1) * STATE)
        maps_in = sin_ref[:, gc]
        gram = lax.dot_general(
            sout_ref[:, gc], maps_in, (((1,), (1,)), ((), ())), preferred_element_type=F32
        )
        gram_ref[g] = jnp.where(col <= row, gram, 0.0).astype(BF16)
        turned_ref[g] = lax.dot_general(
            maps_in, eye, (((0,), (0,)), ((), ())), preferred_element_type=F32
        ).astype(BF16)
    ready("x")

    def spread(first, final, begin, wide=size):
        rows = fac_ref[places[first][0] : places[final][1]]
        return jnp.dot(rows, pick_ref[:, lanes(begin, wide)], preferred_element_type=F32)

    def local_state(begin):
        here = lanes(begin, 2 * size)
        by = spread("z", "tail", begin, 2 * size)
        scaled = (x_ref[:, here].astype(F32) * by[:tokens]).astype(BF16)
        z_ref[:, here] = scaled
        sums = jnp.dot(
            turned_ref[begin // (per_group * HEAD_DIM)], scaled, preferred_element_type=F32
        )
        sums = (sums * by[tokens : tokens + 1]).astype(BF16)
        return sums[:, :size], sums[:, size:]

    def sib_copy(j):
        return remote(give_ref.at[j], sib_ref.at[j], sib_s.at[j], sib_r.at[j], other)

    shift = (c % 2) * (1 - c // 2) * mid

    def give(s, _):
        j = (2 * s + shift) % chunks
        for e, state in enumerate(local_state((1 - i) * half + j * size)):
            give_ref[j + e] = state
            sib_copy(j + e).start()
        return 0

    def pass_cache():
        arrived(0, dev(cx))

        @pl.when(c >= 1)
        def _():
            pass_copy(0, 0, cx, cy).start()

        forward(0, cx).start()
        arrived(0, dev(cy))

        @pl.when(c == 3)
        def _():
            pass_copy(0, 1, cy, cx).start()

        forward(0, cy).start()

    lax.fori_loop(0, chunks // 2, give, 0)
    pass_cache()
    meta_arrived(other)

    def logs_of(r):
        return allm_ref[r, :, channels : channels + heads]

    def set_fades(third):
        logs = jnp.concatenate(
            [logs_of(2 * c), logs_of(2 * c + 1), third, jnp.zeros((13, heads), F32)], axis=0
        )
        fade_ref[...] = split2(jnp.exp2(logs))

    def fades(j):
        return jnp.dot(
            fade_ref[...],
            pick_ref[:, lanes(i * half + j * size, size)],
            preferred_element_type=F32,
        )

    set_fades(jnp.zeros((1, heads), F32))

    def full_copy(j):
        slot = jnp.where(c == 0, 0, 1)
        return remote(
            full_ref.at[j], rx_ref.at[slot, j], out_s.at[0, j], in_r.at[slot, j], dev(cx)
        )

    def full_sent(j):
        return (c == 0) | ((c == 1) & (j >= near)) | ((c == 2) & (j < near))

    def own(s, _):
        j = (2 * s + shift) % chunks
        states = local_state(i * half + j * size)
        for e, mine in enumerate(states):
            mine_ref[j + e] = mine
        for e in range(2):
            sib_copy(j + e).wait_recv()
        for e, mine in enumerate(states):
            mine, theirs = mine.astype(F32), sib_ref[j + e].astype(F32)
            d1 = fades(j + e)[1:2]
            full = jnp.where(i == 0, d1 * mine + theirs, d1 * theirs + mine)
            full_ref[j + e] = full.astype(BF16)

        for e in range(2):

            @pl.when(full_sent(j + e))
            def _():
                full_copy(j + e).start()

        return 0

    lax.fori_loop(0, chunks // 2, own, 0)
    bias_ref[...] = jnp.where(
        iota((tokens, 2 * tokens), 1) <= i * tokens + iota((tokens, 2 * tokens), 0), 0.0, NEG
    )

    def within(s, _):
        begin = s * 2 * size
        here = lanes(begin, 2 * size)
        by = spread("z0" if nb > 1 else "out", "fade", begin, 2 * size)
        at = 0
        gram = gram_ref[begin // (per_group * HEAD_DIM)]
        x = x_ref[:, here].astype(F32)
        parts = []
        for b in range(nb):
            high = (b + 1) * bs
            if b + 1 < nb:
                scaled = (x[:high] * by[at : at + high]).astype(BF16)
                at += high
            else:
                scaled = z_ref[:, here]
            parts.append(
                jnp.dot(gram[b * bs : high, :high], scaled, preferred_element_type=F32)
            )
        y = by[at : at + tokens] * jnp.concatenate(parts, axis=0)
        y_ref[:, here] = (y + by[at + tokens : at + tokens + 1] * x).astype(BF16)
        wide_ref[:, here] = by[at + tokens + 16 :].astype(BF16)
        return 0

    @pl.when(cx < c)
    def _():
        arrived(1, dev(cx))

        @pl.when(c == 1)
        def _():
            pass_copy(1, 0, cx, cy).start()

        forward(1, cx).start()

    @pl.when(cy < c)
    def _():
        arrived(1, dev(cy))

        @pl.when(c == 3)
        def _():
            pass_copy(1, 1, cy, cx).start()

        forward(1, cy).start()

    lax.fori_loop(0, chunks // 2, within, 0)
    arrived(0, dev(cd))
    forward(0, cd).start()
    lax.fori_loop(chunks // 2, chunks, within, 0)

    for d in range(1, n):
        r = (me + d) % n

        @pl.when(r != other)
        def _():
            meta_arrived(r)

    chip = jnp.where(c == 0, 1, jnp.where(c == 3, 2, c))
    set_fades(logs_of(2 * chip) + logs_of(2 * chip + 1))
    scale = (jnp.max(allm_ref[:, 0, :channels], axis=0, keepdims=True) + 1e-6) / 127.0
    scale_ref[...] = scale
    code_ref[...] = (nk_ref[...].astype(F32) / scale).astype(BF16)

    allc_ref[me] = kvc_ref[...]
    alln_ref[me] = kvn_ref[...]
    arrived(0, other)
    for d in range(1, 4):
        arrived(0, (c + d) % 4 * 2 + 1 - i)

    ready("q")

    def span_arrived():
        @pl.when(cd < c)
        def _():
            arrived(1, dev(cd))
            forward(1, cd).start()

        arrived(1, other)
        for d in range(1, 4):
            there = (c + d) % 4

            @pl.when(there < c)
            def _():
                arrived(1, there * 2 + 1 - i)

    def second_way(s):
        late = s // mid
        return mid + s - late * (2 * mid - near)

    def order(s):
        later = s // (chunks - near)
        even = (1 - later) * second_way(s * (1 - later)) + later * (s - chunks + near)
        last = (s + chunks - near) // chunks
        odd = (1 - last) * s + last * second_way((s - near) * last)
        third = c // 2
        return (1 - c % 2) * even + (c % 2) * (third * odd + (1 - third) * s)

    def prior(begin, carried):
        here = lanes(begin, size)
        group = begin // (per_group * HEAD_DIM)
        term = jnp.dot(sout_ref[:, lanes(group * STATE, STATE)], carried, preferred_element_type=F32)
        by = wide_ref[:, here].astype(F32)
        return begin, (y_ref[:, here].astype(F32) + by * term).astype(BF16)

    def put_prior(result):
        begin, value = result
        y_ref[:, lanes(begin, size)] = value

    def rx_wait(slot, j):
        remote(
            full_ref.at[j], rx_ref.at[slot, j], out_s.at[0, j], in_r.at[slot, j], dev(cx)
        ).wait_recv()

    def tx_copy(j, chip):
        return remote(tx_ref.at[j], rx_ref.at[0, j], out_s.at[1, j], in_r.at[0, j], dev(chip))

    def relay_copy(j):
        return remote(
            rx_ref.at[0, j], rx_ref.at[0, j], out_s.at[2, j], in_r.at[0, j], dev(cx)
        )

    def back_copy(j):
        return remote(back_ref.at[j], other_ref.at[j], back_s.at[j], back_r.at[j], other)

    def pass_on(s):
        @pl.when((c == 1) | (c == 2))
        def _():
            j = (c % 2) * s + (1 - c % 2) * second_way(s)
            rx_wait(0, j)
            keep = fades(j)[2:3]
            tx_ref[j] = (keep * rx_ref[0, j].astype(F32) + full_ref[j].astype(F32)).astype(BF16)
            tx_copy(j, 3).start()

        @pl.when(c == 0)
        def _():
            j = second_way(s)
            rx_wait(1, j)
            keep = fades(j)[2:3]
            tx_ref[j] = (keep * full_ref[j].astype(F32) + rx_ref[1, j].astype(F32)).astype(BF16)
            tx_copy(j, 2).start()

        @pl.when(c == 3)
        def _():
            rx_wait(0, s)
            relay_copy(s).start()

    base = 2 + (c // 2) * (4 + c % 2)
    stride = 2 - c // 2
    passes = (c % 2) * near + (1 - c % 2) * (chunks - near)

    def pass_at(place):
        ahead = place - base
        s = ahead // stride

        @pl.when((ahead >= 0) & (ahead % stride == 0) & (s < passes))
        def _():
            pass_on(s)

    def settle(s):
        j = order(s)
        by = fades(j)
        d0, keep = by[0:1], by[2:3]

        @pl.when((c > 0) & (s >= passes))
        def _():
            rx_wait(0, j)

        @pl.when((c == 3) & (s < near))
        def _():
            rx_wait(1, j)
            enter_ref[...] = keep * rx_ref[0, j].astype(F32) + rx_ref[1, j].astype(F32)

        @pl.when(c == 0)
        def _():
            enter_ref[...] = jnp.zeros(enter_ref.shape, F32)

        @pl.when((c == 1) | (c == 2) | ((c == 3) & (s >= near)))
        def _():
            enter_ref[...] = rx_ref[0, j].astype(F32)

        enter = enter_ref[...]
        first = jnp.where(i == 0, mine_ref[j].astype(F32), sib_ref[j].astype(F32))
        middle = d0 * enter + first
        back_ref[j] = jnp.where(i == 0, middle, enter).astype(BF16)
        back_copy(j).start()
        carry_ref[...] = jnp.where(i == 0, enter, middle).astype(BF16)

    def slot(s, _):
        settle(s)

        @pl.when(s == 0)
        def _():
            put_prior(prior(i * half + order(s) * size, carry_ref[...]))

        @pl.when(s > 0)
        def _():
            far = order(s - 1)
            back_copy(far).wait_recv()
            both = [
                prior(i * half + order(s) * size, carry_ref[...]),
                prior((1 - i) * half + far * size, other_ref[far]),
            ]
            for each in both:
                put_prior(each)

        return 0

    streams, together = 4, 1
    steps = q_heads // (streams * together)
    pass_at(2)

    def first_part(h, _):
        attend_cache(h, streams, 2 * together, q_ref, allc_ref, sum_ref, peak_ref)
        pass_at(3 + 2 * h)
        pass_at(4 + 2 * h)
        return 0

    lax.fori_loop(0, steps // 2, first_part, 0)
    span_arrived()

    def second_part(h, _):
        for chip in range(n // 2):

            @pl.when(c == chip)
            def _():
                attend_span(
                    h,
                    streams,
                    together,
                    chip,
                    q_ref,
                    alln_ref,
                    bias_ref,
                    sum_ref,
                    peak_ref,
                    att_ref,
                )

        pass_at(3 + steps + h)
        return slot(h, 0)

    lax.fori_loop(0, steps, second_part, 0)
    lax.fori_loop(steps, chunks, slot, 0)
    far = order(chunks - 1)
    back_copy(far).wait_recv()
    put_prior(prior((1 - i) * half + far * size, other_ref[far]))

    def drain(j, _):
        back_copy(j).wait_send()
        sib_copy(j).wait_send()

        @pl.when(full_sent(j))
        def _():
            full_copy(j).wait_send()

        @pl.when(((c == 1) & (j < near)) | ((c == 2) & (j >= near)))
        def _():
            tx_copy(j, 3).wait_send()

        @pl.when((c == 0) & (j >= near))
        def _():
            tx_copy(j, 2).wait_send()

        @pl.when((c == 3) & (j < near))
        def _():
            relay_copy(j).wait_send()

        return 0

    lax.fori_loop(0, chunks, drain, 0)
    for d in range(1, n):
        meta_copy(d).wait_send()
    for way in (1, 2, 0):
        own_copy(0, way).wait_send()
    own_copy(1, 0).wait_send()

    @pl.when(cx > c)
    def _():
        own_copy(1, 1).wait_send()

    @pl.when(cy > c)
    def _():
        own_copy(1, 2).wait_send()

    @pl.when(c >= 1)
    def _():
        pass_copy(0, 0, cx, cy).wait_send()

    @pl.when(c == 3)
    def _():
        pass_copy(0, 1, cy, cx).wait_send()
        pass_copy(1, 1, cy, cx).wait_send()

    @pl.when(c == 1)
    def _():
        pass_copy(1, 0, cx, cy).wait_send()

    for chip_ in (cx, cy, cd):
        forward(0, chip_).wait_send()

        @pl.when(chip_ < c)
        def _():
            forward(1, chip_).wait_send()


def finish_kernel(*refs):
    count = (len(refs) - 1) // 2
    copies = [
        pltpu.make_async_copy(refs[k], refs[count + k], refs[-1].at[k]) for k in range(count)
    ]
    for copy in copies:
        copy.start()
    for copy in copies:
        copy.wait()


def fused_body(
    ssm_input,
    state_in,
    state_out,
    step_size,
    decay_rate,
    forget,
    skip_gain,
    queries,
    new_keys,
    new_values,
    cache_keys,
    cache_values,
    cache_key_scale,
    cache_value_scale,
):
    n = 8
    tokens, width = ssm_input.shape
    heads = step_size.shape[1]
    rows = cache_keys.shape[0]
    channels = new_keys.shape[1]
    q_width = queries.shape[1]
    kv_here = max(1, q_width // ATT_DIM // (ATT_HEADS // KV_HEADS))
    kvw = kv_here * ATT_DIM
    groups_here = heads // min(SSM_HEADS // GROUPS, heads)
    half = width // 2
    size = min(256, half)
    chunks = half // size
    _, fac = factor_rows(tokens)
    shape = jax.ShapeDtypeStruct
    dma = pltpu.SemaphoreType.DMA
    any_ = pl.BlockSpec(memory_space=pl.ANY)
    piece = pltpu.VMEM((chunks, STATE, size), BF16)
    results = pl.pallas_call(
        functools.partial(fused_kernel, chunks),
        out_shape=(
            pltpu.VMEM((tokens, width), BF16),
            pltpu.VMEM((tokens, q_width), BF16),
            pltpu.VMEM((tokens, channels), BF16),
            pltpu.VMEM((1, channels), F32),
        ),
        in_specs=[any_] * 14,
        out_specs=(VMEM,) * 4,
        scratch_shapes=[
            pltpu.VMEM((heads, tokens), F32),
            pltpu.VMEM((1, heads), F32),
            pltpu.VMEM((1, tokens), F32),
            pltpu.VMEM((1, heads), F32),
            pltpu.VMEM((1, kvw), F32),
            pltpu.VMEM((1, kvw), F32),
            pltpu.VMEM((tokens, width), BF16),
            pltpu.VMEM((tokens, groups_here * STATE), BF16),
            pltpu.VMEM((tokens, groups_here * STATE), BF16),
            pltpu.VMEM((tokens, q_width), BF16),
            pltpu.VMEM((tokens, channels), BF16),
            pltpu.VMEM((tokens, kvw), BF16),
            pltpu.VMEM((rows, kvw), BF16),
            pltpu.VMEM((rows, kvw), BF16),
            pltpu.VMEM((rows, 2 * kvw), BF16),
            pltpu.VMEM((tokens, 2 * kvw), BF16),
            pltpu.VMEM((n, rows, 2 * kvw), BF16),
            pltpu.VMEM((n, tokens, 2 * kvw), BF16),
            pltpu.VMEM((tokens, 2 * tokens), F32),
            pltpu.VMEM((1, channels + 128), F32),
            pltpu.VMEM((n, 1, channels + 128), F32),
            pltpu.VMEM((fac, 2 * heads), BF16),
            pltpu.VMEM((16, 2 * heads), BF16),
            pltpu.VMEM((tokens, width), BF16),
            pltpu.VMEM((groups_here, tokens, tokens), BF16),
            pltpu.VMEM((groups_here, STATE, tokens), BF16),
            piece,
            piece,
            piece,
            piece,
            piece,
            pltpu.VMEM((2, chunks, STATE, size), BF16),
            pltpu.VMEM((STATE, size), F32),
            piece,
            piece,
            pltpu.VMEM((q_width // ATT_DIM * tokens, 2 * ATT_DIM), F32),
            pltpu.VMEM((q_width // ATT_DIM * tokens, 128), F32),
            pltpu.VMEM((2 * heads, width), BF16),
            pltpu.VMEM((STATE, size), BF16),
            pltpu.VMEM((tokens, width), BF16),
            dma((14,)),
            dma((n,)),
            dma((n,)),
            dma((2, 3)),
            dma((2, n)),
            dma((2, 4)),
            dma((2, 2)),
            dma((chunks,)),
            dma((chunks,)),
            dma((3, chunks)),
            dma((2, chunks)),
            dma((chunks,)),
            dma((chunks,)),
        ],
        compiler_params=pltpu.CompilerParams(
            collective_id=0, has_side_effects=True, vmem_limit_bytes=612 * 1024 * 1024 // 10
        ),
        name="fused",
    )(
        ssm_input,
        state_in,
        state_out,
        step_size.T,
        decay_rate.reshape(1, heads),
        forget.reshape(1, tokens),
        skip_gain.reshape(1, heads),
        queries,
        new_keys,
        new_values,
        cache_keys,
        cache_values,
        cache_key_scale.reshape(1, channels),
        cache_value_scale.reshape(1, channels),
    )
    y, attended, codes, scale = pl.pallas_call(
        finish_kernel,
        out_shape=(
            shape((tokens, width), BF16),
            shape((tokens, q_width), BF16),
            shape((tokens, channels), BF16),
            shape((1, channels), F32),
        ),
        in_specs=[VMEM] * 4,
        out_specs=(any_,) * 4,
        scratch_shapes=[dma((4,))],
        compiler_params=pltpu.CompilerParams(vmem_limit_bytes=4 * 1024 * 1024),
        name="finish",
    )(*results)
    return (y, attended, codes, scale.reshape(channels))


def fits_fused(mesh):
    heads = SSM_HEADS // mesh.shape["head"]
    return mesh.shape["seq"] == 8 and heads == 64


def solution(mesh):
    in_specs = (
        P("seq", "head"),
        P("seq", None),
        P("seq", None),
        P("seq", "head"),
        P("head"),
        P("seq"),
        P("head"),
        P("seq", "head"),
        P("seq", None),
        P("seq", None),
        P("seq", None),
        P("seq", None),
        P(),
        P(),
    )
    out_specs = (P("seq", "head"), P("seq", "head"), P("seq", None), P())
    general = functools.partial(body, mesh.shape["seq"])
    return jax.shard_map(
        fused_body if fits_fused(mesh) else general,
        mesh=mesh,
        in_specs=in_specs,
        out_specs=out_specs,
        check_vma=False,
    )
```

```python
import functools
import jax
import jax.numpy as jnp
from jax import lax
from jax.experimental import pallas as pl
from jax.experimental.pallas import tpu as pltpu
from jax.sharding import PartitionSpec as P

SSM_HEADS = 256
HEAD_DIM = 64
STATE = 256
GROUPS = 8
ATT_HEADS = 64
KV_HEADS = 8
ATT_DIM = 128

NEG = -1e30
LOG2E = 1.4426950408889634
HIGHEST = lax.Precision.HIGHEST
MESH = pl.DeviceIdType.MESH
VMEM = pl.BlockSpec(memory_space=pltpu.VMEM)
F32 = jnp.float32
BF16 = jnp.bfloat16


def iota(shape, axis):
    return lax.broadcasted_iota(jnp.int32, shape, axis)


def lanes(start, size):
    return pl.ds(pl.multiple_of(start, 128), size)


def local_kernel(
    x_ref,
    sin_ref,
    sout_ref,
    step_ref,
    decay_ref,
    forget_ref,
    skip_ref,
    nk_ref,
    nv_ref,
    ck_ref,
    cv_ref,
    cks_ref,
    cvs_ref,
    state_ref,
    run_ref,
    fade_ref,
    at_ref,
    gram_ref,
    meta_ref,
    kvc_ref,
    kvn_ref,
):
    tokens, width = x_ref.shape
    heads = step_ref.shape[0]
    per_group = min(SSM_HEADS // GROUPS, heads)
    groups_here = heads // per_group
    z = lax.axis_index("head")
    group0 = z * heads // (SSM_HEADS // GROUPS)
    kvw = kvc_ref.shape[1] // 2
    q_heads = heads * ATT_HEADS // SSM_HEADS
    first = z * q_heads // (ATT_HEADS // KV_HEADS)
    cols = lanes(first * ATT_DIM, kvw)
    kvc_ref[:, :kvw] = (ck_ref[:, cols].astype(F32) * cks_ref[:, cols]).astype(BF16)
    kvc_ref[:, kvw:] = (cv_ref[:, cols].astype(F32) * cvs_ref[:, cols]).astype(BF16)
    kvn_ref[:, :kvw] = nk_ref[:, cols]
    kvn_ref[:, kvw:] = nv_ref[:, cols]
    meta_ref[:, width:] = jnp.max(jnp.abs(nk_ref[...].astype(F32)), axis=0, keepdims=True)

    row, col = iota((tokens, tokens), 0), iota((tokens, tokens), 1)
    lower = jnp.where(col <= row, 1.0, 0.0)
    eye = jnp.where(col == row, 1.0, 0.0)
    step = step_ref[...].T
    forgotten = jnp.sum(lower * forget_ref[...], axis=1, keepdims=True)
    decayed = jnp.dot(
        lower, decay_ref[...] * step, precision=HIGHEST, preferred_element_type=F32
    )
    running = -(decayed + forgotten) * LOG2E
    start = running - jnp.log2(step)
    at_ref[...] = start.T
    rest = jnp.concatenate(
        [running, jnp.broadcast_to(skip_ref[...], (16, heads))], axis=0
    )
    for third in range(3):
        piece = rest.astype(BF16)
        run_ref[:, third * heads : (third + 1) * heads] = piece
        rest = rest - piece.astype(F32)
    fade_ref[...] = jnp.exp2(running).astype(BF16)
    tail = jnp.exp2(running[tokens - 1 : tokens] - start).astype(BF16)
    last = running[tokens - 8 : tokens]
    block = min(512, width)
    for g in range(groups_here):
        gcols = lanes((group0 + g) * STATE, STATE)
        maps_in = sin_ref[:, gcols]
        gram_ref[g] = lax.dot_general(
            sout_ref[:, gcols], maps_in, (((1,), (1,)), ((), ())), preferred_element_type=F32
        )
        turned = lax.dot_general(
            maps_in,
            eye.astype(BF16),
            (((0,), (0,)), ((), ())),
            preferred_element_type=F32,
        ).astype(BF16)
        for b in range(per_group * HEAD_DIM // block):
            begin = g * per_group * HEAD_DIM + b * block
            here = pl.ds(begin, block)
            pick = choose(heads, begin, block)
            meta_ref[:, here] = jnp.dot(
                last, pick, precision=HIGHEST, preferred_element_type=F32
            )[7:8]
            scale = jnp.dot(tail, pick.astype(BF16), preferred_element_type=F32)
            scaled = (x_ref[:, here].astype(F32) * scale).astype(BF16)
            state_ref[:, here] = jnp.dot(
                turned, scaled, preferred_element_type=F32
            ).astype(BF16)


def choose(heads, begin, size):
    lane = begin + iota((heads, size), 1)
    return (iota((heads, size), 0) == lane // HEAD_DIM).astype(F32)


def within_pair(p, x_ref, run_ref, at_ref, gram_ref, part_ref):
    tokens = x_ref.shape[0]
    heads = run_ref.shape[1] // 3
    per_group = min(SSM_HEADS // GROUPS, heads)
    here = lanes(p * 128, 128)
    pick = choose(heads, p * 128, 128).astype(BF16)
    both = jnp.dot(
        run_ref[...], jnp.concatenate([pick] * 3, axis=0), preferred_element_type=F32
    )
    run, skip = both[:tokens], both[tokens : tokens + 1]
    x = x_ref[:, here]
    gram = gram_ref[(2 * p) // per_group]
    causal = iota((tokens, tokens), 1) <= iota((tokens, tokens), 0)

    def one(k):
        spread = run[:, k * HEAD_DIM : k * HEAD_DIM + 1] - at_ref[pl.ds(2 * p + k, 1), :]
        return (jnp.exp2(jnp.where(causal, spread, NEG)) * gram).astype(BF16)

    pair = jnp.dot(
        jnp.concatenate([one(0), one(1)], axis=0), x, preferred_element_type=F32
    )
    y = jnp.where(iota((tokens, 128), 1) < HEAD_DIM, pair[:tokens], pair[tokens:])
    part_ref[:, here] = (y + skip * x.astype(F32)).astype(BF16)


def attend(h, q_ref, allc_ref, alln_ref, bias_ref, vc_ref, vn_ref, att_ref):
    q_heads = q_ref.shape[1] // ATT_DIM
    kv_here = vc_ref.shape[0]
    share = q_heads // kv_here
    together = 2 if share % 2 == 0 else 1
    tokens = q_ref.shape[0]
    k = (h * together) // share
    factor = ATT_DIM**-0.5 * LOG2E
    nt = (((1,), (1,)), ((), ()))
    own = [lanes((h * together + e) * ATT_DIM, ATT_DIM) for e in range(together)]
    q = jnp.concatenate([q_ref[:, o] for o in own], axis=0)
    at = lanes(k * ATT_DIM, ATT_DIM)
    keys_c = allc_ref[:, :, at].reshape(-1, ATT_DIM)
    keys_n = alln_ref[:, :, at].reshape(-1, ATT_DIM)
    old = lax.dot_general(q, keys_c, nt, preferred_element_type=F32)
    new = lax.dot_general(q, keys_n, nt, preferred_element_type=F32)
    bias = bias_ref[...]
    new = (new.reshape(together, tokens, -1) + bias[None]).reshape(together * tokens, -1)
    peak = jnp.maximum(
        jnp.max(old, axis=1, keepdims=True), jnp.max(new, axis=1, keepdims=True)
    )
    old = jnp.exp2((old - peak) * factor).astype(BF16)
    new = jnp.exp2((new - peak) * factor).astype(BF16)
    both = jnp.dot(old, vc_ref[k], preferred_element_type=F32) + jnp.dot(
        new, vn_ref[k], preferred_element_type=F32
    )
    result = (both[:, :ATT_DIM] / both[:, ATT_DIM:]).astype(BF16)
    for e in range(together):
        att_ref[:, own[e]] = result[e * tokens : (e + 1) * tokens]


def comm_kernel(
    n,
    chunks,
    state_ref,
    kvc_ref,
    kvn_ref,
    meta_ref,
    x_ref,
    run_ref,
    at_ref,
    gram_ref,
    q_ref,
    out_ref,
    allm_ref,
    part_ref,
    att_ref,
    allc_ref,
    alln_ref,
    vc_ref,
    vn_ref,
    bias_ref,
    sib_ref,
    own_ref,
    incl_ref,
    recv_ref,
    back_ref,
    meta_s,
    meta_r,
    kv_s,
    kv_r,
    kv_f,
    sib_s,
    sib_r,
    pre_s,
    pre_r,
    rel_s,
    back_s,
    back_r,
):
    n2 = n // 2
    levels = n2.bit_length() - 1
    me = lax.axis_index("seq")
    i, c = me % 2, me // 2
    other = me + 1 - 2 * i
    width = state_ref.shape[1]
    half = width // 2
    size = half // chunks

    barrier = pltpu.get_barrier_semaphore()
    for d in range(1, n):
        pl.semaphore_signal(
            barrier, inc=1, device_id={"seq": (me + d) % n}, device_id_type=MESH
        )
    pl.semaphore_wait(barrier, n - 1)

    def remote(src, dst, ssem, rsem, to):
        return pltpu.make_async_remote_copy(
            src_ref=src,
            dst_ref=dst,
            send_sem=ssem,
            recv_sem=rsem,
            device_id={"seq": to},
            device_id_type=MESH,
        )

    def sib_copy(j):
        return remote(
            state_ref.at[:, lanes((1 - i) * half + j * size, size)],
            sib_ref.at[j],
            sib_s.at[j],
            sib_r.at[j],
            other,
        )

    for j in range(chunks):
        sib_copy(j).start()
    for d in range(1, n):
        remote(
            meta_ref, allm_ref.at[me], meta_s.at[d], meta_r.at[me], (me + d) % n
        ).start()

    def cache_copy(d, to):
        return remote(kvc_ref, allc_ref.at[me], kv_s.at[0, d], kv_r.at[0, me], to)

    def new_copy(d, to):
        return remote(kvn_ref, alln_ref.at[me], kv_s.at[1, d], kv_r.at[1, me], to)

    cache_copy(0, other).start()
    new_copy(0, other).start()
    for d in range(1, n2):
        to = ((c + d) % n2) * 2 + i
        cache_copy(d, to).start()

        @pl.when(c + d < n2)
        def _():
            new_copy(d, to).start()

    allm_ref[me] = meta_ref[...]
    allc_ref[me] = kvc_ref[...]
    alln_ref[me] = kvn_ref[...]
    for d in range(1, n2):
        later = c + d

        @pl.when(later < n2)
        def _():
            for k in range(2):
                alln_ref[later * 2 + k] = jnp.zeros(kvn_ref.shape, BF16)

    for d in range(1, n):
        r = (me + d) % n
        remote(meta_ref, allm_ref.at[r], meta_s.at[d], meta_r.at[r], r).wait_recv()

    def sends(l):
        return c % (2 ** (l + 1)) == 2**l - 1

    def targets(l):
        return [0] if l == 0 else list(range(1, 2**l, 2))

    def pre_copy(l, j, r):
        return remote(
            incl_ref.at[l, j],
            recv_ref.at[l, j],
            pre_s.at[l, j, r],
            pre_r.at[l, j],
            ((c + 1 + r) % n2) * 2 + i,
        )

    def relay_copy(l, j):
        return remote(
            recv_ref.at[l, j],
            recv_ref.at[l, j],
            rel_s.at[l, j],
            pre_r.at[l, j],
            ((c + n2 - 1) % n2) * 2 + i,
        )

    def logs(r, j):
        return allm_ref[r, :, lanes(i * half + j * size, size)]

    def gather_first(j, _):
        sib_copy(j).wait_recv()
        mine = state_ref[:, lanes(i * half + j * size, size)].astype(F32)
        theirs = sib_ref[j].astype(F32)
        d1 = jnp.exp2(logs(2 * c + 1, j))
        total = jnp.where(i == 0, d1 * mine + theirs, d1 * theirs + mine)
        incl_ref[0, j] = total.astype(BF16)
        own_ref[j] = jnp.zeros(own_ref.shape[1:], F32)

        @pl.when(sends(0))
        def _():
            pre_copy(0, j, 0).start()

        return 0

    lax.fori_loop(0, chunks, gather_first, 0)
    fresh = bias_ref.shape[1]
    tokens = x_ref.shape[0]
    seen = iota((tokens, fresh), 1) <= me * tokens + iota((tokens, fresh), 0)
    bias_ref[...] = jnp.where(seen, 0.0, NEG)
    pairs = width // 128
    early = n2
    ahead = pairs * 3 // 4

    def pair(p, _):
        within_pair(p, x_ref, run_ref, at_ref, gram_ref, part_ref)
        return 0


    def forward(kind, d):
        src = allc_ref if kind == 0 else alln_ref
        slot = ((c + d) % n2) * 2 + i
        return remote(
            src.at[slot], src.at[slot], kv_f.at[kind, d], kv_r.at[kind, slot], other
        )

    def combine(j, _):
        for l in range(levels):

            @pl.when(c % (2 ** (l + 1)) >= 2**l)
            def _():
                pre_copy(l, j, 0).wait_recv()
                if l >= 1:

                    @pl.when(c % 2 == 1)
                    def _():
                        relay_copy(l, j).start()

                base = c - c % (2**l)
                logsum = jnp.zeros((1, size), F32)
                for back in range(1, 2**l):
                    at = (c + n2 - back) % n2
                    both = logs(2 * at, j) + logs(2 * at + 1, j)
                    logsum += jnp.where(c - back >= base, both, 0.0)
                own_ref[j] = jnp.exp2(logsum) * recv_ref[l, j].astype(F32) + own_ref[j]

            if l + 1 < levels:

                @pl.when(sends(l + 1))
                def _():
                    keep = jnp.exp2(logs(2 * c, j) + logs(2 * c + 1, j))
                    incl_ref[l + 1, j] = (
                        keep * own_ref[j] + incl_ref[0, j].astype(F32)
                    ).astype(BF16)
                    for r in targets(l + 1):
                        pre_copy(l + 1, j, r).start()

        enter = own_ref[j]
        mine = state_ref[:, lanes(i * half + j * size, size)].astype(F32)
        first = jnp.where(i == 0, mine, sib_ref[j].astype(F32))
        middle = jnp.exp2(logs(2 * c, j)) * enter + first
        out_ref[:, lanes(i * half + j * size, size)] = jnp.where(
            i == 0, enter, middle
        ).astype(BF16)
        back_ref[j] = jnp.where(i == 0, middle, enter).astype(BF16)
        back_copy(j, i).start()
        return 0

    def remote_slot(kind, d):
        src = allc_ref if kind == 0 else alln_ref
        mine = kvc_ref if kind == 0 else kvn_ref
        slot = ((c + d) % n2) * 2 + i
        return remote(mine, src.at[slot], kv_s.at[kind, d], kv_r.at[kind, slot], slot)

    def back_copy(j, who):
        return remote(
            back_ref.at[j],
            out_ref.at[:, lanes(who * half + j * size, size)],
            back_s.at[j],
            back_r.at[j],
            other,
        )

    def first_part(j, _):
        lax.fori_loop(j * ahead // early, (j + 1) * ahead // early, pair, 0)
        for d in range(1, n2):

            @pl.when(j == d)
            def _():
                remote_slot(0, d).wait_recv()
                forward(0, d).start()

                @pl.when((c + d) % n2 < c)
                def _():
                    remote_slot(1, d).wait_recv()
                    forward(1, d).start()

        return 0

    lax.fori_loop(0, early, first_part, 0)

    def other_slot(kind, d):
        src = allc_ref if kind == 0 else alln_ref
        mine = kvc_ref if kind == 0 else kvn_ref
        slot = ((c + d) % n2) * 2 + (1 - i)
        return remote(mine, src.at[slot], kv_f.at[kind, d], kv_r.at[kind, slot], other)

    for d in range(n2):
        other_slot(0, d).wait_recv()
    other_slot(1, 0).wait_recv()
    for d in range(1, n2):

        @pl.when((c + d) % n2 < c)
        def _():
            other_slot(1, d).wait_recv()

    kv_here = vc_ref.shape[0]
    for k in range(kv_here):
        at = (kv_here + k) * ATT_DIM
        for all_ref, ext_ref in ((allc_ref, vc_ref), (alln_ref, vn_ref)):
            ext_ref[k, :, :ATT_DIM] = all_ref[:, :, at : at + ATT_DIM].reshape(-1, ATT_DIM)
            ext_ref[k, :, ATT_DIM:] = jnp.ones((ext_ref.shape[1], ATT_DIM), BF16)

    q_heads = q_ref.shape[1] // ATT_DIM
    steps = q_heads // 2 if (q_heads // kv_here) % 2 == 0 else q_heads

    def head(h, _):
        attend(h, q_ref, allc_ref, alln_ref, bias_ref, vc_ref, vn_ref, att_ref)
        return 0

    def second_part(j, _):
        rest = pairs - ahead
        lax.fori_loop(
            ahead + j * rest // chunks, ahead + (j + 1) * rest // chunks, pair, 0
        )
        lax.fori_loop(j * steps // chunks, (j + 1) * steps // chunks, head, 0)
        combine(j, 0)
        return 0

    lax.fori_loop(0, chunks, second_part, 0)

    def drain(j, _):
        back_copy(j, 1 - i).wait_recv()
        back_copy(j, i).wait_send()
        sib_copy(j).wait_send()
        for l in range(levels):

            @pl.when(sends(l))
            def _():
                for r in targets(l):
                    pre_copy(l, j, r).wait_send()

            if l >= 1:

                @pl.when((c % (2 ** (l + 1)) >= 2**l) & (c % 2 == 1))
                def _():
                    relay_copy(l, j).wait_send()

        return 0

    lax.fori_loop(0, chunks, drain, 0)
    for d in range(1, n):
        remote(
            meta_ref, allm_ref.at[me], meta_s.at[d], meta_r.at[me], (me + d) % n
        ).wait_send()
    cache_copy(0, other).wait_send()
    new_copy(0, other).wait_send()
    for d in range(1, n2):
        to = ((c + d) % n2) * 2 + i
        cache_copy(d, to).wait_send()
        forward(0, d).wait_send()

        @pl.when(c + d < n2)
        def _():
            new_copy(d, to).wait_send()

        @pl.when((c + d) % n2 < c)
        def _():
            forward(1, d).wait_send()


def final_kernel(
    part_ref,
    fade_ref,
    sout_ref,
    state_ref,
    meta_ref,
    nk_ref,
    y_ref,
    code_ref,
    scale_ref,
):
    tokens, width = part_ref.shape
    heads = fade_ref.shape[1]
    per_group = min(SSM_HEADS // GROUPS, heads)
    z = lax.axis_index("head")
    group0 = z * heads // (SSM_HEADS // GROUPS)
    block = min(512, width)

    magnitude = jnp.max(meta_ref[:, 0, width:], axis=0, keepdims=True)
    scale = (magnitude + 1e-6) / 127.0
    scale_ref[...] = scale
    code_ref[...] = (nk_ref[...].astype(F32) / scale).astype(BF16)
    fade = fade_ref[...]
    for b in range(width // block):
        here = pl.ds(b * block, block)
        g = group0 + (b * block) // (per_group * HEAD_DIM)
        prior = jnp.dot(
            sout_ref[:, lanes(g * STATE, STATE)], state_ref[:, here], preferred_element_type=F32
        )
        pick = choose(heads, b * block, block).astype(BF16)
        spread = jnp.dot(fade, pick, preferred_element_type=F32)
        y_ref[:, here] = (part_ref[:, here].astype(F32) + spread * prior).astype(BF16)


def body(
    n,
    ssm_input,
    state_in,
    state_out,
    step_size,
    decay_rate,
    forget,
    skip_gain,
    queries,
    new_keys,
    new_values,
    cache_keys,
    cache_values,
    cache_key_scale,
    cache_value_scale,
):
    tokens, width = ssm_input.shape
    heads = step_size.shape[1]
    rows = cache_keys.shape[0]
    channels = new_keys.shape[1]
    q_heads = queries.shape[1] // ATT_DIM
    kv_here = max(1, q_heads // (ATT_HEADS // KV_HEADS))
    kvw = kv_here * ATT_DIM
    per_group = min(SSM_HEADS // GROUPS, heads)
    groups_here = heads // per_group
    limit = pltpu.CompilerParams(vmem_limit_bytes=60 * 1024 * 1024)
    shape = jax.ShapeDtypeStruct
    state, run, fade, at, gram, meta, kvc, kvn = pl.pallas_call(
        local_kernel,
        out_shape=(
            shape((STATE, width), BF16),
            shape((tokens + 16, 3 * heads), BF16),
            shape((tokens, heads), BF16),
            shape((heads, tokens), F32),
            shape((groups_here, tokens, tokens), F32),
            shape((1, width + channels), F32),
            shape((rows, 2 * kvw), BF16),
            shape((tokens, 2 * kvw), BF16),
        ),
        in_specs=[VMEM] * 13,
        out_specs=(VMEM,) * 8,
        compiler_params=limit,
        name="local",
    )(
        ssm_input,
        state_in,
        state_out,
        step_size.T,
        decay_rate.reshape(1, heads),
        forget.reshape(1, tokens),
        skip_gain.reshape(1, heads),
        new_keys,
        new_values,
        cache_keys,
        cache_values,
        cache_key_scale.reshape(1, channels),
        cache_value_scale.reshape(1, channels),
    )
    half = width // 2
    size = min(256, half)
    chunks = half // size
    n2 = n // 2
    levels = n2.bit_length() - 1
    fan = max(1, n2 // 2)
    dma = pltpu.SemaphoreType.DMA
    carried, allm, part, attended = pl.pallas_call(
        functools.partial(comm_kernel, n, chunks),
        out_shape=(
            shape((STATE, width), BF16),
            shape((n, 1, width + channels), F32),
            shape((tokens, width), BF16),
            shape((tokens, queries.shape[1]), BF16),
        ),
        in_specs=[VMEM] * 9,
        out_specs=(VMEM,) * 4,
        scratch_shapes=[
            pltpu.VMEM((n, rows, 2 * kvw), BF16),
            pltpu.VMEM((n, tokens, 2 * kvw), BF16),
            pltpu.VMEM((kv_here, n * rows, 2 * ATT_DIM), BF16),
            pltpu.VMEM((kv_here, n * tokens, 2 * ATT_DIM), BF16),
            pltpu.VMEM((tokens, n * tokens), F32),
            pltpu.VMEM((chunks, STATE, size), BF16),
            pltpu.VMEM((chunks, STATE, size), F32),
            pltpu.VMEM((levels, chunks, STATE, size), BF16),
            pltpu.VMEM((levels, chunks, STATE, size), BF16),
            pltpu.VMEM((chunks, STATE, size), BF16),
            dma((n,)),
            dma((n,)),
            dma((2, n2)),
            dma((2, n)),
            dma((2, n2)),
            dma((chunks,)),
            dma((chunks,)),
            dma((levels, chunks, fan)),
            dma((levels, chunks)),
            dma((levels, chunks)),
            dma((chunks,)),
            dma((chunks,)),
        ],
        compiler_params=pltpu.CompilerParams(
            collective_id=0, has_side_effects=True, vmem_limit_bytes=60 * 1024 * 1024
        ),
        name="exchange",
    )(state, kvc, kvn, meta, ssm_input, run, at, gram, queries)
    y, codes, scale = pl.pallas_call(
        final_kernel,
        out_shape=(
            shape((tokens, width), BF16),
            shape((tokens, channels), BF16),
            shape((1, channels), F32),
        ),
        in_specs=[VMEM] * 6,
        out_specs=(VMEM,) * 3,
        compiler_params=limit,
        name="finish",
    )(part, fade, state_out, carried, allm, new_keys)
    return (y, attended, codes, scale.reshape(channels))

BLOCK = 96


def span_blocks(tokens):
    return max(1, tokens // BLOCK)


def split2(value):
    high = value.astype(BF16)
    low = (value - high.astype(F32)).astype(BF16)
    return jnp.concatenate([high, low], axis=1)


def choose2(heads, begin, size):
    lane = begin + iota((2 * heads, size), 1)
    row = iota((2 * heads, size), 0)
    return (row % heads == lane // HEAD_DIM).astype(BF16)


def factor_rows(tokens):
    nb = span_blocks(tokens)
    size = tokens // nb
    places, at = {}, 0
    for name, rows in (
        [("z", tokens), ("tail", 16)]
        + [(f"z{b}", (b + 1) * size) for b in range(nb - 1)]
        + [("out", tokens), ("skip", 16), ("fade", tokens)]
    ):
        places[name] = (at, at + rows)
        at += rows
    return places, at


def with_ones(v):
    return jnp.concatenate([v, jnp.ones(v.shape, BF16)], axis=1)


NT = (((1,), (1,)), ((), ()))
FACTOR = ATT_DIM**-0.5 * LOG2E


def stream_heads(step, streams, together):
    first = step * streams * together
    return [
        [lanes((first + e * together + f) * ATT_DIM, ATT_DIM) for f in range(together)]
        for e in range(streams)
    ]


def key_columns(step, streams, together, q_ref, all_ref):
    kvw = all_ref.shape[2] // 2
    share = (q_ref.shape[1] // ATT_DIM) // (kvw // ATT_DIM)
    k = (step * streams * together) // share
    return lanes(k * ATT_DIM, ATT_DIM), lanes(kvw + k * ATT_DIM, ATT_DIM)


def score_streams(own, q_ref, keys):
    return [
        lax.dot_general(
            jnp.concatenate([q_ref[:, o] for o in heads], axis=0),
            keys,
            NT,
            preferred_element_type=F32,
        )
        for heads in own
    ]


def attend_cache(step, streams, together, q_ref, allc_ref, sum_ref, peak_ref):
    rows = together * q_ref.shape[0]
    at, av = key_columns(step, streams, together, q_ref, allc_ref)
    keys = allc_ref[:, :, at].reshape(-1, ATT_DIM)
    values = with_ones(allc_ref[:, :, av].reshape(-1, ATT_DIM))
    own = stream_heads(step, streams, together)
    scores = score_streams(own, q_ref, keys)
    for e in range(streams):
        peak = jnp.max(scores[e], axis=1, keepdims=True)
        p = jnp.exp2((scores[e] - peak) * FACTOR).astype(BF16)
        here = pl.ds(pl.multiple_of((step * streams + e) * rows, rows), rows)
        sum_ref[here, :] = jnp.dot(p, values, preferred_element_type=F32)
        peak_ref[here, :] = jnp.broadcast_to(peak, (rows, 128))


def attend_span(
    step, streams, together, chip, q_ref, alln_ref, bias_ref, sum_ref, peak_ref, att_ref
):
    tokens = q_ref.shape[0]
    rows = together * tokens
    at, av = key_columns(step, streams, together, q_ref, alln_ref)
    seen = 2 * chip + 2
    keys = alln_ref[:seen, :, at].reshape(-1, ATT_DIM)
    values = with_ones(alln_ref[:seen, :, av].reshape(-1, ATT_DIM))
    free = keys.shape[0] - 2 * tokens
    own = stream_heads(step, streams, together)
    scores = score_streams(own, q_ref, keys)
    bias = bias_ref[...]
    for e in range(streams):
        near = scores[e][:, free:].reshape(together, tokens, -1) + bias[None]
        near = near.reshape(rows, -1)
        s = jnp.concatenate([scores[e][:, :free], near], axis=1) if free else near
        here = pl.ds(pl.multiple_of((step * streams + e) * rows, rows), rows)
        before = peak_ref[here, :][:, :1]
        peak = jnp.maximum(before, jnp.max(s, axis=1, keepdims=True))
        p = jnp.exp2((s - peak) * FACTOR).astype(BF16)
        both = jnp.dot(p, values, preferred_element_type=F32)
        both += sum_ref[here, :] * jnp.exp2((before - peak) * FACTOR)
        result = (both[:, :ATT_DIM] / both[:, ATT_DIM:]).astype(BF16)
        for f, o in enumerate(own[e]):
            att_ref[:, o] = result[f * tokens : (f + 1) * tokens]


def fused_kernel(
    chunks,
    x_hbm,
    sin_hbm,
    sout_hbm,
    step_hbm,
    decay_hbm,
    forget_hbm,
    skip_hbm,
    q_hbm,
    nk_hbm,
    nv_hbm,
    ck_hbm,
    cv_hbm,
    cks_hbm,
    cvs_hbm,
    y_ref,
    att_ref,
    code_ref,
    scale_ref,
    step_ref,
    decay_ref,
    forget_ref,
    skip_ref,
    cks_ref,
    cvs_ref,
    x_ref,
    sin_ref,
    sout_ref,
    q_ref,
    nk_ref,
    nv_ref,
    ck_ref,
    cv_ref,
    kvc_ref,
    kvn_ref,
    allc_ref,
    alln_ref,
    bias_ref,
    meta_ref,
    allm_ref,
    fac_ref,
    fade_ref,
    z_ref,
    gram_ref,
    turned_ref,
    give_ref,
    sib_ref,
    mine_ref,
    full_ref,
    tx_ref,
    rx_ref,
    enter_ref,
    back_ref,
    other_ref,
    sum_ref,
    peak_ref,
    pick_ref,
    carry_ref,
    wide_ref,
    load_s,
    meta_s,
    meta_r,
    kv_s,
    kv_r,
    kv_f,
    kv_p,
    sib_s,
    sib_r,
    out_s,
    in_r,
    back_s,
    back_r,
):
    n = 8
    tokens, width = x_ref.shape
    heads = step_ref.shape[0]
    per_group = min(SSM_HEADS // GROUPS, heads)
    groups_here = heads // per_group
    channels = nk_ref.shape[1]
    kvw = kvc_ref.shape[1] // 2
    half = width // 2
    size = half // chunks
    near = chunks * 3 // 8
    mid = chunks // 2
    places, _ = factor_rows(tokens)
    nb = span_blocks(tokens)
    bs = tokens // nb

    me = lax.axis_index("seq")
    z = lax.axis_index("head")
    i, c = me % 2, me // 2
    other = me + 1 - 2 * i
    cx, cy = c + 1 - 2 * (c % 2), (c + 2) % 4
    cd = 3 - c
    group0 = z * heads // (SSM_HEADS // GROUPS)
    q_heads = heads * ATT_HEADS // SSM_HEADS
    first_kv = z * q_heads // (ATT_HEADS // KV_HEADS)
    cols = lanes(first_kv * ATT_DIM, kvw)
    gcols = lanes(group0 * STATE, groups_here * STATE)

    barrier = pltpu.get_barrier_semaphore()
    for d in range(1, n):
        pl.semaphore_signal(
            barrier, inc=1, device_id={"seq": (me + d) % n}, device_id_type=MESH
        )

    moves = dict(
        ck=(ck_hbm.at[:, cols], ck_ref),
        cks=(cks_hbm.at[:, cols], cks_ref),
        cv=(cv_hbm.at[:, cols], cv_ref),
        cvs=(cvs_hbm.at[:, cols], cvs_ref),
        nv=(nv_hbm.at[:, cols], nv_ref),
        nk=(nk_hbm, nk_ref),
        step=(step_hbm, step_ref),
        decay=(decay_hbm, decay_ref),
        forget=(forget_hbm, forget_ref),
        skip=(skip_hbm, skip_ref),
        sin=(sin_hbm.at[:, gcols], sin_ref),
        sout=(sout_hbm.at[:, gcols], sout_ref),
        x=(x_hbm, x_ref),
        q=(q_hbm, q_ref),
    )
    loads = {
        name: pltpu.make_async_copy(src, dst, load_s.at[k])
        for k, (name, (src, dst)) in enumerate(moves.items())
    }
    for copy in loads.values():
        copy.start()

    def ready(*names):
        for name in names:
            loads[name].wait()

    def remote(src, dst, ssem, rsem, to):
        return pltpu.make_async_remote_copy(
            src_ref=src,
            dst_ref=dst,
            send_sem=ssem,
            recv_sem=rsem,
            device_id={"seq": to},
            device_id_type=MESH,
        )

    def dev(chip):
        return chip * 2 + i

    alls = (allc_ref, alln_ref)
    owns = (kvc_ref, kvn_ref)

    def own_copy(kind, way):
        to = (other, dev(cx), dev(cy))[way]
        return remote(
            owns[kind], alls[kind].at[me], kv_s.at[kind, way], kv_r.at[kind, me], to
        )

    def pass_copy(kind, way, chip, to):
        slot = dev(chip)
        return remote(
            alls[kind].at[slot],
            alls[kind].at[slot],
            kv_p.at[kind, way],
            kv_r.at[kind, slot],
            dev(to),
        )

    def forward(kind, chip):
        slot = dev(chip)
        return remote(
            alls[kind].at[slot],
            alls[kind].at[slot],
            kv_f.at[kind, chip],
            kv_r.at[kind, slot],
            other,
        )

    def arrived(kind, slot):
        remote(
            owns[kind], alls[kind].at[slot], kv_s.at[kind, 0], kv_r.at[kind, slot], other
        ).wait_recv()

    for k in range(width // 512):
        pick_ref[:, k * 512 : (k + 1) * 512] = choose2(heads, k * 512, 512)
    ready("ck", "cks", "cv", "cvs")
    kvc_ref[:, :kvw] = (ck_ref[...].astype(F32) * cks_ref[...]).astype(BF16)
    kvc_ref[:, kvw:] = (cv_ref[...].astype(F32) * cvs_ref[...]).astype(BF16)
    pl.semaphore_wait(barrier, n - 1)
    for way in (1, 2, 0):
        own_copy(0, way).start()
    ready("nv", "nk")
    kvn_ref[:, :kvw] = nk_ref[:, cols]
    kvn_ref[:, kvw:] = nv_ref[...]

    @pl.when(cx > c)
    def _():
        own_copy(1, 1).start()

    @pl.when(cy > c)
    def _():
        own_copy(1, 2).start()

    own_copy(1, 0).start()

    row, col = iota((tokens, tokens), 0), iota((tokens, tokens), 1)
    lower = jnp.where(col <= row, 1.0, 0.0)
    eye = jnp.where(col == row, 1.0, 0.0).astype(BF16)
    ready("step", "decay", "forget", "skip")
    step = step_ref[...].T
    forgotten = jnp.sum(lower * forget_ref[...], axis=1, keepdims=True)
    decayed = jnp.dot(
        lower, decay_ref[...] * step, precision=HIGHEST, preferred_element_type=F32
    )
    running = -(decayed + forgotten) * LOG2E
    start = running - jnp.log2(step)
    last = running[tokens - 1 : tokens]
    middles = [running[b * bs + bs // 2 - 1 : b * bs + bs // 2] for b in range(nb)]

    meta_ref[:, :channels] = jnp.max(jnp.abs(nk_ref[...].astype(F32)), axis=0, keepdims=True)
    meta_ref[:, channels:] = jnp.concatenate([last, jnp.zeros((1, 128 - heads), F32)], axis=1)

    def meta_copy(d):
        return remote(
            meta_ref, allm_ref.at[me], meta_s.at[d], meta_r.at[me], (me + d) % n
        )

    def meta_arrived(r):
        remote(meta_ref, allm_ref.at[r], meta_s.at[1], meta_r.at[r], r).wait_recv()

    for d in range(1, n):
        meta_copy(d).start()
    allm_ref[me] = meta_ref[...]

    def put(name, value):
        begin, end = places[name]
        fac_ref[begin:end] = split2(jnp.broadcast_to(value, (end - begin, heads)))

    put("z", jnp.exp2(middles[nb - 1] - start))
    put("tail", jnp.exp2(last - middles[nb - 1]))
    for b in range(nb - 1):
        put(f"z{b}", jnp.exp2(middles[b] - start[: (b + 1) * bs]))
    put(
        "out",
        jnp.concatenate(
            [jnp.exp2(running[b * bs : (b + 1) * bs] - middles[b]) for b in range(nb)], axis=0
        ),
    )
    put("skip", skip_ref[...])
    put("fade", jnp.exp2(running))
    ready("sin", "sout")
    for g in range(groups_here):
        gc = slice(g * STATE, (g + 1) * STATE)
        maps_in = sin_ref[:, gc]
        gram = lax.dot_general(
            sout_ref[:, gc], maps_in, (((1,), (1,)), ((), ())), preferred_element_type=F32
        )
        gram_ref[g] = jnp.where(col <= row, gram, 0.0).astype(BF16)
        turned_ref[g] = lax.dot_general(
            maps_in, eye, (((0,), (0,)), ((), ())), preferred_element_type=F32
        ).astype(BF16)
    ready("x")

    def spread(first, final, begin, wide=size):
        rows = fac_ref[places[first][0] : places[final][1]]
        return jnp.dot(rows, pick_ref[:, lanes(begin, wide)], preferred_element_type=F32)

    def local_state(begin):
        here = lanes(begin, 2 * size)
        by = spread("z", "tail", begin, 2 * size)
        scaled = (x_ref[:, here].astype(F32) * by[:tokens]).astype(BF16)
        z_ref[:, here] = scaled
        sums = jnp.dot(
            turned_ref[begin // (per_group * HEAD_DIM)], scaled, preferred_element_type=F32
        )
        sums = (sums * by[tokens : tokens + 1]).astype(BF16)
        return sums[:, :size], sums[:, size:]

    def sib_copy(j):
        return remote(give_ref.at[j], sib_ref.at[j], sib_s.at[j], sib_r.at[j], other)

    shift = (c % 2) * (1 - c // 2) * mid

    def give(s, _):
        j = (2 * s + shift) % chunks
        for e, state in enumerate(local_state((1 - i) * half + j * size)):
            give_ref[j + e] = state
            sib_copy(j + e).start()
        return 0

    def pass_cache():
        arrived(0, dev(cx))

        @pl.when(c >= 1)
        def _():
            pass_copy(0, 0, cx, cy).start()

        forward(0, cx).start()
        arrived(0, dev(cy))

        @pl.when(c == 3)
        def _():
            pass_copy(0, 1, cy, cx).start()

        forward(0, cy).start()

    lax.fori_loop(0, chunks // 2, give, 0)
    pass_cache()
    meta_arrived(other)

    def logs_of(r):
        return allm_ref[r, :, channels : channels + heads]

    def set_fades(third):
        logs = jnp.concatenate(
            [logs_of(2 * c), logs_of(2 * c + 1), third, jnp.zeros((13, heads), F32)], axis=0
        )
        fade_ref[...] = split2(jnp.exp2(logs))

    def fades(j):
        return jnp.dot(
            fade_ref[...],
            pick_ref[:, lanes(i * half + j * size, size)],
            preferred_element_type=F32,
        )

    set_fades(jnp.zeros((1, heads), F32))

    def full_copy(j):
        slot = jnp.where(c == 0, 0, 1)
        return remote(
            full_ref.at[j], rx_ref.at[slot, j], out_s.at[0, j], in_r.at[slot, j], dev(cx)
        )

    def full_sent(j):
        return (c == 0) | ((c == 1) & (j >= near)) | ((c == 2) & (j < near))

    def own(s, _):
        j = (2 * s + shift) % chunks
        states = local_state(i * half + j * size)
        for e, mine in enumerate(states):
            mine_ref[j + e] = mine
        for e in range(2):
            sib_copy(j + e).wait_recv()
        for e, mine in enumerate(states):
            mine, theirs = mine.astype(F32), sib_ref[j + e].astype(F32)
            d1 = fades(j + e)[1:2]
            full = jnp.where(i == 0, d1 * mine + theirs, d1 * theirs + mine)
            full_ref[j + e] = full.astype(BF16)

        for e in range(2):

            @pl.when(full_sent(j + e))
            def _():
                full_copy(j + e).start()

        return 0

    lax.fori_loop(0, chunks // 2, own, 0)
    bias_ref[...] = jnp.where(
        iota((tokens, 2 * tokens), 1) <= i * tokens + iota((tokens, 2 * tokens), 0), 0.0, NEG
    )

    def within(s, _):
        begin = s * 2 * size
        here = lanes(begin, 2 * size)
        by = spread("z0" if nb > 1 else "out", "fade", begin, 2 * size)
        at = 0
        gram = gram_ref[begin // (per_group * HEAD_DIM)]
        x = x_ref[:, here].astype(F32)
        parts = []
        for b in range(nb):
            high = (b + 1) * bs
            if b + 1 < nb:
                scaled = (x[:high] * by[at : at + high]).astype(BF16)
                at += high
            else:
                scaled = z_ref[:, here]
            parts.append(
                jnp.dot(gram[b * bs : high, :high], scaled, preferred_element_type=F32)
            )
        y = by[at : at + tokens] * jnp.concatenate(parts, axis=0)
        y_ref[:, here] = (y + by[at + tokens : at + tokens + 1] * x).astype(BF16)
        wide_ref[:, here] = by[at + tokens + 16 :].astype(BF16)
        return 0

    @pl.when(cx < c)
    def _():
        arrived(1, dev(cx))

        @pl.when(c == 1)
        def _():
            pass_copy(1, 0, cx, cy).start()

        forward(1, cx).start()

    @pl.when(cy < c)
    def _():
        arrived(1, dev(cy))

        @pl.when(c == 3)
        def _():
            pass_copy(1, 1, cy, cx).start()

        forward(1, cy).start()

    lax.fori_loop(0, chunks // 2, within, 0)
    arrived(0, dev(cd))
    forward(0, cd).start()
    lax.fori_loop(chunks // 2, chunks, within, 0)

    for d in range(1, n):
        r = (me + d) % n

        @pl.when(r != other)
        def _():
            meta_arrived(r)

    chip = jnp.where(c == 0, 1, jnp.where(c == 3, 2, c))
    set_fades(logs_of(2 * chip) + logs_of(2 * chip + 1))
    scale = (jnp.max(allm_ref[:, 0, :channels], axis=0, keepdims=True) + 1e-6) / 127.0
    scale_ref[...] = scale
    code_ref[...] = (nk_ref[...].astype(F32) / scale).astype(BF16)

    allc_ref[me] = kvc_ref[...]
    alln_ref[me] = kvn_ref[...]
    arrived(0, other)
    for d in range(1, 4):
        arrived(0, (c + d) % 4 * 2 + 1 - i)

    ready("q")

    def span_arrived():
        @pl.when(cd < c)
        def _():
            arrived(1, dev(cd))
            forward(1, cd).start()

        arrived(1, other)
        for d in range(1, 4):
            there = (c + d) % 4

            @pl.when(there < c)
            def _():
                arrived(1, there * 2 + 1 - i)

    def second_way(s):
        late = s // mid
        return mid + s - late * (2 * mid - near)

    def order(s):
        later = s // (chunks - near)
        even = (1 - later) * second_way(s * (1 - later)) + later * (s - chunks + near)
        last = (s + chunks - near) // chunks
        odd = (1 - last) * s + last * second_way((s - near) * last)
        third = c // 2
        return (1 - c % 2) * even + (c % 2) * (third * odd + (1 - third) * s)

    def prior(begin, carried):
        here = lanes(begin, size)
        group = begin // (per_group * HEAD_DIM)
        term = jnp.dot(sout_ref[:, lanes(group * STATE, STATE)], carried, preferred_element_type=F32)
        by = wide_ref[:, here].astype(F32)
        return begin, (y_ref[:, here].astype(F32) + by * term).astype(BF16)

    def put_prior(result):
        begin, value = result
        y_ref[:, lanes(begin, size)] = value

    def rx_wait(slot, j):
        remote(
            full_ref.at[j], rx_ref.at[slot, j], out_s.at[0, j], in_r.at[slot, j], dev(cx)
        ).wait_recv()

    def tx_copy(j, chip):
        return remote(tx_ref.at[j], rx_ref.at[0, j], out_s.at[1, j], in_r.at[0, j], dev(chip))

    def relay_copy(j):
        return remote(
            rx_ref.at[0, j], rx_ref.at[0, j], out_s.at[2, j], in_r.at[0, j], dev(cx)
        )

    def back_copy(j):
        return remote(back_ref.at[j], other_ref.at[j], back_s.at[j], back_r.at[j], other)

    def pass_on(s):
        @pl.when((c == 1) | (c == 2))
        def _():
            j = (c % 2) * s + (1 - c % 2) * second_way(s)
            rx_wait(0, j)
            keep = fades(j)[2:3]
            tx_ref[j] = (keep * rx_ref[0, j].astype(F32) + full_ref[j].astype(F32)).astype(BF16)
            tx_copy(j, 3).start()

        @pl.when(c == 0)
        def _():
            j = second_way(s)
            rx_wait(1, j)
            keep = fades(j)[2:3]
            tx_ref[j] = (keep * full_ref[j].astype(F32) + rx_ref[1, j].astype(F32)).astype(BF16)
            tx_copy(j, 2).start()

        @pl.when(c == 3)
        def _():
            rx_wait(0, s)
            relay_copy(s).start()

    base = 2 + (c // 2) * (4 + c % 2)
    stride = 2 - c // 2
    passes = (c % 2) * near + (1 - c % 2) * (chunks - near)

    def pass_at(place):
        ahead = place - base
        s = ahead // stride

        @pl.when((ahead >= 0) & (ahead % stride == 0) & (s < passes))
        def _():
            pass_on(s)

    def settle(s):
        j = order(s)
        by = fades(j)
        d0, keep = by[0:1], by[2:3]

        @pl.when((c > 0) & (s >= passes))
        def _():
            rx_wait(0, j)

        @pl.when((c == 3) & (s < near))
        def _():
            rx_wait(1, j)
            enter_ref[...] = keep * rx_ref[0, j].astype(F32) + rx_ref[1, j].astype(F32)

        @pl.when(c == 0)
        def _():
            enter_ref[...] = jnp.zeros(enter_ref.shape, F32)

        @pl.when((c == 1) | (c == 2) | ((c == 3) & (s >= near)))
        def _():
            enter_ref[...] = rx_ref[0, j].astype(F32)

        enter = enter_ref[...]
        first = jnp.where(i == 0, mine_ref[j].astype(F32), sib_ref[j].astype(F32))
        middle = d0 * enter + first
        back_ref[j] = jnp.where(i == 0, middle, enter).astype(BF16)
        back_copy(j).start()
        carry_ref[...] = jnp.where(i == 0, enter, middle).astype(BF16)

    def slot(s, _):
        settle(s)

        @pl.when(s == 0)
        def _():
            put_prior(prior(i * half + order(s) * size, carry_ref[...]))

        @pl.when(s > 0)
        def _():
            far = order(s - 1)
            back_copy(far).wait_recv()
            both = [
                prior(i * half + order(s) * size, carry_ref[...]),
                prior((1 - i) * half + far * size, other_ref[far]),
            ]
            for each in both:
                put_prior(each)

        return 0

    streams, together = 4, 1
    steps = q_heads // (streams * together)
    pass_at(2)

    def first_part(h, _):
        attend_cache(h, streams, 2 * together, q_ref, allc_ref, sum_ref, peak_ref)
        pass_at(3 + 2 * h)
        pass_at(4 + 2 * h)
        return 0

    lax.fori_loop(0, steps // 2, first_part, 0)
    span_arrived()

    def second_part(h, _):
        for chip in range(n // 2):

            @pl.when(c == chip)
            def _():
                attend_span(
                    h,
                    streams,
                    2 * together,
                    chip,
                    q_ref,
                    alln_ref,
                    bias_ref,
                    sum_ref,
                    peak_ref,
                    att_ref,
                )

        for e in range(2):
            pass_at(3 + steps + 2 * h + e)
            slot(2 * h + e, 0)
        return 0

    lax.fori_loop(0, steps // 2, second_part, 0)
    lax.fori_loop(steps, chunks, slot, 0)
    far = order(chunks - 1)
    back_copy(far).wait_recv()
    put_prior(prior((1 - i) * half + far * size, other_ref[far]))

    def drain(j, _):
        back_copy(j).wait_send()
        sib_copy(j).wait_send()

        @pl.when(full_sent(j))
        def _():
            full_copy(j).wait_send()

        @pl.when(((c == 1) & (j < near)) | ((c == 2) & (j >= near)))
        def _():
            tx_copy(j, 3).wait_send()

        @pl.when((c == 0) & (j >= near))
        def _():
            tx_copy(j, 2).wait_send()

        @pl.when((c == 3) & (j < near))
        def _():
            relay_copy(j).wait_send()

        return 0

    lax.fori_loop(0, chunks, drain, 0)
    for d in range(1, n):
        meta_copy(d).wait_send()
    for way in (1, 2, 0):
        own_copy(0, way).wait_send()
    own_copy(1, 0).wait_send()

    @pl.when(cx > c)
    def _():
        own_copy(1, 1).wait_send()

    @pl.when(cy > c)
    def _():
        own_copy(1, 2).wait_send()

    @pl.when(c >= 1)
    def _():
        pass_copy(0, 0, cx, cy).wait_send()

    @pl.when(c == 3)
    def _():
        pass_copy(0, 1, cy, cx).wait_send()
        pass_copy(1, 1, cy, cx).wait_send()

    @pl.when(c == 1)
    def _():
        pass_copy(1, 0, cx, cy).wait_send()

    for chip_ in (cx, cy, cd):
        forward(0, chip_).wait_send()

        @pl.when(chip_ < c)
        def _():
            forward(1, chip_).wait_send()


def finish_kernel(*refs):
    count = (len(refs) - 1) // 2
    copies = [
        pltpu.make_async_copy(refs[k], refs[count + k], refs[-1].at[k]) for k in range(count)
    ]
    for copy in copies:
        copy.start()
    for copy in copies:
        copy.wait()


def fused_body(
    ssm_input,
    state_in,
    state_out,
    step_size,
    decay_rate,
    forget,
    skip_gain,
    queries,
    new_keys,
    new_values,
    cache_keys,
    cache_values,
    cache_key_scale,
    cache_value_scale,
):
    n = 8
    tokens, width = ssm_input.shape
    heads = step_size.shape[1]
    rows = cache_keys.shape[0]
    channels = new_keys.shape[1]
    q_width = queries.shape[1]
    kv_here = max(1, q_width // ATT_DIM // (ATT_HEADS // KV_HEADS))
    kvw = kv_here * ATT_DIM
    groups_here = heads // min(SSM_HEADS // GROUPS, heads)
    half = width // 2
    size = min(256, half)
    chunks = half // size
    _, fac = factor_rows(tokens)
    shape = jax.ShapeDtypeStruct
    dma = pltpu.SemaphoreType.DMA
    any_ = pl.BlockSpec(memory_space=pl.ANY)
    piece = pltpu.VMEM((chunks, STATE, size), BF16)
    results = pl.pallas_call(
        functools.partial(fused_kernel, chunks),
        out_shape=(
            pltpu.VMEM((tokens, width), BF16),
            pltpu.VMEM((tokens, q_width), BF16),
            pltpu.VMEM((tokens, channels), BF16),
            pltpu.VMEM((1, channels), F32),
        ),
        in_specs=[any_] * 14,
        out_specs=(VMEM,) * 4,
        scratch_shapes=[
            pltpu.VMEM((heads, tokens), F32),
            pltpu.VMEM((1, heads), F32),
            pltpu.VMEM((1, tokens), F32),
            pltpu.VMEM((1, heads), F32),
            pltpu.VMEM((1, kvw), F32),
            pltpu.VMEM((1, kvw), F32),
            pltpu.VMEM((tokens, width), BF16),
            pltpu.VMEM((tokens, groups_here * STATE), BF16),
            pltpu.VMEM((tokens, groups_here * STATE), BF16),
            pltpu.VMEM((tokens, q_width), BF16),
            pltpu.VMEM((tokens, channels), BF16),
            pltpu.VMEM((tokens, kvw), BF16),
            pltpu.VMEM((rows, kvw), BF16),
            pltpu.VMEM((rows, kvw), BF16),
            pltpu.VMEM((rows, 2 * kvw), BF16),
            pltpu.VMEM((tokens, 2 * kvw), BF16),
            pltpu.VMEM((n, rows, 2 * kvw), BF16),
            pltpu.VMEM((n, tokens, 2 * kvw), BF16),
            pltpu.VMEM((tokens, 2 * tokens), F32),
            pltpu.VMEM((1, channels + 128), F32),
            pltpu.VMEM((n, 1, channels + 128), F32),
            pltpu.VMEM((fac, 2 * heads), BF16),
            pltpu.VMEM((16, 2 * heads), BF16),
            pltpu.VMEM((tokens, width), BF16),
            pltpu.VMEM((groups_here, tokens, tokens), BF16),
            pltpu.VMEM((groups_here, STATE, tokens), BF16),
            piece,
            piece,
            piece,
            piece,
            piece,
            pltpu.VMEM((2, chunks, STATE, size), BF16),
            pltpu.VMEM((STATE, size), F32),
            piece,
            piece,
            pltpu.VMEM((q_width // ATT_DIM * tokens, 2 * ATT_DIM), F32),
            pltpu.VMEM((q_width // ATT_DIM * tokens, 128), F32),
            pltpu.VMEM((2 * heads, width), BF16),
            pltpu.VMEM((STATE, size), BF16),
            pltpu.VMEM((tokens, width), BF16),
            dma((14,)),
            dma((n,)),
            dma((n,)),
            dma((2, 3)),
            dma((2, n)),
            dma((2, 4)),
            dma((2, 2)),
            dma((chunks,)),
            dma((chunks,)),
            dma((3, chunks)),
            dma((2, chunks)),
            dma((chunks,)),
            dma((chunks,)),
        ],
        compiler_params=pltpu.CompilerParams(
            collective_id=0, has_side_effects=True, vmem_limit_bytes=612 * 1024 * 1024 // 10
        ),
        name="fused",
    )(
        ssm_input,
        state_in,
        state_out,
        step_size.T,
        decay_rate.reshape(1, heads),
        forget.reshape(1, tokens),
        skip_gain.reshape(1, heads),
        queries,
        new_keys,
        new_values,
        cache_keys,
        cache_values,
        cache_key_scale.reshape(1, channels),
        cache_value_scale.reshape(1, channels),
    )
    y, attended, codes, scale = pl.pallas_call(
        finish_kernel,
        out_shape=(
            shape((tokens, width), BF16),
            shape((tokens, q_width), BF16),
            shape((tokens, channels), BF16),
            shape((1, channels), F32),
        ),
        in_specs=[VMEM] * 4,
        out_specs=(any_,) * 4,
        scratch_shapes=[dma((4,))],
        compiler_params=pltpu.CompilerParams(vmem_limit_bytes=4 * 1024 * 1024),
        name="finish",
    )(*results)
    return (y, attended, codes, scale.reshape(channels))


def fits_fused(mesh):
    heads = SSM_HEADS // mesh.shape["head"]
    return mesh.shape["seq"] == 8 and heads == 64


def solution(mesh):
    in_specs = (
        P("seq", "head"),
        P("seq", None),
        P("seq", None),
        P("seq", "head"),
        P("head"),
        P("seq"),
        P("head"),
        P("seq", "head"),
        P("seq", None),
        P("seq", None),
        P("seq", None),
        P("seq", None),
        P(),
        P(),
    )
    out_specs = (P("seq", "head"), P("seq", "head"), P("seq", None), P())
    general = functools.partial(body, mesh.shape["seq"])
    return jax.shard_map(
        fused_body if fits_fused(mesh) else general,
        mesh=mesh,
        in_specs=in_specs,
        out_specs=out_specs,
        check_vma=False,
    )
```
